32 devices in a mesh: batch: 4 (over z), seq: 8 (over y, x, core).
Axes of the slice: x: 2, y: 2, z: 4, core: 2. Of those that a mesh axis runs over, the one named last changes fastest.
Arguments:
- hidden: bfloat16 [4, 1024, 1536], P('batch', 'seq'), may hold values from -6 to 6
- norm_gain: bfloat16 [1536], P(('batch', 'seq')), may hold values from 0.5 to 1.5
- w_gate_in: bfloat16 [1536, 3072], P(('batch', 'seq')), may hold values from -0.15625 to 0.15625
- w_conv_in: bfloat16 [1536, 3328], P(('batch', 'seq')), may hold values from -0.15625 to 0.15625
- w_step: bfloat16 [1536, 48], P(('batch', 'seq')), may hold values from -0.375 to 0.375
- conv_weight: bfloat16 [4, 3328], P(None, ('batch', 'seq')), may hold values from -3 to 3
- conv_bias: bfloat16 [3328], P(('batch', 'seq')), may hold values from -3 to 3
- step_bias: float32 [48], replicated, may hold values from -4 to -1
- decay_log: float32 [48], replicated, may hold values from -6 to 0
- skip_gain: float32 [48], replicated, may hold values from 0.5 to 2
- gate_gain: bfloat16 [3072], P(('batch', 'seq')), may hold values from 0.5 to 1.5
- w_out: bfloat16 [3072, 1536], P(('batch', 'seq')), may hold values from -0.109375 to 0.109375
- cotangent: bfloat16 [4, 1024, 1536], P('batch', 'seq'), may hold values from -6 to 6
Outputs:
- output: bfloat16 [4, 1024, 1536], P('batch', 'seq')
- grad_hidden: float32 [4, 1024, 1536], P('batch', 'seq')
- grad_norm_gain: float32 [1536], P(('batch', 'seq'))
- grad_w_gate_in: float32 [1536, 3072], P(('batch', 'seq'))
- grad_w_conv_in: float32 [1536, 3328], P(('batch', 'seq'))
- grad_w_step: float32 [1536, 48], P(('batch', 'seq'))
- grad_conv_weight: float32 [4, 3328], P(None, ('batch', 'seq'))
- grad_conv_bias: float32 [3328], P(('batch', 'seq'))
- grad_step_bias: float32 [48], replicated
- grad_decay_log: float32 [48], replicated
- grad_skip_gain: float32 [48], replicated
- grad_gate_gain: float32 [3072], P(('batch', 'seq'))
- grad_w_out: float32 [3072, 1536], P(('batch', 'seq'))
The draws below stay inside these ranges and needn't reach their ends.
All inputs are finite; a program needn't handle non-finite values.
Results may differ from the reference program's by a relative error of at most 0.01.
Values may be sent and summed in bfloat16 or wider, within the bound.
No kernel may reach another device: no remote copies, remote signals or barrier semaphores. Data moves between devices by JAX's collectives and lax.ppermute only.
A program may use at most 256 MiB of HBM per device.

```python
import jax
import jax.numpy as jnp
from jax import lax

D = 1536
HEADS = 48
HEAD_DIM = 64
STATE = 128
KERNEL = 4
SPAN = 128
INNER = 3072
CONV_CH = 3328
LENGTH = 1024
BATCH_SEQS = 4


def draw_decay_log(key, part):
    return jax.random.uniform(key, (HEADS,), jnp.float32, -5.0, 0.0)


def block_scale(key, dims, shards, smallest, high):
    factor_of, own = 1.0, jax.random.fold_in(key, 6)
    for dim, shards_of in shards:
        draws = jnp.exp(jax.random.uniform(jax.random.fold_in(own, dim), (shards_of,), jnp.float32, smallest / len(shards), high / len(shards)))
        factor_of = factor_of * jnp.repeat(draws, dims[dim] // shards_of).reshape([-1 if axis == dim else 1 for axis in range(len(dims))])
    return factor_of


def noise(stream_key, shape, scale, most, pieces=(), dtype=jnp.bfloat16):
    drawn = scale * jax.random.normal(stream_key, shape, jnp.float32)
    if pieces:
        drawn = drawn * block_scale(stream_key, shape, pieces, -0.22, 0.18)
    return jnp.clip(drawn, -most, most).astype(dtype)


def setup_inputs(seed: int = 0) -> dict:
    key_of = jax.random.split(jax.random.key(seed), 14)
    return {
        "hidden": noise(key_of[0], (BATCH_SEQS, LENGTH, D), 1.0, 6.0, ((0, 4), (1, 8))),
        "norm_gain": jnp.clip(1.0 + 0.1 * jax.random.normal(key_of[1], (D,), jnp.float32), 0.5, 1.5).astype(jnp.bfloat16),
        "w_gate_in": noise(key_of[2], (D, INNER), D ** -0.5, 0.15625, ((0, 32),)),
        "w_conv_in": noise(key_of[3], (D, CONV_CH), D ** -0.5, 0.15625, ((0, 32),)),
        "w_step": noise(key_of[4], (D, HEADS), (D // 6) ** -0.5, 0.375, ((0, 32),)),
        "conv_weight": noise(key_of[5], (KERNEL, CONV_CH), KERNEL ** -0.5, 3.0, ((1, 32),)),
        "conv_bias": noise(key_of[6], (CONV_CH,), 0.5, 3.0, ((0, 32),)),
        "step_bias": jnp.clip(jax.random.uniform(key_of[7], (HEADS,), jnp.float32, -4.0, -1.0), -4.0, -1.0),
        "decay_log": draw_decay_log(jax.random.fold_in(key_of[13], 71), 0),
        "skip_gain": jnp.clip(jax.random.uniform(key_of[9], (HEADS,), jnp.float32, 0.5, 2.0), 0.5, 2.0),
        "gate_gain": jnp.clip(1.0 + 0.1 * jax.random.normal(key_of[10], (INNER,), jnp.float32), 0.5, 1.5).astype(jnp.bfloat16),
        "w_out": noise(key_of[11], (INNER, D), INNER ** -0.5, 0.109375, ((0, 32),)),
        "cotangent": noise(key_of[12], (BATCH_SEQS, LENGTH, D), 1.0, 6.0, ((0, 4), (1, 8))),
    }


norm_epsilon = 1e-05

def narrow_product(pattern, former, latter):
    return jnp.einsum(pattern, former.astype(jnp.float32), latter.astype(jnp.float32))

def wide_product(pattern, former, latter):
    return jnp.einsum(pattern, former, latter, precision=lax.Precision.HIGHEST)

def silu_slope(inputs):
    logistic = jax.nn.sigmoid(inputs)
    return logistic * (1.0 + inputs * (1.0 - logistic))

def span_parts(value_b, key_b, query_b, step_size, head_rate):
    length = step_size.shape[0]
    cumulative = jnp.cumsum(step_size * head_rate[None, :], axis=0).T
    row_index = lax.broadcasted_iota(jnp.int32, (1, length, length), 1)
    col_index = lax.broadcasted_iota(jnp.int32, (1, length, length), 2)
    causal = row_index >= col_index
    spread = cumulative[:, :, None] - cumulative[:, None, :]
    decays = jnp.where(causal, jnp.exp(jnp.where(causal, spread, 0.0)), 0.0)
    affinity = jnp.dot(query_b, key_b.T, preferred_element_type=jnp.float32)
    step_rows = step_size.T
    scores = affinity[None] * decays * step_rows[:, None, :]
    mixing = scores.astype(jnp.bfloat16)
    within = narrow_product('hts,shp->thp', mixing, value_b)
    tail_decay = jnp.exp(cumulative[:, -1:] - cumulative) * step_rows
    weighted = (tail_decay.T[:, :, None] * value_b.astype(jnp.float32)).astype(jnp.bfloat16)
    span_state = narrow_product('shp,sn->hpn', weighted, key_b)
    total_decay = jnp.exp(cumulative[:, -1])
    return (within, span_state, total_decay, cumulative, decays, affinity, scores, mixing, weighted)

def span_inter(query_b, cumulative, carried):
    base = wide_product('tn,hpn->thp', query_b.astype(jnp.float32), carried)
    return jnp.exp(cumulative).T[:, :, None] * base

def carried_grad(query_b, cumulative, grad_y):
    scaled = grad_y * jnp.exp(cumulative).T[:, :, None]
    return wide_product('thp,tn->hpn', scaled, query_b.astype(jnp.float32))

def span_backward(value_b, key_b, query_b, step_size, carried, grad_y, grad_state, grad_total, head_rate):
    parts = span_parts(value_b, key_b, query_b, step_size, head_rate)
    total_decay, cumulative, decays, affinity, scores, mixing, weighted = parts[2:]
    length = step_size.shape[0]
    query_f = query_b.astype(jnp.float32)
    key_f = key_b.astype(jnp.float32)
    value_f = value_b.astype(jnp.float32)
    step_rows = step_size.T
    growth = jnp.exp(cumulative)
    base = wide_product('tn,hpn->thp', query_f, carried)
    grad_cumul = growth * lax.optimization_barrier(jnp.sum(grad_y * base, axis=2)).T
    grad_query = wide_product('thp,hpn->tn', grad_y * growth.T[:, :, None], carried)
    grad_low = grad_y.astype(jnp.bfloat16)
    grad_mixing = narrow_product('thp,shp->hts', grad_low, value_b)
    grad_value = narrow_product('hts,thp->shp', mixing, grad_low)
    grad_affinity = lax.optimization_barrier(jnp.sum(grad_mixing * decays * step_rows[:, None, :], axis=0))
    grad_steps = lax.optimization_barrier(jnp.sum(grad_mixing * affinity[None] * decays, axis=1))
    through = grad_mixing * scores
    grad_cumul = grad_cumul + lax.optimization_barrier(jnp.sum(through, axis=2)) - lax.optimization_barrier(jnp.sum(through, axis=1))
    grad_query = grad_query + wide_product('ts,sn->tn', grad_affinity, key_f)
    grad_key = wide_product('ts,tn->sn', grad_affinity, query_f)
    grad_weighted = wide_product('hpn,sn->shp', grad_state, key_f)
    grad_key = grad_key + wide_product('shp,hpn->sn', weighted.astype(jnp.float32), grad_state)
    grad_end = lax.optimization_barrier(jnp.sum(grad_weighted * value_f, axis=2)).T
    tail_only = jnp.exp(cumulative[:, -1:] - cumulative)
    grad_value = grad_value + grad_weighted * (tail_only * step_rows).T[:, :, None]
    grad_steps = grad_steps + grad_end * tail_only
    push = grad_end * tail_only * step_rows
    last_flag = lax.broadcasted_iota(jnp.int32, (1, length), 1) == length - 1
    last_term = (lax.optimization_barrier(jnp.sum(push, axis=1)) + grad_total * total_decay)[:, None]
    grad_cumul = grad_cumul - push + jnp.where(last_flag, last_term, 0.0)
    grad_log = jnp.flip(jnp.cumsum(jnp.flip(grad_cumul, 1), axis=1), 1)
    grad_steps = grad_steps + grad_log * head_rate[:, None]
    grad_rate = lax.optimization_barrier(jnp.sum(grad_log * step_rows, axis=1))
    return (grad_value, grad_key, grad_query, grad_steps.T, grad_rate)

def conv_apply(padded, kernel_f, bias_f, length):
    time_axis = padded.ndim - 2
    total = bias_f
    for offset in range(kernel_f.shape[0]):
        total = total + kernel_f[offset] * lax.slice_in_dim(padded, offset, offset + length, axis=time_axis)
    return total

def conv_back(grad_mixed, padded, kernel_f):
    length = grad_mixed.shape[-2]
    kernel_taps = kernel_f.shape[0]
    time_axis = grad_mixed.ndim - 2
    leading = tuple(range(grad_mixed.ndim - 1))
    grad_kernel = jnp.stack([lax.optimization_barrier(jnp.sum(grad_mixed * lax.slice_in_dim(padded, offset, offset + length, axis=time_axis), axis=leading)) for offset in range(kernel_taps)])
    grad_padded = jnp.zeros(padded.shape, jnp.float32)
    for offset in range(kernel_taps):
        widths = [(0, 0)] * grad_mixed.ndim
        widths[time_axis] = (offset, kernel_taps - 1 - offset)
        grad_padded = grad_padded + jnp.pad(grad_mixed * kernel_f[offset], widths)
    return (grad_kernel, grad_padded)

def reference(hidden, norm_gain, w_gate_in, w_conv_in, w_step, conv_weight, conv_bias, step_bias, decay_log, skip_gain, gate_gain, w_out, cotangent):
    head_rate = -jnp.exp(decay_log)
    kernel_f = conv_weight.astype(jnp.float32)
    spans = LENGTH // SPAN
    zero_state = jnp.zeros((HEADS, HEAD_DIM, STATE), jnp.float32)

    def one_sequence(totals, pair):
        tokens, incoming = pair
        tokens_f = tokens.astype(jnp.float32)
        inv_rms = lax.rsqrt(lax.optimization_barrier(jnp.mean(tokens_f * tokens_f, axis=1, keepdims=True)) + norm_epsilon)
        unit = tokens_f * inv_rms
        normed = (unit * norm_gain.astype(jnp.float32)[None]).astype(jnp.bfloat16)
        gate_pre = jnp.dot(normed, w_gate_in, preferred_element_type=jnp.float32)
        conv_pre = jnp.dot(normed, w_conv_in, preferred_element_type=jnp.float32).astype(jnp.bfloat16)
        raw_step = jnp.dot(normed, w_step, preferred_element_type=jnp.float32)
        padded = jnp.concatenate([jnp.zeros((KERNEL - 1, CONV_CH), jnp.bfloat16), conv_pre], axis=0).astype(jnp.float32)
        mixed_in = conv_apply(padded, kernel_f, conv_bias.astype(jnp.float32), LENGTH)
        conv_out = jax.nn.silu(mixed_in).astype(jnp.bfloat16)
        value_b = conv_out[:, :INNER].reshape(spans, SPAN, HEADS, HEAD_DIM)
        key_b = conv_out[:, INNER:INNER + STATE].reshape(spans, SPAN, STATE)
        query_b = conv_out[:, INNER + STATE:].reshape(spans, SPAN, STATE)
        step_size = jax.nn.softplus(raw_step + step_bias[None]).reshape(spans, SPAN, HEADS)

        def forward_step(carried, piece):
            parts = span_parts(piece[0], piece[1], piece[2], piece[3], head_rate)
            mixed_out = parts[0] + span_inter(piece[2], parts[3], carried)
            return (parts[2][:, None, None] * carried + parts[1], (mixed_out, carried, parts[2]))
        _, (partial_out, carried_all, decay_all) = lax.scan(forward_step, zero_state, (value_b, key_b, query_b, step_size))
        value_f = value_b.astype(jnp.float32)
        ssm_out = partial_out + skip_gain[None, None, :, None] * value_f
        flat_out = ssm_out.reshape(LENGTH, INNER)
        gate_silu = jax.nn.silu(gate_pre)
        gated = flat_out * gate_silu
        inv_gate = lax.rsqrt(lax.optimization_barrier(jnp.mean(gated * gated, axis=1, keepdims=True)) + norm_epsilon)
        normed_gate = gated * inv_gate
        projected_in = (normed_gate * gate_gain.astype(jnp.float32)[None]).astype(jnp.bfloat16)
        output = (tokens_f + jnp.dot(projected_in, w_out, preferred_element_type=jnp.float32)).astype(jnp.bfloat16)
        grad_proj = jnp.dot(incoming, w_out.T, preferred_element_type=jnp.float32)
        grad_w_out = jnp.dot(projected_in.T, incoming, preferred_element_type=jnp.float32)
        grad_gate_gain = lax.optimization_barrier(jnp.sum(grad_proj * normed_gate, axis=0))
        grad_ngate = grad_proj * gate_gain.astype(jnp.float32)[None]
        grad_gated = inv_gate * (grad_ngate - normed_gate * lax.optimization_barrier(jnp.mean(grad_ngate * normed_gate, axis=1, keepdims=True)))
        grad_flat = grad_gated * gate_silu
        grad_gate_pre = (grad_gated * flat_out * silu_slope(gate_pre)).astype(jnp.bfloat16)
        grad_ssm = grad_flat.reshape(spans, SPAN, HEADS, HEAD_DIM)
        grad_skip = lax.optimization_barrier(jnp.sum(grad_ssm * value_f, axis=(0, 1, 3)))

        def backward_step(grad_next, piece):
            value_piece, key_piece, query_piece, step_piece, carried_piece, decay_piece, grad_piece = piece
            cumulative = jnp.cumsum(step_piece * head_rate[None, :], axis=0).T
            grad_total = lax.optimization_barrier(jnp.sum(grad_next * carried_piece, axis=(1, 2)))
            results = span_backward(value_piece, key_piece, query_piece, step_piece, carried_piece, grad_piece, grad_next, grad_total, head_rate)
            grad_carried = carried_grad(query_piece, cumulative, grad_piece)
            return (grad_carried + decay_piece[:, None, None] * grad_next, results)
        _, (grad_value, grad_key, grad_query, grad_steps, grad_rate) = lax.scan(backward_step, zero_state, (value_b, key_b, query_b, step_size, carried_all, decay_all, grad_ssm), reverse=True)
        grad_value = grad_value + grad_ssm * skip_gain[None, None, :, None]
        grad_conv_out = jnp.concatenate([grad_value.reshape(LENGTH, INNER), grad_key.reshape(LENGTH, STATE), grad_query.reshape(LENGTH, STATE)], axis=1)
        grad_mixed = grad_conv_out * silu_slope(mixed_in)
        grad_bias = lax.optimization_barrier(jnp.sum(grad_mixed, axis=0))
        grad_kernel, grad_padded = conv_back(grad_mixed, padded, kernel_f)
        grad_pre = grad_padded[KERNEL - 1:].astype(jnp.bfloat16)
        grad_raw = grad_steps.reshape(LENGTH, HEADS) * jax.nn.sigmoid(raw_step + step_bias[None])
        grad_step_bias = lax.optimization_barrier(jnp.sum(grad_raw, axis=0))
        grad_raw_low = grad_raw.astype(jnp.bfloat16)
        grad_decay_log = lax.optimization_barrier(jnp.sum(grad_rate, axis=0)) * head_rate
        grad_w_gate_in = jnp.dot(normed.T, grad_gate_pre, preferred_element_type=jnp.float32)
        grad_w_conv_in = jnp.dot(normed.T, grad_pre, preferred_element_type=jnp.float32)
        grad_w_step = jnp.dot(normed.T, grad_raw_low, preferred_element_type=jnp.float32)
        grad_normed = jnp.dot(grad_gate_pre, w_gate_in.T, preferred_element_type=jnp.float32)
        grad_normed = grad_normed + jnp.dot(grad_pre, w_conv_in.T, preferred_element_type=jnp.float32)
        grad_normed = grad_normed + jnp.dot(grad_raw_low, w_step.T, preferred_element_type=jnp.float32)
        grad_norm_gain = lax.optimization_barrier(jnp.sum(grad_normed * unit, axis=0))
        grad_unit = grad_normed * norm_gain.astype(jnp.float32)[None]
        grad_tokens = inv_rms * (grad_unit - unit * lax.optimization_barrier(jnp.mean(grad_unit * unit, axis=1, keepdims=True)))
        grad_hidden = incoming.astype(jnp.float32) + grad_tokens
        terms = (grad_norm_gain, grad_w_gate_in, grad_w_conv_in, grad_w_step, grad_kernel, grad_bias, grad_step_bias, grad_decay_log, grad_skip, grad_gate_gain, grad_w_out)
        totals = tuple((former + latter for former, latter in zip(totals, terms)))
        return (totals, (output, grad_hidden))
    initial = (jnp.zeros((D,), jnp.float32), jnp.zeros((D, INNER), jnp.float32), jnp.zeros((D, CONV_CH), jnp.float32), jnp.zeros((D, HEADS), jnp.float32), jnp.zeros((KERNEL, CONV_CH), jnp.float32), jnp.zeros((CONV_CH,), jnp.float32), jnp.zeros((HEADS,), jnp.float32), jnp.zeros((HEADS,), jnp.float32), jnp.zeros((HEADS,), jnp.float32), jnp.zeros((INNER,), jnp.float32), jnp.zeros((INNER, D), jnp.float32))
    totals, (output, grad_hidden) = lax.scan(one_sequence, initial, (hidden, cotangent))
    return (output, grad_hidden, totals[0], totals[1], totals[2], totals[3], totals[4], totals[5], totals[6], totals[7], totals[8], totals[9], totals[10])
```

```python
import jax
import jax.numpy as jnp
from jax import lax
from jax.sharding import PartitionSpec as P

norm_epsilon = 1e-05


def shifted(value, axis, steps):
    count = lax.axis_size(axis)
    first, last = (max(0, -steps), min(count, count - steps))
    return lax.ppermute(value, axis, [(source, source + steps) for source in range(first, last)])


def prefix(array, axis, combine, identity, reverse):
    devices, place = (lax.axis_size(axis), lax.axis_index(axis))
    everything = jax.tree.map(lambda part: lax.all_gather(part, axis), array)
    start = jax.tree.map(
        lambda part, zero: jnp.broadcast_to(jnp.asarray(zero, part.dtype), part.shape),
        array,
        identity,
    )

    def hop(k, before):
        at = devices - 1 - k if reverse else k
        reached = at > place if reverse else at < place
        new = combine(before, jax.tree.map(lambda part: part[at], everything))
        return jax.tree.map(lambda a, b: jnp.where(reached, a, b), new, before)

    return lax.fori_loop(0, devices, hop, start)


def for_sending(array):
    return jax.tree.map(lambda a: a.astype(jnp.bfloat16) if a.dtype == jnp.float32 else a, array)


def narrow_product(pattern, former, latter):
    return jnp.einsum(pattern, former, latter, preferred_element_type=jnp.float32)


def wide_product(pattern, former, latter):
    return jnp.einsum(pattern, former, latter, precision=lax.Precision.HIGHEST)


def silu_slope(inputs):
    logistic = jax.nn.sigmoid(inputs)
    return logistic * (1.0 + inputs * (1.0 - logistic))


def upper_table(length):
    rows = lax.broadcasted_iota(jnp.int32, (length, length), 0)
    cols = lax.broadcasted_iota(jnp.int32, (length, length), 1)
    return (rows <= cols).astype(jnp.float32)


def running_total(step_size, head_rate):
    table = upper_table(step_size.shape[0])
    return jnp.dot((step_size * head_rate[None, :]).T, table, precision=lax.Precision.HIGHEST)


def span_parts(value_b, key_b, query_b, step_size, head_rate):
    length = step_size.shape[0]
    cumulative = running_total(step_size, head_rate)
    row_index = lax.broadcasted_iota(jnp.int32, (1, length, length), 1)
    col_index = lax.broadcasted_iota(jnp.int32, (1, length, length), 2)
    causal = row_index >= col_index
    spread = cumulative[:, :, None] - cumulative[:, None, :]
    decays = jnp.where(causal, jnp.exp(jnp.where(causal, spread, 0.0)), 0.0)
    affinity = jnp.dot(query_b, key_b.T, preferred_element_type=jnp.float32)
    step_rows = step_size.T
    scores = affinity[None] * decays * step_rows[:, None, :]
    mixing = scores.astype(jnp.bfloat16)
    within = narrow_product("hts,shp->thp", mixing, value_b)
    tail_decay = jnp.exp(cumulative[:, -1:] - cumulative) * step_rows
    weighted = (tail_decay.T[:, :, None] * value_b.astype(jnp.float32)).astype(jnp.bfloat16)
    span_state = narrow_product("shp,sn->hpn", weighted, key_b)
    total_decay = jnp.exp(cumulative[:, -1])
    return (within, span_state, total_decay, cumulative, decays, affinity, scores, mixing, weighted)


def span_inter(query_b, cumulative, carried):
    base = wide_product("tn,hpn->thp", query_b.astype(jnp.float32), carried)
    return jnp.exp(cumulative).T[:, :, None] * base


def carried_grad(query_b, cumulative, grad_y):
    scaled = grad_y * jnp.exp(cumulative).T[:, :, None]
    return wide_product("thp,tn->hpn", scaled, query_b.astype(jnp.float32))


def span_backward(
    value_b, key_b, query_b, step_size, carried, grad_y, grad_state, grad_total, head_rate
):
    parts = span_parts(value_b, key_b, query_b, step_size, head_rate)
    total_decay, cumulative, decays, affinity, scores, mixing, weighted = parts[2:]
    length = step_size.shape[0]
    query_f = query_b.astype(jnp.float32)
    key_f = key_b.astype(jnp.float32)
    value_f = value_b.astype(jnp.float32)
    step_rows = step_size.T
    growth = jnp.exp(cumulative)
    base = wide_product("tn,hpn->thp", query_f, carried)
    grad_cumul = growth * jnp.sum(grad_y * base, axis=2).T
    grad_query = wide_product("thp,hpn->tn", grad_y * growth.T[:, :, None], carried)
    grad_low = grad_y.astype(jnp.bfloat16)
    grad_mixing = narrow_product("thp,shp->hts", grad_low, value_b)
    grad_value = narrow_product("hts,thp->shp", mixing, grad_low)
    grad_affinity = jnp.sum(grad_mixing * decays * step_rows[:, None, :], axis=0)
    grad_steps = jnp.sum(grad_mixing * affinity[None] * decays, axis=1)
    through = grad_mixing * scores
    grad_cumul = grad_cumul + jnp.sum(through, axis=2) - jnp.sum(through, axis=1)
    grad_query = grad_query + wide_product("ts,sn->tn", grad_affinity, key_f)
    grad_key = wide_product("ts,tn->sn", grad_affinity, query_f)
    grad_weighted = wide_product("hpn,sn->shp", grad_state, key_f)
    grad_key = grad_key + wide_product("shp,hpn->sn", weighted.astype(jnp.float32), grad_state)
    grad_end = jnp.sum(grad_weighted * value_f, axis=2).T
    tail_only = jnp.exp(cumulative[:, -1:] - cumulative)
    grad_value = grad_value + grad_weighted * (tail_only * step_rows).T[:, :, None]
    grad_steps = grad_steps + grad_end * tail_only
    push = grad_end * tail_only * step_rows
    last_flag = lax.broadcasted_iota(jnp.int32, (1, length), 1) == length - 1
    last_term = (jnp.sum(push, axis=1) + grad_total * total_decay)[:, None]
    grad_cumul = grad_cumul - push + jnp.where(last_flag, last_term, 0.0)
    grad_log = jnp.dot(grad_cumul, upper_table(length).T, precision=lax.Precision.HIGHEST)
    grad_steps = grad_steps + grad_log * head_rate[:, None]
    grad_rate = jnp.sum(grad_log * step_rows, axis=1)
    return (grad_value, grad_key, grad_query, grad_steps.T, grad_rate)


def conv_apply(padded, kernel_f, bias_f, length):
    time_axis = padded.ndim - 2
    total = bias_f
    for offset in range(kernel_f.shape[0]):
        total = total + kernel_f[offset] * lax.slice_in_dim(
            padded, offset, offset + length, axis=time_axis
        )
    return total


def conv_back(grad_mixed, padded, kernel_f):
    length = grad_mixed.shape[-2]
    kernel_taps = kernel_f.shape[0]
    time_axis = grad_mixed.ndim - 2
    leading = tuple(range(grad_mixed.ndim - 1))
    grad_kernel = jnp.stack(
        [
            jnp.sum(
                grad_mixed * lax.slice_in_dim(padded, offset, offset + length, axis=time_axis),
                axis=leading,
            )
            for offset in range(kernel_taps)
        ]
    )
    grad_padded = jnp.zeros(padded.shape, jnp.float32)
    for offset in range(kernel_taps):
        widths = [(0, 0)] * grad_mixed.ndim
        widths[time_axis] = (offset, kernel_taps - 1 - offset)
        grad_padded = grad_padded + jnp.pad(grad_mixed * kernel_f[offset], widths)
    return (grad_kernel, grad_padded)


def combine_states(earlier, later):
    return (earlier[0] * later[0], later[0][:, :, None, None] * earlier[1] + later[1])


def local(
    hidden,
    norm_gain,
    w_gate_in,
    w_conv_in,
    w_step,
    conv_weight,
    conv_bias,
    step_bias,
    decay_log,
    skip_gain,
    gate_gain,
    w_out,
    cotangent,
):
    seq_count, length, model_width = hidden.shape
    gathered = (
        lax.all_gather(norm_gain, ("batch", "seq"), axis=0, tiled=True),
        lax.all_gather(w_gate_in, ("batch", "seq"), axis=0, tiled=True),
        lax.all_gather(w_conv_in, ("batch", "seq"), axis=0, tiled=True),
        lax.all_gather(w_step, ("batch", "seq"), axis=0, tiled=True),
        lax.all_gather(conv_weight, ("batch", "seq"), axis=1, tiled=True),
        lax.all_gather(conv_bias, ("batch", "seq"), axis=0, tiled=True),
        lax.all_gather(gate_gain, ("batch", "seq"), axis=0, tiled=True),
        lax.all_gather(w_out, ("batch", "seq"), axis=0, tiled=True),
    )
    (
        norm_full,
        gate_in_full,
        conv_in_full,
        step_full,
        kernel_full,
        bias_full,
        gain_full,
        out_full,
    ) = gathered
    inner_width = gate_in_full.shape[1]
    head_count = step_full.shape[1]
    head_width = inner_width // head_count
    channels = conv_in_full.shape[1]
    state_width = (channels - inner_width) // 2
    kernel_taps = kernel_full.shape[0]
    row_count = seq_count * length
    head_rate = -jnp.exp(decay_log)
    tokens_f = hidden.reshape(row_count, model_width).astype(jnp.float32)
    inv_rms = lax.rsqrt(jnp.mean(tokens_f * tokens_f, axis=1, keepdims=True) + norm_epsilon)
    unit = tokens_f * inv_rms
    normed = (unit * norm_full.astype(jnp.float32)[None]).astype(jnp.bfloat16)
    gate_pre = jnp.dot(normed, gate_in_full, preferred_element_type=jnp.float32)
    conv_pre = (
        jnp.dot(normed, conv_in_full, preferred_element_type=jnp.float32)
        .astype(jnp.bfloat16)
        .reshape(seq_count, length, channels)
    )
    raw_step = jnp.dot(normed, step_full, preferred_element_type=jnp.float32)
    rim = shifted(conv_pre[:, length - (kernel_taps - 1) :, :], "seq", 1)
    extended = jnp.concatenate([rim, conv_pre], axis=1).astype(jnp.float32)
    mixed_in = conv_apply(
        extended, kernel_full.astype(jnp.float32), bias_full.astype(jnp.float32), length
    )
    conv_out = jax.nn.silu(mixed_in).astype(jnp.bfloat16)
    value_b = conv_out[:, :, :inner_width].reshape(seq_count, length, head_count, head_width)
    key_b = conv_out[:, :, inner_width : inner_width + state_width]
    query_b = conv_out[:, :, inner_width + state_width :]
    step_size = jax.nn.softplus(raw_step + step_bias[None]).reshape(seq_count, length, head_count)

    def local_forward(value_piece, key_piece, query_piece, step_piece):
        parts = span_parts(value_piece, key_piece, query_piece, step_piece, head_rate)
        return (parts[0], parts[1], parts[2], parts[3])

    within, span_state, total_decay, cumulative = jax.vmap(local_forward)(
        value_b, key_b, query_b, step_size
    )
    identity = (jnp.ones_like(total_decay), jnp.zeros_like(span_state))
    _, carried = prefix((total_decay, span_state), "seq", combine_states, identity, False)
    inter = jax.vmap(span_inter)(query_b, cumulative, carried)
    value_f = value_b.astype(jnp.float32)
    ssm_out = within + inter + skip_gain[None, None, :, None] * value_f
    flat_out = ssm_out.reshape(row_count, inner_width)
    gate_silu = jax.nn.silu(gate_pre)
    gated = flat_out * gate_silu
    inv_gate = lax.rsqrt(jnp.mean(gated * gated, axis=1, keepdims=True) + norm_epsilon)
    normed_gate = gated * inv_gate
    projected_in = (normed_gate * gain_full.astype(jnp.float32)[None]).astype(jnp.bfloat16)
    output = (
        tokens_f + jnp.dot(projected_in, out_full, preferred_element_type=jnp.float32)
    ).astype(jnp.bfloat16)
    backward_weights = (
        lax.all_gather(norm_gain, ("batch", "seq"), axis=0, tiled=True),
        lax.all_gather(w_gate_in, ("batch", "seq"), axis=0, tiled=True),
        lax.all_gather(w_conv_in, ("batch", "seq"), axis=0, tiled=True),
        lax.all_gather(w_step, ("batch", "seq"), axis=0, tiled=True),
        lax.all_gather(conv_weight, ("batch", "seq"), axis=1, tiled=True),
        lax.all_gather(gate_gain, ("batch", "seq"), axis=0, tiled=True),
        lax.all_gather(w_out, ("batch", "seq"), axis=0, tiled=True),
    )
    norm_back, gate_in_back, conv_in_back, step_back, kernel_back, gain_back, out_back = (
        backward_weights
    )
    incoming = cotangent.reshape(row_count, model_width)
    grad_proj = jnp.dot(incoming, out_back.T, preferred_element_type=jnp.float32)
    grad_w_out = jnp.dot(projected_in.T, incoming, preferred_element_type=jnp.float32)
    grad_gate_gain = jnp.sum(grad_proj * normed_gate, axis=0)
    grad_ngate = grad_proj * gain_back.astype(jnp.float32)[None]
    grad_gated = inv_gate * (
        grad_ngate - normed_gate * jnp.mean(grad_ngate * normed_gate, axis=1, keepdims=True)
    )
    grad_flat = grad_gated * gate_silu
    grad_gate_pre = (grad_gated * flat_out * silu_slope(gate_pre)).astype(jnp.bfloat16)
    grad_ssm = grad_flat.reshape(seq_count, length, head_count, head_width)
    grad_skip = jnp.sum(grad_ssm * value_f, axis=(0, 1, 3))
    grad_carried = jax.vmap(carried_grad)(query_b, cumulative, grad_ssm)
    _, grad_state = prefix((total_decay, grad_carried), "seq", combine_states, identity, True)
    grad_total = jnp.sum(grad_state * carried, axis=(2, 3))

    def local_backward(
        value_piece,
        key_piece,
        query_piece,
        step_piece,
        carried_piece,
        grad_piece,
        state_piece,
        total_piece,
    ):
        return span_backward(
            value_piece,
            key_piece,
            query_piece,
            step_piece,
            carried_piece,
            grad_piece,
            state_piece,
            total_piece,
            head_rate,
        )

    grad_value, grad_key, grad_query, grad_steps, grad_rate = jax.vmap(local_backward)(
        value_b, key_b, query_b, step_size, carried, grad_ssm, grad_state, grad_total
    )
    grad_value = grad_value + grad_ssm * skip_gain[None, None, :, None]
    grad_conv_out = jnp.concatenate(
        [grad_value.reshape(seq_count, length, inner_width), grad_key, grad_query], axis=2
    )
    grad_mixed = grad_conv_out * silu_slope(mixed_in)
    grad_bias = jnp.sum(grad_mixed, axis=(0, 1))
    grad_kernel, grad_padded = conv_back(grad_mixed, extended, kernel_back.astype(jnp.float32))
    back_rim = shifted(for_sending(grad_padded[:, : kernel_taps - 1, :]), "seq", -1)
    grad_core = grad_padded[:, kernel_taps - 1 :, :]
    split_at = length - (kernel_taps - 1)
    grad_core = jnp.concatenate(
        [grad_core[:, :split_at], grad_core[:, split_at:] + back_rim], axis=1
    )
    grad_pre = grad_core.astype(jnp.bfloat16).reshape(row_count, channels)
    grad_raw = grad_steps.reshape(row_count, head_count) * jax.nn.sigmoid(
        raw_step + step_bias[None]
    )
    grad_step_bias = jnp.sum(grad_raw, axis=0)
    grad_raw_low = grad_raw.astype(jnp.bfloat16)
    grad_decay_log = jnp.sum(grad_rate, axis=0) * head_rate
    grad_w_gate_in = jnp.dot(normed.T, grad_gate_pre, preferred_element_type=jnp.float32)
    grad_w_conv_in = jnp.dot(normed.T, grad_pre, preferred_element_type=jnp.float32)
    grad_w_step = jnp.dot(normed.T, grad_raw_low, preferred_element_type=jnp.float32)
    grad_normed = jnp.dot(grad_gate_pre, gate_in_back.T, preferred_element_type=jnp.float32)
    grad_normed = grad_normed + jnp.dot(
        grad_pre, conv_in_back.T, preferred_element_type=jnp.float32
    )
    grad_normed = grad_normed + jnp.dot(
        grad_raw_low, step_back.T, preferred_element_type=jnp.float32
    )
    grad_norm_gain = jnp.sum(grad_normed * unit, axis=0)
    grad_unit = grad_normed * norm_back.astype(jnp.float32)[None]
    grad_tokens = inv_rms * (grad_unit - unit * jnp.mean(grad_unit * unit, axis=1, keepdims=True))
    grad_hidden = (incoming.astype(jnp.float32) + grad_tokens).reshape(
        seq_count, length, model_width
    )
    partial_grads = (
        grad_norm_gain,
        grad_w_gate_in,
        grad_w_conv_in,
        grad_w_step,
        grad_kernel,
        grad_bias,
        grad_gate_gain,
        grad_w_out,
    )
    shares = (
        lax.psum_scatter(partial_grads[0], ("batch", "seq"), scatter_dimension=0, tiled=True),
        lax.psum_scatter(partial_grads[1], ("batch", "seq"), scatter_dimension=0, tiled=True),
        lax.psum_scatter(partial_grads[2], ("batch", "seq"), scatter_dimension=0, tiled=True),
        lax.psum_scatter(partial_grads[3], ("batch", "seq"), scatter_dimension=0, tiled=True),
        lax.psum_scatter(partial_grads[4], ("batch", "seq"), scatter_dimension=1, tiled=True),
        lax.psum_scatter(partial_grads[5], ("batch", "seq"), scatter_dimension=0, tiled=True),
        lax.psum_scatter(partial_grads[6], ("batch", "seq"), scatter_dimension=0, tiled=True),
        lax.psum_scatter(partial_grads[7], ("batch", "seq"), scatter_dimension=0, tiled=True),
    )
    head_sums = lax.psum((grad_step_bias, grad_decay_log, grad_skip), ("batch", "seq"))
    return (
        output.reshape(seq_count, length, model_width),
        grad_hidden,
        shares[0],
        shares[1],
        shares[2],
        shares[3],
        shares[4],
        shares[5],
        head_sums[0],
        head_sums[1],
        head_sums[2],
        shares[6],
        shares[7],
    )


bf16 = jnp.bfloat16
f32 = jnp.float32


def hop(value, distance):
    count = lax.axis_size("seq")
    return lax.ppermute(value, "seq", [(i, i ^ distance) for i in range(count)])


def next_plane(value):
    count = lax.axis_size("batch")
    return lax.ppermute(value, "batch", [(i, (i + 1) % count) for i in range(count)])


def ring_gather(value):
    parts = [value]
    for _ in range(lax.axis_size("batch") - 1):
        parts.append(next_plane(parts[-1]))
    return parts


def ring_sum(blocks):
    total = blocks[1]
    for step in range(1, len(blocks)):
        received = next_plane(total.astype(bf16)).astype(f32)
        total = received + blocks[(step + 1) % len(blocks)]
    return total


def plane_gather(value):
    chips = [value, hop(value, 2), hop(value, 4), hop(value, 6)]
    mine = jnp.stack(chips)
    other = hop(mine, 1)
    return jnp.stack([mine, other], axis=1).reshape(8, *value.shape)


def plane_sum(parts):
    pairs = parts.reshape(4, 2, *parts.shape[1:])
    half = pairs[:, 0] + hop(pairs[:, 1].astype(bf16), 1).astype(f32)
    low = half.astype(bf16)
    return half[0] + sum(hop(low[j], 2 * j).astype(f32) for j in (1, 2, 3))


def plane_total(value):
    value = value + hop(value, 1)
    return value + hop(value, 2) + hop(value, 4) + hop(value, 6)


def own_columns(table):
    rows, inner = table.shape
    by = table.reshape(rows, 4, 4, inner // 16)
    wide, slim = inner // 24, inner // 48
    first = jnp.concatenate(
        [by[:, 0, :, :wide], by[:, 1, :, :slim], by[:, 2, :, :wide], by[:, 3, :, :slim]], axis=-1
    )
    second = jnp.concatenate(
        [by[:, 0, :, wide:], by[:, 1, :, slim:], by[:, 2, :, wide:], by[:, 3, :, slim:]], axis=-1
    )
    return first, second


def all_columns(table):
    _, rows, local = table.shape
    wide, slim = local // 3, local // 6
    pairs = table.reshape(4, 2, rows, local)
    first, second = pairs[:, 0], pairs[:, 1]
    blocks = []
    for plane in range(4):
        at_first = [0, wide, wide + slim, 2 * wide + slim][plane]
        at_second = [0, slim, wide + slim, wide + 2 * slim][plane]
        n_first, n_second = (wide, slim) if plane % 2 == 0 else (slim, wide)
        blocks.append(
            jnp.concatenate(
                [
                    first[:, :, at_first : at_first + n_first],
                    second[:, :, at_second : at_second + n_second],
                ],
                axis=-1,
            )
        )
    return jnp.stack(blocks).transpose(2, 0, 1, 3).reshape(rows, 8 * local)


def local_group(index, core, width):
    wide, slim = 2 * width, width
    starts = (
        jnp.where(core == 0, 0, 0),
        jnp.where(core == 0, wide, slim),
        wide + slim,
        jnp.where(core == 0, 2 * wide + slim, wide + 2 * slim),
    )
    plane = sum((index >= start).astype(jnp.int32) for start in starts[1:])
    start = jnp.where(plane == 0, starts[0], jnp.where(plane == 1, starts[1], jnp.where(plane == 2, starts[2], starts[3])))
    offset = jnp.where(core == 0, 0, jnp.where(plane % 2 == 0, wide, slim))
    return plane, index - start + offset


def split_local(
    hidden,
    norm_gain,
    w_gate_in,
    w_conv_in,
    w_step,
    conv_weight,
    conv_bias,
    step_bias,
    decay_log,
    skip_gain,
    gate_gain,
    w_out,
    cotangent,
):
    plane, rank = lax.axis_index("batch"), lax.axis_index("seq")
    chip, core = rank // 2, rank % 2
    planes, ranks = lax.axis_size("batch"), lax.axis_size("seq")
    _, span, width = hidden.shape
    rows_in, inner = w_gate_in.shape
    channels = w_conv_in.shape[1]
    heads = w_step.shape[1]
    head_width = inner // heads
    states = (channels - inner) // 2
    taps = conv_weight.shape[0]
    own = inner // ranks
    own_heads = heads // ranks
    rows_out = w_out.shape[0]
    tokens = ranks * span
    block = width // planes
    piece = conv_bias.shape[0]

    vectors = jnp.concatenate([norm_gain, gate_gain, conv_bias, conv_weight.reshape(-1)])
    vectors = jnp.broadcast_to(vectors[None, None], (planes * ranks, 1, vectors.shape[0]))
    vectors = lax.all_to_all(vectors, ("batch", "seq"), 0, 0)[:, 0].astype(f32)
    norm_full = vectors[:, :rows_in].reshape(1, width)
    gain_full = vectors[:, rows_in : rows_in + rows_out].reshape(1, inner)
    small_all = vectors[:, rows_in + rows_out :].reshape(planes * ranks, taps + 1, piece)
    small_all = small_all.transpose(1, 0, 2).reshape(taps + 1, channels)
    shared = jnp.concatenate([w_conv_in[:, inner:], w_step], axis=1)
    shared_width = shared.shape[1]
    padded = -(-shared_width // 128) * 128
    message = jnp.pad(shared, ((0, 0), (0, padded - shared_width)))

    tokens_f = hidden[0].astype(f32)
    inv_rms = lax.rsqrt(jnp.mean(tokens_f * tokens_f, axis=1, keepdims=True) + norm_epsilon)
    unit = tokens_f * inv_rms
    normed = (unit * norm_full).astype(bf16)

    def turned(array):
        return jnp.concatenate(
            [
                lax.dynamic_slice_in_dim(array, ((plane - o) % planes) * block, block, 1)
                for o in range(planes)
            ],
            axis=1,
        )

    def turned_back(array):
        return jnp.concatenate(
            [
                lax.dynamic_slice_in_dim(array, ((plane - p) % planes) * block, block, 1)
                for p in range(planes)
            ],
            axis=1,
        )

    time_order = jnp.arange(ranks) ^ rank
    message_all = jnp.stack(ring_gather(message))
    unit_rel = plane_gather(turned(normed))
    conv_cols = jnp.stack(own_columns(w_conv_in[:, :inner]), axis=2)
    conv_cols = conv_cols.reshape(rows_in, ranks, own).transpose(1, 0, 2)
    gate_cols = jnp.stack(own_columns(w_gate_in), axis=2).reshape(rows_in, ranks, own).transpose(1, 0, 2)
    conv_plane = lax.all_to_all(conv_cols, "seq", 0, 0).reshape(ranks * rows_in, own)
    gate_plane = lax.all_to_all(gate_cols, "seq", 0, 0).reshape(ranks * rows_in, own)
    out_parts = ring_gather(w_out)
    conv_w = jnp.concatenate(ring_gather(conv_plane))
    gate_w = jnp.concatenate(ring_gather(gate_plane))
    cot_rel = plane_gather(cotangent[0])
    shared_rel = plane_gather(message_all)
    shared_all = shared_rel[time_order]
    shared_w = shared_all[:, :, :rows_in].transpose(1, 0, 2, 3).reshape(width, padded)

    out_rel = jnp.stack(out_parts).reshape(planes // 2, 2, rows_out, width)
    third = rows_out // 3
    lent = (plane + 1 + core) % 2
    lent_rows = jnp.where(lent == 1, out_rel[:, 1], out_rel[:, 0])
    lent_rows = jnp.where(core == 1, lent_rows[:, :third], lent_rows[:, 2 * third :])
    borrowed = hop(lent_rows, 1)
    source = jnp.concatenate([out_rel.reshape(planes * rows_out, width), borrowed.reshape(-1, width)])
    place = jnp.arange(own)
    at_plane, at = local_group(place, core, head_width)
    back = (plane - at_plane) % planes
    mine = (at // rows_out) == core
    at_row = jnp.where(
        mine,
        back * rows_out + at % rows_out,
        planes * rows_out + (back // 2) * third + jnp.where(core == 0, at - rows_out, at - 2 * third),
    )
    pick = (at_row[:, None] == jnp.arange(source.shape[0])[None]).astype(bf16)
    out_w = jnp.dot(pick, source, preferred_element_type=f32).astype(bf16)

    head_plane, head_at = local_group(jnp.arange(own_heads), core, 1)
    own_head = 3 * (planes * head_plane + chip) + head_at
    head_pick = (own_head[:, None] == jnp.arange(heads)[None]).astype(f32)

    def of_heads(vector):
        return jnp.sum(head_pick * vector[None], axis=1)

    bias_own, skip_own = of_heads(step_bias), of_heads(skip_gain)
    rate_own = -jnp.exp(of_heads(decay_log))
    table_all = jnp.concatenate([gain_full, small_all[:, :inner]], axis=0)
    by_group = table_all.reshape(taps + 2, planes, planes, inner // 16)
    by_chip = lax.dynamic_index_in_dim(by_group, chip, 2, keepdims=True).reshape(taps + 2, inner // 4)
    pair = [jnp.concatenate(parts, axis=-1) for parts in (
        [by_chip[:, 0:128], by_chip[:, 192:256], by_chip[:, 384:512], by_chip[:, 576:640]],
        [by_chip[:, 128:192], by_chip[:, 256:384], by_chip[:, 512:576], by_chip[:, 640:768]],
    )]
    small_own = jnp.where(core == 0, pair[0], pair[1])
    gain_own = small_own[:1]
    small_use = jnp.concatenate([small_own[1:], small_all[:, inner:]], axis=1)
    bias_f, tap_f = small_use[0], small_use[1:]

    unit_t = unit_rel[time_order].reshape(tokens, width)
    cot_t = cot_rel[time_order].reshape(tokens, width)
    proj = jnp.dot(unit_t, shared_w, preferred_element_type=f32)
    conv_pre = jnp.concatenate(
        [jnp.dot(unit_t, conv_w, preferred_element_type=f32), proj[:, : 2 * states]], axis=1
    ).astype(bf16)
    raw = jnp.sum(proj[:, None, 2 * states : 2 * states + heads] * head_pick[None], axis=2)
    gate_pre = jnp.dot(unit_t, gate_w, preferred_element_type=f32)
    extended = jnp.pad(conv_pre, ((taps - 1, 0), (0, 0))).astype(f32)
    mixed_in = bias_f
    for offset in range(taps):
        mixed_in = mixed_in + tap_f[offset] * extended[offset : offset + tokens]
    conv_out = jax.nn.silu(mixed_in).astype(bf16)
    value = conv_out[:, :own].reshape(ranks, span, own_heads, head_width)
    key = conv_out[:, own : own + states].reshape(ranks, span, states)
    query = conv_out[:, own + states :].reshape(ranks, span, states)
    step = jax.nn.softplus(raw + bias_own).reshape(ranks, span, own_heads)
    table = upper_table(span)
    cum = jnp.einsum("csh,st->cth", step * rate_own, table, precision=lax.Precision.HIGHEST)
    cum_h = cum.transpose(0, 2, 1)
    causal = (lax.broadcasted_iota(jnp.int32, (span, span), 0) >= lax.broadcasted_iota(jnp.int32, (span, span), 1))
    spread = cum_h[:, :, :, None] - cum_h[:, :, None, :]
    decays = jnp.where(causal, jnp.exp(jnp.where(causal, spread, 0.0)), 0.0)
    affinity = narrow_product("ctn,csn->cts", query, key)
    step_h = step.transpose(0, 2, 1)
    scores = affinity[:, None] * decays * step_h[:, :, None, :]
    mixing = scores.astype(bf16)
    within = narrow_product("chts,cshp->cthp", mixing, value)
    tail = jnp.exp(cum[:, -1:] - cum)
    tailed = ((tail * step)[..., None] * value.astype(f32)).astype(bf16)
    span_state = narrow_product("cshp,csn->chpn", tailed, key)
    total_decay = jnp.exp(cum[:, -1])
    carried = [jnp.zeros_like(span_state[0])]
    for c in range(ranks):
        carried.append(total_decay[c][:, None, None] * carried[-1] + span_state[c])
    carried = jnp.stack(carried)
    carried_low = carried[:-1].astype(bf16)
    growth = jnp.exp(cum)
    inter = growth[..., None] * wide_product("ctn,chpn->cthp", query.astype(f32), carried[:-1])
    ssm = (within + inter).reshape(tokens, own)
    skip_row = jnp.repeat(skip_own, head_width)
    value_f = conv_out[:, :own].astype(f32)
    ssm_out = ssm + skip_row * value_f
    gate = jax.nn.sigmoid(gate_pre)
    gate_silu = gate_pre * gate
    gated = ssm_out * gate_silu
    grad_ngate = jnp.dot(cot_t, out_w.T, preferred_element_type=f32) * gain_own
    sums = plane_total(jnp.stack([jnp.sum(gated * gated, axis=1), jnp.sum(grad_ngate * gated, axis=1)]))
    gated_low = (gated * gain_own).astype(bf16)
    out_part = jnp.dot(gated_low, out_w, preferred_element_type=f32)
    inv_gate = lax.rsqrt(sums[0] / inner + norm_epsilon)[:, None]
    inner_mean = inv_gate * sums[1][:, None] / inner
    out_own = plane_sum(out_part.reshape(ranks, span, width)[time_order])
    inv_own = lax.dynamic_slice_in_dim(inv_gate, rank * span, span, 0)
    output = (tokens_f + inv_own * out_own).astype(bf16)

    normed_gate = gated * inv_gate
    grad_gated = inv_gate * (grad_ngate - normed_gate * inner_mean)
    grad_flat = grad_gated * gate_silu
    grad_gate_pre = (grad_gated * ssm_out * (gate * (1.0 + gate_pre * (1.0 - gate)))).astype(bf16)
    grad_skip = jnp.sum((grad_flat * value_f).reshape(tokens, own_heads, head_width), axis=(0, 2))
    grad_y = grad_flat.reshape(ranks, span, own_heads, head_width)
    grad_low = grad_y.astype(bf16)
    grad_cum = jnp.sum(grad_y * inter, axis=3)
    grown_f = grad_y * growth[..., None]
    grown = grown_f.astype(bf16)
    grad_carried = wide_product("cthp,ctn->chpn", grown_f, query.astype(f32))
    grad_state = [jnp.zeros_like(grad_carried[0])]
    for c in range(ranks - 1, 0, -1):
        grad_state.append(grad_carried[c] + total_decay[c][:, None, None] * grad_state[-1])
    grad_state = jnp.stack(grad_state[::-1])
    state_low = grad_state.astype(bf16)
    grad_query = narrow_product("cthp,chpn->ctn", grown, carried_low)
    grad_mixing = narrow_product("cthp,cshp->chts", grad_low, value)
    by_decay = grad_mixing * decays
    grad_affinity = jnp.sum(by_decay * step_h[:, :, None, :], axis=1).astype(bf16)
    direct = jnp.sum(by_decay * affinity[:, None], axis=2).transpose(0, 2, 1)
    grad_cum = grad_cum + jnp.sum(grad_mixing * scores, axis=3).transpose(0, 2, 1)
    grad_value = narrow_product("chts,cthp->cshp", mixing, grad_low)
    grad_weighted = wide_product("csn,chpn->cshp", key.astype(f32), grad_state)
    direct = direct + tail * jnp.sum(grad_weighted * value.astype(f32), axis=3)
    grad_value = grad_value + (tail * step)[..., None] * grad_weighted + skip_own[:, None] * grad_y
    grad_query = grad_query + narrow_product("cts,csn->ctn", grad_affinity, key)
    grad_key = narrow_product("cts,ctn->csn", grad_affinity, query)
    grad_key = grad_key + narrow_product("cshp,chpn->csn", tailed, state_low)
    last = jnp.sum(grad_state * carried[1:], axis=(2, 3))
    grad_cum = grad_cum - step * direct
    grad_cum = grad_cum.at[:, -1].add(last)
    grad_log = jnp.einsum("cth,st->csh", grad_cum, table, precision=lax.Precision.HIGHEST)
    grad_steps = direct + grad_log * rate_own
    grad_decay_log = rate_own * jnp.sum(grad_log * step, axis=(0, 1))
    grad_conv_out = jnp.concatenate(
        [grad_value.reshape(tokens, own), grad_key.reshape(tokens, states), grad_query.reshape(tokens, states)],
        axis=1,
    )
    grad_mixed = grad_conv_out * silu_slope(mixed_in)
    grad_taps = jnp.stack(
        [jnp.sum(grad_mixed * extended[offset : offset + tokens], axis=0) for offset in range(taps)]
        + [jnp.sum(grad_mixed, axis=0)]
    )
    ahead = jnp.pad(grad_mixed, ((0, taps - 1), (0, 0)))
    grad_pre = sum(
        ahead[taps - 1 - offset : taps - 1 - offset + tokens] * tap_f[offset] for offset in range(taps)
    ).astype(bf16)
    grad_raw = grad_steps.reshape(tokens, own_heads) * jax.nn.sigmoid(raw + bias_own)
    grad_step_bias = jnp.sum(grad_raw, axis=0)
    grad_raw_all = jnp.dot(grad_raw.astype(bf16), head_pick.astype(bf16), preferred_element_type=f32).astype(bf16)
    grad_shared = jnp.concatenate(
        [grad_pre[:, own:], grad_raw_all, jnp.zeros((tokens, padded - shared_width), bf16)], axis=1
    )

    projected = (normed_gate * gain_own).astype(bf16)
    given = jnp.dot(projected, pick, preferred_element_type=f32).astype(bf16)
    d_out = jnp.dot(given.T, cot_t, preferred_element_type=f32)
    returned = hop(d_out[planes * rows_out :].astype(bf16), 1).astype(f32).reshape(planes // 2, third, width)
    spread_rows = jnp.where(
        core == 1,
        jnp.pad(returned, ((0, 0), (0, 2 * third), (0, 0))),
        jnp.pad(returned, ((0, 0), (2 * third, 0), (0, 0))),
    )
    d_out_rel = d_out[: planes * rows_out].reshape(planes, rows_out, width)
    d_out_rel = [
        d_out_rel[o] + jnp.where(lent == o % 2, spread_rows[o // 2], 0.0) for o in range(planes)
    ]
    d_gate = jnp.dot(unit_t.T, grad_gate_pre, preferred_element_type=f32).reshape(planes, block, own)
    d_conv = jnp.dot(unit_t.T, grad_pre[:, :own], preferred_element_type=f32).reshape(planes, block, own)
    d_shared = jnp.dot(unit_t.T, grad_shared, preferred_element_type=f32)
    d_gate = ring_sum(d_gate)
    d_out = ring_sum(d_out_rel)
    d_conv = ring_sum(d_conv)
    d_gate = lax.all_to_all(d_gate.astype(bf16).reshape(ranks, rows_in, own), "seq", 0, 0)
    d_conv = lax.all_to_all(d_conv.astype(bf16).reshape(ranks, rows_in, own), "seq", 0, 0)
    d_shared = d_shared.astype(bf16).reshape(planes, ranks, rows_in, padded).transpose(1, 0, 2, 3)
    d_shared = jnp.sum(lax.all_to_all(d_shared, "seq", 0, 0).astype(f32), axis=0)
    d_shared = ring_sum(d_shared)
    d_gate = all_columns(d_gate.astype(f32))
    d_conv = jnp.concatenate([all_columns(d_conv.astype(f32)), d_shared[:, : 2 * states]], axis=1)
    d_step = d_shared[:, 2 * states : shared_width]

    grad_unit = jnp.dot(grad_gate_pre, gate_w.T, preferred_element_type=f32)
    grad_unit = grad_unit + jnp.dot(grad_pre[:, :own], conv_w.T, preferred_element_type=f32)
    grad_unit = grad_unit + jnp.dot(grad_shared, shared_w.T, preferred_element_type=f32)
    grad_unit = norm_full * turned_back(plane_sum(grad_unit.reshape(ranks, span, width)[time_order]))
    grad_tokens = inv_rms * (grad_unit - unit * jnp.mean(grad_unit * unit, axis=1, keepdims=True))
    grad_hidden = cotangent[0].astype(f32) + grad_tokens

    own_taps = grad_taps[:, :own]
    halves = []
    for k, sizes in ((0, (128, 64, 128, 64)), (1, (64, 128, 64, 128))):
        at, groups = 0, []
        for size in sizes:
            part = own_taps[:, at : at + size]
            at += size
            groups.append(jnp.pad(part, ((0, 0), (0, 192 - size) if k == 0 else (192 - size, 0))))
        halves.append(jnp.stack(groups, axis=1))
    wide_taps = jnp.where(core == 0, halves[0], halves[1])
    wide_taps = jnp.where(
        (jnp.arange(planes) == chip)[None, None, :, None], wide_taps[:, :, None, :], 0.0
    ).reshape(taps + 1, inner)
    wide_taps = jnp.concatenate([wide_taps, grad_taps[:, own:]], axis=1)
    per_device = wide_taps.reshape(taps + 1, planes * ranks, piece).transpose(1, 0, 2).reshape(planes * ranks, -1)
    head_grads = jnp.concatenate(
        [jnp.sum(head_pick * g[:, None], axis=0) for g in (grad_step_bias, grad_decay_log, grad_skip)]
    )
    per_device = jnp.concatenate(
        [per_device, jnp.broadcast_to(head_grads[None], (planes * ranks, 3 * heads))], axis=1
    )
    small_sum = jnp.sum(lax.all_to_all(per_device, ("batch", "seq"), 0, 0), axis=0)
    taps_out = small_sum[: (taps + 1) * piece].reshape(taps + 1, piece)
    heads_out = small_sum[(taps + 1) * piece :].reshape(3, heads)

    grad_norm_gain = (
        jnp.sum(w_gate_in.astype(f32) * d_gate, axis=1)
        + jnp.sum(w_conv_in.astype(f32) * d_conv, axis=1)
        + jnp.sum(w_step.astype(f32) * d_step, axis=1)
    )
    grad_norm_gain = grad_norm_gain / norm_gain.astype(f32)
    return (
        output[None],
        grad_hidden[None],
        grad_norm_gain,
        d_gate,
        d_conv,
        d_step,
        taps_out[:taps],
        taps_out[taps],
        heads_out[0],
        heads_out[1],
        heads_out[2],
        jnp.sum(w_out.astype(f32) * d_out, axis=1) / gate_gain.astype(f32),
        d_out,
    )


def solution(mesh):
    body = split_local if (mesh.shape["batch"], mesh.shape["seq"]) == (4, 8) else local
    return jax.shard_map(
        body,
        mesh=mesh,
        in_specs=(
            P("batch", "seq", None),
            P(("batch", "seq")),
            P(("batch", "seq"), None),
            P(("batch", "seq"), None),
            P(("batch", "seq"), None),
            P(None, ("batch", "seq")),
            P(("batch", "seq")),
            P(),
            P(),
            P(),
            P(("batch", "seq")),
            P(("batch", "seq"), None),
            P("batch", "seq", None),
        ),
        out_specs=(
            P("batch", "seq", None),
            P("batch", "seq", None),
            P(("batch", "seq")),
            P(("batch", "seq"), None),
            P(("batch", "seq"), None),
            P(("batch", "seq"), None),
            P(None, ("batch", "seq")),
            P(("batch", "seq")),
            P(),
            P(),
            P(),
            P(("batch", "seq")),
            P(("batch", "seq"), None),
        ),
        check_vma=False,
    )
```

```python
import functools
import typing

import jax
import jax.numpy as jnp
from jax import lax
from jax.experimental import pallas as pl
from jax.experimental.pallas import tpu as pltpu
from jax.sharding import PartitionSpec as P

norm_epsilon = 1e-05


def shifted(value, axis, steps):
    count = lax.axis_size(axis)
    first, last = (max(0, -steps), min(count, count - steps))
    return lax.ppermute(value, axis, [(source, source + steps) for source in range(first, last)])


def prefix(array, axis, combine, identity, reverse):
    devices, place = (lax.axis_size(axis), lax.axis_index(axis))
    everything = jax.tree.map(lambda part: lax.all_gather(part, axis), array)
    start = jax.tree.map(
        lambda part, zero: jnp.broadcast_to(jnp.asarray(zero, part.dtype), part.shape),
        array,
        identity,
    )

    def hop(k, before):
        at = devices - 1 - k if reverse else k
        reached = at > place if reverse else at < place
        new = combine(before, jax.tree.map(lambda part: part[at], everything))
        return jax.tree.map(lambda a, b: jnp.where(reached, a, b), new, before)

    return lax.fori_loop(0, devices, hop, start)


def for_sending(array):
    return jax.tree.map(lambda a: a.astype(jnp.bfloat16) if a.dtype == jnp.float32 else a, array)


def narrow_product(pattern, former, latter):
    return jnp.einsum(pattern, former, latter, preferred_element_type=jnp.float32)


def wide_product(pattern, former, latter):
    return jnp.einsum(pattern, former, latter, precision=lax.Precision.HIGHEST)


def silu_slope(inputs):
    logistic = jax.nn.sigmoid(inputs)
    return logistic * (1.0 + inputs * (1.0 - logistic))


def upper_table(length):
    rows = lax.broadcasted_iota(jnp.int32, (length, length), 0)
    cols = lax.broadcasted_iota(jnp.int32, (length, length), 1)
    return (rows <= cols).astype(jnp.float32)


def running_total(step_size, head_rate):
    table = upper_table(step_size.shape[0])
    return jnp.dot((step_size * head_rate[None, :]).T, table, precision=lax.Precision.HIGHEST)


def span_parts(value_b, key_b, query_b, step_size, head_rate):
    length = step_size.shape[0]
    cumulative = running_total(step_size, head_rate)
    row_index = lax.broadcasted_iota(jnp.int32, (1, length, length), 1)
    col_index = lax.broadcasted_iota(jnp.int32, (1, length, length), 2)
    causal = row_index >= col_index
    spread = cumulative[:, :, None] - cumulative[:, None, :]
    decays = jnp.where(causal, jnp.exp(jnp.where(causal, spread, 0.0)), 0.0)
    affinity = jnp.dot(query_b, key_b.T, preferred_element_type=jnp.float32)
    step_rows = step_size.T
    scores = affinity[None] * decays * step_rows[:, None, :]
    mixing = scores.astype(jnp.bfloat16)
    within = narrow_product("hts,shp->thp", mixing, value_b)
    tail_decay = jnp.exp(cumulative[:, -1:] - cumulative) * step_rows
    weighted = (tail_decay.T[:, :, None] * value_b.astype(jnp.float32)).astype(jnp.bfloat16)
    span_state = narrow_product("shp,sn->hpn", weighted, key_b)
    total_decay = jnp.exp(cumulative[:, -1])
    return (within, span_state, total_decay, cumulative, decays, affinity, scores, mixing, weighted)


def span_inter(query_b, cumulative, carried):
    base = wide_product("tn,hpn->thp", query_b.astype(jnp.float32), carried)
    return jnp.exp(cumulative).T[:, :, None] * base


def carried_grad(query_b, cumulative, grad_y):
    scaled = grad_y * jnp.exp(cumulative).T[:, :, None]
    return wide_product("thp,tn->hpn", scaled, query_b.astype(jnp.float32))


def span_backward(
    value_b, key_b, query_b, step_size, carried, grad_y, grad_state, grad_total, head_rate
):
    parts = span_parts(value_b, key_b, query_b, step_size, head_rate)
    total_decay, cumulative, decays, affinity, scores, mixing, weighted = parts[2:]
    length = step_size.shape[0]
    query_f = query_b.astype(jnp.float32)
    key_f = key_b.astype(jnp.float32)
    value_f = value_b.astype(jnp.float32)
    step_rows = step_size.T
    growth = jnp.exp(cumulative)
    base = wide_product("tn,hpn->thp", query_f, carried)
    grad_cumul = growth * jnp.sum(grad_y * base, axis=2).T
    grad_query = wide_product("thp,hpn->tn", grad_y * growth.T[:, :, None], carried)
    grad_low = grad_y.astype(jnp.bfloat16)
    grad_mixing = narrow_product("thp,shp->hts", grad_low, value_b)
    grad_value = narrow_product("hts,thp->shp", mixing, grad_low)
    grad_affinity = jnp.sum(grad_mixing * decays * step_rows[:, None, :], axis=0)
    grad_steps = jnp.sum(grad_mixing * affinity[None] * decays, axis=1)
    through = grad_mixing * scores
    grad_cumul = grad_cumul + jnp.sum(through, axis=2) - jnp.sum(through, axis=1)
    grad_query = grad_query + wide_product("ts,sn->tn", grad_affinity, key_f)
    grad_key = wide_product("ts,tn->sn", grad_affinity, query_f)
    grad_weighted = wide_product("hpn,sn->shp", grad_state, key_f)
    grad_key = grad_key + wide_product("shp,hpn->sn", weighted.astype(jnp.float32), grad_state)
    grad_end = jnp.sum(grad_weighted * value_f, axis=2).T
    tail_only = jnp.exp(cumulative[:, -1:] - cumulative)
    grad_value = grad_value + grad_weighted * (tail_only * step_rows).T[:, :, None]
    grad_steps = grad_steps + grad_end * tail_only
    push = grad_end * tail_only * step_rows
    last_flag = lax.broadcasted_iota(jnp.int32, (1, length), 1) == length - 1
    last_term = (jnp.sum(push, axis=1) + grad_total * total_decay)[:, None]
    grad_cumul = grad_cumul - push + jnp.where(last_flag, last_term, 0.0)
    grad_log = jnp.dot(grad_cumul, upper_table(length).T, precision=lax.Precision.HIGHEST)
    grad_steps = grad_steps + grad_log * head_rate[:, None]
    grad_rate = jnp.sum(grad_log * step_rows, axis=1)
    return (grad_value, grad_key, grad_query, grad_steps.T, grad_rate)


def conv_apply(padded, kernel_f, bias_f, length):
    time_axis = padded.ndim - 2
    total = bias_f
    for offset in range(kernel_f.shape[0]):
        total = total + kernel_f[offset] * lax.slice_in_dim(
            padded, offset, offset + length, axis=time_axis
        )
    return total


def conv_back(grad_mixed, padded, kernel_f):
    length = grad_mixed.shape[-2]
    kernel_taps = kernel_f.shape[0]
    time_axis = grad_mixed.ndim - 2
    leading = tuple(range(grad_mixed.ndim - 1))
    grad_kernel = jnp.stack(
        [
            jnp.sum(
                grad_mixed * lax.slice_in_dim(padded, offset, offset + length, axis=time_axis),
                axis=leading,
            )
            for offset in range(kernel_taps)
        ]
    )
    grad_padded = jnp.zeros(padded.shape, jnp.float32)
    for offset in range(kernel_taps):
        widths = [(0, 0)] * grad_mixed.ndim
        widths[time_axis] = (offset, kernel_taps - 1 - offset)
        grad_padded = grad_padded + jnp.pad(grad_mixed * kernel_f[offset], widths)
    return (grad_kernel, grad_padded)


def combine_states(earlier, later):
    return (earlier[0] * later[0], later[0][:, :, None, None] * earlier[1] + later[1])


def local(
    hidden,
    norm_gain,
    w_gate_in,
    w_conv_in,
    w_step,
    conv_weight,
    conv_bias,
    step_bias,
    decay_log,
    skip_gain,
    gate_gain,
    w_out,
    cotangent,
):
    seq_count, length, model_width = hidden.shape
    gathered = (
        lax.all_gather(norm_gain, ("batch", "seq"), axis=0, tiled=True),
        lax.all_gather(w_gate_in, ("batch", "seq"), axis=0, tiled=True),
        lax.all_gather(w_conv_in, ("batch", "seq"), axis=0, tiled=True),
        lax.all_gather(w_step, ("batch", "seq"), axis=0, tiled=True),
        lax.all_gather(conv_weight, ("batch", "seq"), axis=1, tiled=True),
        lax.all_gather(conv_bias, ("batch", "seq"), axis=0, tiled=True),
        lax.all_gather(gate_gain, ("batch", "seq"), axis=0, tiled=True),
        lax.all_gather(w_out, ("batch", "seq"), axis=0, tiled=True),
    )
    (
        norm_full,
        gate_in_full,
        conv_in_full,
        step_full,
        kernel_full,
        bias_full,
        gain_full,
        out_full,
    ) = gathered
    inner_width = gate_in_full.shape[1]
    head_count = step_full.shape[1]
    head_width = inner_width // head_count
    channels = conv_in_full.shape[1]
    state_width = (channels - inner_width) // 2
    kernel_taps = kernel_full.shape[0]
    row_count = seq_count * length
    head_rate = -jnp.exp(decay_log)
    tokens_f = hidden.reshape(row_count, model_width).astype(jnp.float32)
    inv_rms = lax.rsqrt(jnp.mean(tokens_f * tokens_f, axis=1, keepdims=True) + norm_epsilon)
    unit = tokens_f * inv_rms
    normed = (unit * norm_full.astype(jnp.float32)[None]).astype(jnp.bfloat16)
    gate_pre = jnp.dot(normed, gate_in_full, preferred_element_type=jnp.float32)
    conv_pre = (
        jnp.dot(normed, conv_in_full, preferred_element_type=jnp.float32)
        .astype(jnp.bfloat16)
        .reshape(seq_count, length, channels)
    )
    raw_step = jnp.dot(normed, step_full, preferred_element_type=jnp.float32)
    rim = shifted(conv_pre[:, length - (kernel_taps - 1) :, :], "seq", 1)
    extended = jnp.concatenate([rim, conv_pre], axis=1).astype(jnp.float32)
    mixed_in = conv_apply(
        extended, kernel_full.astype(jnp.float32), bias_full.astype(jnp.float32), length
    )
    conv_out = jax.nn.silu(mixed_in).astype(jnp.bfloat16)
    value_b = conv_out[:, :, :inner_width].reshape(seq_count, length, head_count, head_width)
    key_b = conv_out[:, :, inner_width : inner_width + state_width]
    query_b = conv_out[:, :, inner_width + state_width :]
    step_size = jax.nn.softplus(raw_step + step_bias[None]).reshape(seq_count, length, head_count)

    def local_forward(value_piece, key_piece, query_piece, step_piece):
        parts = span_parts(value_piece, key_piece, query_piece, step_piece, head_rate)
        return (parts[0], parts[1], parts[2], parts[3])

    within, span_state, total_decay, cumulative = jax.vmap(local_forward)(
        value_b, key_b, query_b, step_size
    )
    identity = (jnp.ones_like(total_decay), jnp.zeros_like(span_state))
    _, carried = prefix((total_decay, span_state), "seq", combine_states, identity, False)
    inter = jax.vmap(span_inter)(query_b, cumulative, carried)
    value_f = value_b.astype(jnp.float32)
    ssm_out = within + inter + skip_gain[None, None, :, None] * value_f
    flat_out = ssm_out.reshape(row_count, inner_width)
    gate_silu = jax.nn.silu(gate_pre)
    gated = flat_out * gate_silu
    inv_gate = lax.rsqrt(jnp.mean(gated * gated, axis=1, keepdims=True) + norm_epsilon)
    normed_gate = gated * inv_gate
    projected_in = (normed_gate * gain_full.astype(jnp.float32)[None]).astype(jnp.bfloat16)
    output = (
        tokens_f + jnp.dot(projected_in, out_full, preferred_element_type=jnp.float32)
    ).astype(jnp.bfloat16)
    backward_weights = (
        lax.all_gather(norm_gain, ("batch", "seq"), axis=0, tiled=True),
        lax.all_gather(w_gate_in, ("batch", "seq"), axis=0, tiled=True),
        lax.all_gather(w_conv_in, ("batch", "seq"), axis=0, tiled=True),
        lax.all_gather(w_step, ("batch", "seq"), axis=0, tiled=True),
        lax.all_gather(conv_weight, ("batch", "seq"), axis=1, tiled=True),
        lax.all_gather(gate_gain, ("batch", "seq"), axis=0, tiled=True),
        lax.all_gather(w_out, ("batch", "seq"), axis=0, tiled=True),
    )
    norm_back, gate_in_back, conv_in_back, step_back, kernel_back, gain_back, out_back = (
        backward_weights
    )
    incoming = cotangent.reshape(row_count, model_width)
    grad_proj = jnp.dot(incoming, out_back.T, preferred_element_type=jnp.float32)
    grad_w_out = jnp.dot(projected_in.T, incoming, preferred_element_type=jnp.float32)
    grad_gate_gain = jnp.sum(grad_proj * normed_gate, axis=0)
    grad_ngate = grad_proj * gain_back.astype(jnp.float32)[None]
    grad_gated = inv_gate * (
        grad_ngate - normed_gate * jnp.mean(grad_ngate * normed_gate, axis=1, keepdims=True)
    )
    grad_flat = grad_gated * gate_silu
    grad_gate_pre = (grad_gated * flat_out * silu_slope(gate_pre)).astype(jnp.bfloat16)
    grad_ssm = grad_flat.reshape(seq_count, length, head_count, head_width)
    grad_skip = jnp.sum(grad_ssm * value_f, axis=(0, 1, 3))
    grad_carried = jax.vmap(carried_grad)(query_b, cumulative, grad_ssm)
    _, grad_state = prefix((total_decay, grad_carried), "seq", combine_states, identity, True)
    grad_total = jnp.sum(grad_state * carried, axis=(2, 3))

    def local_backward(
        value_piece,
        key_piece,
        query_piece,
        step_piece,
        carried_piece,
        grad_piece,
        state_piece,
        total_piece,
    ):
        return span_backward(
            value_piece,
            key_piece,
            query_piece,
            step_piece,
            carried_piece,
            grad_piece,
            state_piece,
            total_piece,
            head_rate,
        )

    grad_value, grad_key, grad_query, grad_steps, grad_rate = jax.vmap(local_backward)(
        value_b, key_b, query_b, step_size, carried, grad_ssm, grad_state, grad_total
    )
    grad_value = grad_value + grad_ssm * skip_gain[None, None, :, None]
    grad_conv_out = jnp.concatenate(
        [grad_value.reshape(seq_count, length, inner_width), grad_key, grad_query], axis=2
    )
    grad_mixed = grad_conv_out * silu_slope(mixed_in)
    grad_bias = jnp.sum(grad_mixed, axis=(0, 1))
    grad_kernel, grad_padded = conv_back(grad_mixed, extended, kernel_back.astype(jnp.float32))
    back_rim = shifted(for_sending(grad_padded[:, : kernel_taps - 1, :]), "seq", -1)
    grad_core = grad_padded[:, kernel_taps - 1 :, :]
    split_at = length - (kernel_taps - 1)
    grad_core = jnp.concatenate(
        [grad_core[:, :split_at], grad_core[:, split_at:] + back_rim], axis=1
    )
    grad_pre = grad_core.astype(jnp.bfloat16).reshape(row_count, channels)
    grad_raw = grad_steps.reshape(row_count, head_count) * jax.nn.sigmoid(
        raw_step + step_bias[None]
    )
    grad_step_bias = jnp.sum(grad_raw, axis=0)
    grad_raw_low = grad_raw.astype(jnp.bfloat16)
    grad_decay_log = jnp.sum(grad_rate, axis=0) * head_rate
    grad_w_gate_in = jnp.dot(normed.T, grad_gate_pre, preferred_element_type=jnp.float32)
    grad_w_conv_in = jnp.dot(normed.T, grad_pre, preferred_element_type=jnp.float32)
    grad_w_step = jnp.dot(normed.T, grad_raw_low, preferred_element_type=jnp.float32)
    grad_normed = jnp.dot(grad_gate_pre, gate_in_back.T, preferred_element_type=jnp.float32)
    grad_normed = grad_normed + jnp.dot(
        grad_pre, conv_in_back.T, preferred_element_type=jnp.float32
    )
    grad_normed = grad_normed + jnp.dot(
        grad_raw_low, step_back.T, preferred_element_type=jnp.float32
    )
    grad_norm_gain = jnp.sum(grad_normed * unit, axis=0)
    grad_unit = grad_normed * norm_back.astype(jnp.float32)[None]
    grad_tokens = inv_rms * (grad_unit - unit * jnp.mean(grad_unit * unit, axis=1, keepdims=True))
    grad_hidden = (incoming.astype(jnp.float32) + grad_tokens).reshape(
        seq_count, length, model_width
    )
    partial_grads = (
        grad_norm_gain,
        grad_w_gate_in,
        grad_w_conv_in,
        grad_w_step,
        grad_kernel,
        grad_bias,
        grad_gate_gain,
        grad_w_out,
    )
    shares = (
        lax.psum_scatter(partial_grads[0], ("batch", "seq"), scatter_dimension=0, tiled=True),
        lax.psum_scatter(partial_grads[1], ("batch", "seq"), scatter_dimension=0, tiled=True),
        lax.psum_scatter(partial_grads[2], ("batch", "seq"), scatter_dimension=0, tiled=True),
        lax.psum_scatter(partial_grads[3], ("batch", "seq"), scatter_dimension=0, tiled=True),
        lax.psum_scatter(partial_grads[4], ("batch", "seq"), scatter_dimension=1, tiled=True),
        lax.psum_scatter(partial_grads[5], ("batch", "seq"), scatter_dimension=0, tiled=True),
        lax.psum_scatter(partial_grads[6], ("batch", "seq"), scatter_dimension=0, tiled=True),
        lax.psum_scatter(partial_grads[7], ("batch", "seq"), scatter_dimension=0, tiled=True),
    )
    head_sums = lax.psum((grad_step_bias, grad_decay_log, grad_skip), ("batch", "seq"))
    return (
        output.reshape(seq_count, length, model_width),
        grad_hidden,
        shares[0],
        shares[1],
        shares[2],
        shares[3],
        shares[4],
        shares[5],
        head_sums[0],
        head_sums[1],
        head_sums[2],
        shares[6],
        shares[7],
    )


bf16 = jnp.bfloat16
f32 = jnp.float32
EXACT = lax.Precision.HIGHEST
LANES = 128


def mm(former, latter, dims=((1,), (0,))):
    return lax.dot_general(former, latter, (dims, ((), ())), preferred_element_type=f32)


def mm_exact(former, latter, dims=((1,), (0,))):
    return lax.dot_general(
        former, latter, (dims, ((), ())), precision=EXACT, preferred_element_type=f32
    )


def halves(array):
    high = array.astype(bf16)
    return high, (array - high.astype(f32)).astype(bf16)


def iota(shape, axis):
    return lax.broadcasted_iota(jnp.int32, shape, axis)


def head_map(own, head_width):
    return (iota((LANES, own), 0) == iota((LANES, own), 1) // head_width).astype(f32)


def triangle_sum(table, array):
    high, low = halves(array)
    table = table.astype(bf16)
    return mm(jnp.concatenate([table, table], axis=1), jnp.concatenate([high, low], axis=0))


def twice(array):
    return jnp.concatenate([array, array], axis=1)


def stacked_halves(array):
    return jnp.concatenate(halves(array), axis=0)


def step_tables(raw, rate):
    span = raw.shape[0]
    step = jnp.maximum(raw, 0.0) + jnp.log1p(jnp.exp(-jnp.abs(raw)))
    return step, triangle_sum(iota((span, span), 0) >= iota((span, span), 1), step * rate)


def pair_masked(array, head_width):
    low = iota(array.shape, 1) < head_width
    zero = jnp.zeros_like(array)
    return jnp.concatenate([jnp.where(low, array, zero), jnp.where(low, zero, array)], axis=0)


def by_pair_lanes(array, pair, head_width):
    shape = (array.shape[0], 2 * head_width)
    first = jnp.broadcast_to(array[:, 2 * pair : 2 * pair + 1], shape)
    second = jnp.broadcast_to(array[:, 2 * pair + 1 : 2 * pair + 2], shape)
    return jnp.where(iota(shape, 1) < head_width, first, second)


def place(i, rank):
    m = lax.bitwise_xor(i, rank)
    return 4 * lax.bitwise_and(m, 1) + lax.shift_right_logical(m, 1)


def span_at(place_index, rank):
    m = 2 * lax.bitwise_and(place_index, 3) + lax.shift_right_logical(place_index, 2)
    return lax.bitwise_xor(m, rank)


def project_kernel(
    where_ref, t0, t1, t2, t3, t4, t5, t6, t7, gain_ref, w0, w1, w2, w3, shared_ref,
    normed_ref, pre_ref, raw_ref, weight_ref, *, states,
):
    step = pl.program_id(0)
    plane = where_ref[1]
    span, width = t0.shape
    own = w0.shape[1]
    block = width // 4

    @pl.when(step == 0)
    def _():
        for o, w in enumerate((w0, w1, w2, w3)):
            weight_ref[o * block : (o + 1) * block, :own] = w[...]
        weight_ref[:, own:] = shared_ref[...]

    parts = (t0, t1, t2, t3, t4, t5, t6, t7)
    for half in range(4):

        @pl.when(step == half)
        def _(half=half):
            for i in range(2):
                part = parts[2 * half + i]
                tokens = part[...].astype(f32)
                inv_rms = lax.rsqrt(jnp.mean(tokens * tokens, axis=1, keepdims=True) + norm_epsilon)
                for o in range(4):
                    at = pl.multiple_of(lax.bitwise_and(plane - o + 4, 3) * block, LANES)
                    value = part[:, pl.ds(at, block)].astype(f32) * inv_rms
                    value = (value * gain_ref[:, pl.ds(at, block)]).astype(bf16)
                    normed_ref[i * span : (i + 1) * span, o * block : (o + 1) * block] = value

    product = mm(normed_ref[...], weight_ref[...])
    local = own + 2 * states
    pre_ref[...] = product[:, :local].astype(bf16)
    raw_ref[...] = product[:, local:]


def forward_kernel(
    where_ref, pre_ref, raw_ref, taps_ref, heads_ref, rows_ref,
    mixed_ref, conv_ref, inter_ref, ssm_ref, state_ref,
    ext, state, *, n_taps, head_width, states,
):
    span, own = ssm_ref.shape[1:]

    @pl.when(pl.program_id(0) == 0)
    def _():
        ext[0:8, :] = jnp.zeros((8, ext.shape[1]), f32)
        state[...] = jnp.zeros_like(state)

    ext[8 : 8 + span, :] = pre_ref[0].astype(f32)
    mixed = taps_ref[n_taps : n_taps + 1, :]
    for k in range(n_taps):
        first = 8 - (n_taps - 1) + k
        mixed = mixed + taps_ref[k : k + 1, :] * ext[first : first + span, :]
    mixed_ref[0] = mixed
    ext[0:8, :] = ext[span : span + 8, :]
    conv = (mixed * jax.nn.sigmoid(mixed)).astype(bf16)
    conv_ref[0] = conv
    key, query = conv[:, own : own + states], conv[:, own + states :]
    step, cum = step_tables(raw_ref[0] + heads_ref[0:1, :], heads_ref[1:2, :])
    cum_t, step_t = cum.T, step.T
    affinity = mm(query, key, ((1,), (1,)))
    causal = iota((span, span), 0) >= iota((span, span), 1)
    entering = state[...]
    state_ref[0] = entering
    base = mm(twice(query), stacked_halves(entering))
    weighted, kept = [], []
    for pair in range(own // (2 * head_width)):
        lanes = slice(2 * pair * head_width, 2 * (pair + 1) * head_width)
        value = conv_ref[0, :, lanes]
        mixing = []
        for h in (2 * pair, 2 * pair + 1):
            decay = jnp.exp(jnp.where(causal, cum[:, h : h + 1] - cum_t[h : h + 1, :], -1e30))
            mixing.append((affinity * decay * step_t[h : h + 1, :]).astype(bf16))
        cum_pair = by_pair_lanes(cum, pair, head_width)
        growth = jnp.exp(cum_pair)
        tailed = jnp.exp(cum_pair[span - 1 : span, :] - cum_pair) * by_pair_lanes(step, pair, head_width)
        inter = growth * base[:, lanes]
        inter_ref[0, :, lanes] = inter
        value_f = value.astype(f32)
        within = mm(jnp.concatenate(mixing, axis=1), pair_masked(value, head_width))
        ssm_ref[0, :, lanes] = within + inter + rows_ref[1:2, lanes] * value_f
        weighted.append((tailed * value_f).astype(bf16))
        kept.append(growth[span - 1 : span, :])
    weighted, kept = jnp.concatenate(weighted, axis=1), jnp.concatenate(kept, axis=1)
    state[...] = kept * entering + mm(key, weighted, ((0,), (0,)))


def gate_kernel(
    where_ref, normed_ref, g0, g1, g2, g3, c0, c1, c2, c3, c4, c5, c6, c7, out_ref, rows_ref, ssm_ref,
    gate_ref, ngate_ref, sums_ref, mine_ref, other_ref, weight_ref, cot_ref,
):
    step = pl.program_id(0)
    block = g0.shape[0]
    span = c0.shape[0]

    @pl.when(step == 0)
    def _():
        for o, w in enumerate((g0, g1, g2, g3)):
            weight_ref[o * block : (o + 1) * block, :] = w[...]

    parts = (c0, c1, c2, c3, c4, c5, c6, c7)
    for half in range(4):

        @pl.when(step == half)
        def _(half=half):
            for i in range(2):
                cot_ref[i * span : (i + 1) * span, :] = parts[2 * half + i][...]

    gate = mm(normed_ref[...], weight_ref[...])
    gate_ref[...] = gate
    gated = ssm_ref[...] * (gate * jax.nn.sigmoid(gate))
    gain = rows_ref[0:1, :]
    ngate = mm(cot_ref[...], out_ref[...], ((1,), (1,))) * gain
    ngate_ref[...] = ngate
    squares, cross = gated * gated, ngate * gated
    for i in range(2):
        rows = slice(i * span, (i + 1) * span)
        sums = []
        for product in (squares[rows], cross[rows]):
            folded = product[:, :LANES] + product[:, LANES : 2 * LANES] + product[:, 2 * LANES :]
            sums.append(jnp.sum(folded.T, axis=0, keepdims=True))
        row = iota((8, LANES), 0)
        sums_ref[span_at(2 * step + i, where_ref[0])] = jnp.where(row == 0, sums[0], sums[1])
    part = mm((gated * gain).astype(bf16), out_ref[...]).astype(bf16)

    @pl.when(step < 2)
    def _():
        mine_ref[...] = part

    @pl.when(step >= 2)
    def _():
        other_ref[...] = part


def gate_back_kernel(
    where_ref, sums_ref, ssm_ref, gate_ref, ngate_ref, rows_ref,
    grad_ref, grad_gate_ref, projected_ref, lent_ref, *, inner, third,
):
    step = pl.program_id(0)
    rows, own = ssm_ref.shape
    core = lax.bitwise_and(where_ref[0], 1)
    lent_ref[...] = jnp.zeros_like(lent_ref)
    span = LANES
    for i in range(rows // span):
        at = slice(i * span, (i + 1) * span)
        sums = sums_ref[span_at(rows // span * step + i, where_ref[0])]
        sums = jnp.concatenate([sums, jnp.zeros((LANES - 8, LANES), f32)], axis=0).T
        inv_gate = lax.rsqrt(sums[:, 0:1] / inner + norm_epsilon)
        mean = inv_gate * sums[:, 1:2] / inner
        inv_gate = jnp.broadcast_to(inv_gate, (span, own))
        ssm, gate = ssm_ref[at], gate_ref[at]
        logistic = jax.nn.sigmoid(gate)
        silu = gate * logistic
        normed = ssm * silu * inv_gate
        grad_gated = inv_gate * (ngate_ref[at] - normed * mean)
        grad_ref[at] = grad_gated * silu
        slope = logistic * (1.0 + gate * (1.0 - logistic))
        grad_gate_ref[at] = (grad_gated * ssm * slope).astype(bf16)
        projected_ref[at] = (normed * rows_ref[0:1, :]).astype(bf16)
    for k in range(2):

        @pl.when(core == k)
        def _(k=k):
            for plane, first, _, count in local_slices(k, 2 * third):
                if count == 4 * third:
                    source = first + 3 * third if k == 0 else first
                    to = plane // 2 * third
                    lent_ref[:, to : to + third] = projected_ref[:, source : source + third]


def early_grads_kernel(
    where_ref, normed_ref, grad_gate_ref, projected_ref, borrowed_ref, c0, c1, c2, c3, c4, c5, c6, c7,
    b0, b1, b2, b3, cot_ref, rows_ref, total_ref, *, third,
):
    step = pl.program_id(0)
    core, plane = lax.bitwise_and(where_ref[0], 1), where_ref[1]
    span = c0.shape[0]
    rows = 3 * third
    block = normed_ref.shape[1]
    half = normed_ref.shape[0] // 2

    def swap(to, lent):
        rows_ref[:half, to] = borrowed_ref[half:, lent]
        rows_ref[half:, to] = borrowed_ref[:half, lent]

    @pl.when(step == 0)
    def _():
        for i, part in enumerate((c0, c1, c2, c3, c4, c5, c6, c7)):
            cot_ref[i * span : (i + 1) * span, :] = part[...]
        for k in range(2):

            @pl.when(core == k)
            def _(k=k):
                for at_plane, at, _, count in local_slices(k, 2 * third):
                    to = at_plane * rows
                    lent = slice(at_plane // 2 * third, (at_plane // 2 + 1) * third)
                    if count == rows + third:
                        own_at = at if k == 0 else at + third
                        rows_ref[:, to : to + rows] = projected_ref[:, own_at : own_at + rows]
                    elif k == 0:
                        rows_ref[:, to : to + count] = projected_ref[:, at : at + count]
                        swap(slice(to + count, to + rows), lent)
                    else:
                        rows_ref[:, to + third : to + rows] = projected_ref[:, at : at + count]
                        swap(slice(to, to + third), lent)

        total_ref[...] = mm(rows_ref[...], cot_ref[...], ((0,), (0,))).astype(bf16)

    gate = mm(normed_ref[...], grad_gate_ref[...], ((0,), (0,))).astype(bf16)
    first = pl.multiple_of(rows * lax.bitwise_and(plane - step + 4, 3), third)
    for o, out_ref in enumerate((b0, b1, b2, b3)):

        @pl.when(step == o)
        def _(out_ref=out_ref):
            out_ref[:block, :] = gate
            for g in range(4):
                own = total_ref[pl.ds(first, rows), g * block : (g + 1) * block]
                out_ref[block + g * rows : block + (g + 1) * rows, :] = own


def backward_kernel(
    where_ref, grad_ref, inter_ref, state_ref, conv_ref, pre_ref, mixed_ref, raw_ref,
    taps_ref, heads_ref, rows_ref,
    grad_pre_ref, grad_taps_ref, grad_heads_ref,
    ext, grad_state, next_state, *, n_taps, head_width, states,
):
    span, own = grad_ref.shape[1:]

    @pl.when(pl.program_id(0) == 0)
    def _():
        ext[span : span + 8, :] = jnp.zeros((8, ext.shape[1]), f32)
        grad_state[...] = jnp.zeros_like(grad_state)
        next_state[...] = jnp.zeros_like(next_state)
        grad_taps_ref[...] = jnp.zeros_like(grad_taps_ref)
        grad_heads_ref[...] = jnp.zeros_like(grad_heads_ref)

    key, query = conv_ref[0, :, own : own + states], conv_ref[0, :, own + states :]
    rate = heads_ref[1:2, :]
    raw = raw_ref[0] + heads_ref[0:1, :]
    step, cum = step_tables(raw, rate)
    cum_t, step_t = cum.T, step.T
    tail = jnp.exp(cum[span - 1 : span, :] - cum)
    affinity = mm(query, key, ((1,), (1,)))
    causal = iota((span, span), 0) >= iota((span, span), 1)
    after = grad_state[...]
    after_halves = stacked_halves(after)
    grad_weighted = mm(twice(key), after_halves)
    grad_affinity = jnp.zeros((span, span), f32)
    direct_t = jnp.zeros((span, span), f32)
    grad_cum = jnp.zeros((span, LANES), f32)
    row, lane = iota((span, span), 0), iota((span, LANES), 1)
    weighted, grown, grown_rest, kept = [], [], [], []
    products = [[], [], []]
    mixed = mixed_ref[0]
    logistic = jax.nn.sigmoid(mixed)
    slope = logistic * (1.0 + mixed * (1.0 - logistic))
    for pair in range(own // (2 * head_width)):
        lanes = slice(2 * pair * head_width, 2 * (pair + 1) * head_width)
        value, grad_y = conv_ref[0, :, lanes], grad_ref[0, :, lanes]
        value_f, grad_low = value.astype(f32), grad_y.astype(bf16)
        cum_pair = by_pair_lanes(cum, pair, head_width)
        growth = jnp.exp(cum_pair)
        tailed = jnp.exp(cum_pair[span - 1 : span, :] - cum_pair) * by_pair_lanes(step, pair, head_width)
        kept.append(growth[span - 1 : span, :])
        high, low = halves(grad_y * growth)
        grown.append(high)
        grown_rest.append(low)
        weighted.append((tailed * value_f).astype(bf16))
        grad_mixing = mm(grad_low, pair_masked(value, head_width), ((1,), (1,)))
        mixing = []
        for i in (0, 1):
            h = 2 * pair + i
            given = grad_mixing[:, i * span : (i + 1) * span]
            decay = jnp.exp(jnp.where(causal, cum[:, h : h + 1] - cum_t[h : h + 1, :], -1e30))
            grad_affinity = grad_affinity + given * decay * step_t[h : h + 1, :]
            table = affinity * decay
            scores = table * step_t[h : h + 1, :]
            mixing.append(scores.astype(bf16))
            direct_t = jnp.where(row == h, jnp.sum(given * table, axis=0, keepdims=True), direct_t)
            grad_cum = jnp.where(lane == h, jnp.sum(given * scores, axis=1, keepdims=True), grad_cum)
        grad_value = mm(jnp.concatenate(mixing, axis=0), pair_masked(grad_low, head_width), ((0,), (0,)))
        by_state = grad_weighted[:, lanes]
        grad_value = grad_value + tailed * by_state + rows_ref[1:2, lanes] * grad_y
        ext[0:span, lanes] = grad_value * slope[:, lanes]
        products[0].append(by_state * value_f)
        products[1].append(grad_y * inter_ref[0, :, lanes])
        products[2].append(jnp.sum(grad_y * value_f, axis=0, keepdims=True))
    weighted, grown = jnp.concatenate(weighted, axis=1), jnp.concatenate(grown, axis=1)
    grown_rest, kept = jnp.concatenate(grown_rest, axis=1), jnp.concatenate(kept, axis=1)
    grad_affinity = grad_affinity.astype(bf16)
    grad_query = mm(grown, state_ref[0].astype(bf16), ((1,), (1,))) + mm(grad_affinity, key)
    grad_key = mm(weighted, after_halves[:states], ((1,), (1,))) + mm(grad_affinity, query, ((0,), (0,)))
    ext[0:span, own : own + states] = grad_key * slope[:, own : own + states]
    ext[0:span, own + states :] = grad_query * slope[:, own + states :]
    to_lanes = head_map(own, head_width).astype(bf16)
    last = jnp.sum(after * next_state[...], axis=0, keepdims=True)
    by_head = jnp.concatenate(
        [
            jnp.concatenate(products[0], axis=1),
            jnp.concatenate(products[1], axis=1),
            jnp.broadcast_to(jnp.concatenate(products[2], axis=1), (8, own)),
            jnp.broadcast_to(last, (8, own)),
        ],
        axis=0,
    )
    high, low = halves(by_head)
    by_head = mm(high, to_lanes, ((1,), (1,))) + mm(low, to_lanes, ((1,), (1,)))
    direct = direct_t.T + by_head[:span] * tail
    grad_cum = grad_cum + by_head[span : 2 * span] - step * direct
    last = by_head[2 * span + 8 : 2 * span + 9]
    grad_cum = grad_cum + jnp.where(iota(grad_cum.shape, 0) == span - 1, last, 0.0)
    grad_log = triangle_sum(iota((span, span), 0) <= iota((span, span), 1), grad_cum)
    grad_raw = (direct + grad_log * rate) * jax.nn.sigmoid(raw)
    grad_heads_ref[0:1, :] += jnp.sum(grad_raw, axis=0, keepdims=True)
    grad_heads_ref[1:2, :] += jnp.sum(grad_log * step, axis=0, keepdims=True) * rate
    grad_heads_ref[2:3, :] += by_head[2 * span : 2 * span + 1]
    pre = pre_ref[0].astype(f32)
    grad_pre = jnp.zeros(pre.shape, f32)
    for k in range(n_taps):
        ahead = ext[n_taps - 1 - k : n_taps - 1 - k + span, :]
        grad_pre = grad_pre + ahead * taps_ref[k : k + 1, :]
        grad_taps_ref[k : k + 1, :] += jnp.sum(ahead * pre, axis=0, keepdims=True)
    grad_taps_ref[n_taps : n_taps + 1, :] += jnp.sum(ext[0:span, :], axis=0, keepdims=True)
    ext[span : span + 8, :] = ext[0:8, :]
    grad_pre_ref[0, :, : own + 2 * states] = grad_pre.astype(bf16)
    grad_pre_ref[0, :, own + 2 * states :] = grad_raw.astype(bf16)
    grad_state[...] = kept * after + mm(
        jnp.concatenate([query, query], axis=0), jnp.concatenate([grown, grown_rest], axis=0), ((0,), (0,))
    )
    next_state[...] = state_ref[0]


def input_grad_kernel(gate_ref, rest_ref, w_gate_ref, w_rest_ref, mine_ref, other_ref):
    half = mine_ref.shape[0]
    total = mm(gate_ref[...], w_gate_ref[...], ((1,), (1,))) + mm(rest_ref[...], w_rest_ref[...], ((1,), (1,)))
    mine_ref[...] = total[:half].astype(bf16)
    other_ref[...] = total[half:].astype(bf16)


def input_grad_call(gate, rest, w_gate, w_rest):
    half, width, block = gate.shape[0] // 2, w_gate.shape[0], w_gate.shape[0] // 3
    return pl.pallas_call(
        input_grad_kernel,
        out_shape=[jax.ShapeDtypeStruct((half, width), bf16)] * 2,
        grid=(3,),
        in_specs=[pl.BlockSpec(a.shape, lambda i: (0, 0)) for a in (gate, rest)]
        + [pl.BlockSpec((block, a.shape[1]), lambda i: (i, 0)) for a in (w_gate, w_rest)],
        out_specs=[pl.BlockSpec((half, block), lambda i: (0, i))] * 2,
    )(gate, rest, w_gate, w_rest)


def by_span(shape, order):
    return pl.BlockSpec((1, *shape), lambda i, where: (order(i, where), 0, 0))


def spans_call(kernel, where, spans, inputs, outputs, scratch=()):
    in_specs = [
        by_span(a.shape[1:], order) if order else pl.BlockSpec(a.shape, lambda i, where, n=a.ndim: (0,) * n)
        for a, order in inputs
    ]
    out_specs = [
        by_span(shape, order) if order else pl.BlockSpec(shape, lambda i, where, n=len(shape): (0,) * n)
        for shape, _, order in outputs
    ]
    out_shape = [
        jax.ShapeDtypeStruct(
            (spans, *shape) if order else shape, dtype
        )
        for shape, dtype, order in outputs
    ]
    return pl.pallas_call(
        kernel,
        out_shape=out_shape,
        grid_spec=pltpu.PrefetchScalarGridSpec(
            num_scalar_prefetch=1,
            grid=(spans,),
            in_specs=in_specs,
            out_specs=out_specs,
            scratch_shapes=list(scratch),
        ),
        compiler_params=pltpu.CompilerParams(dimension_semantics=("arbitrary",)),
    )(where, *[a for a, _ in inputs])


def in_time(i, where):
    return i


def in_reverse(i, where):
    return 7 - i


def relative(i, where):
    return place(i, where[0])


def relative_reverse(i, where):
    return place(7 - i, where[0])


class Columns(typing.NamedTuple):
    shape: tuple


def rows_call(kernel, where, steps, rows, inputs, outputs, scratch=()):
    def spec(shape, index):
        if isinstance(index, Columns):
            return pl.BlockSpec(index.shape, lambda i, where: (0, i))
        if index is None:
            return pl.BlockSpec(shape, lambda i, where, n=len(shape): (0,) * n)
        return pl.BlockSpec((rows, *shape[1:]), lambda i, where: (index(i), 0))

    return pl.pallas_call(
        kernel,
        out_shape=[jax.ShapeDtypeStruct(shape, dtype) for shape, dtype, _ in outputs],
        grid_spec=pltpu.PrefetchScalarGridSpec(
            num_scalar_prefetch=1,
            grid=(steps,),
            in_specs=[spec(a.shape, index) for a, index in inputs],
            out_specs=[spec(shape, index) for shape, _, index in outputs],
            scratch_shapes=list(scratch),
        ),
    )(where, *[a for a, _ in inputs])


def each(i):
    return i


def lower(i):
    return lax.min(i, 1)


def upper(i):
    return lax.max(i - 2, 0)


def local_slices(core, width):
    at, slices = 0, []
    for plane in range(4):
        count = 2 * width if plane % 2 == core else width
        slices.append((plane, at, 0 if core == 0 else 3 * width - count, count))
        at += count
    return slices


def pack_kernel(
    gate_ref, conv_ref, step_ref, norm_ref, gain_ref, bias_ref, taps_ref,
    cols_ref, message_ref, *, head_width,
):
    inner = gate_ref.shape[1]
    group = 3 * head_width
    for chip in range(4):
        for core in range(2):
            for plane, at, start, count in local_slices(core, head_width):
                source = group * (4 * plane + chip) + start
                for first, ref in ((0, conv_ref), (cols_ref.shape[2] // 2, gate_ref)):
                    to = slice(first + at, first + at + count)
                    cols_ref[2 * chip + core, :, to] = ref[:, source : source + count]
    rest = conv_ref.shape[1] - inner
    rows = gate_ref.shape[0]
    message_ref[...] = jnp.zeros_like(message_ref)
    message_ref[:rows, :rest] = conv_ref[:, inner:]
    message_ref[:rows, rest : rest + step_ref.shape[1]] = step_ref[...]
    vectors = jnp.zeros((8, LANES), f32)

    def put(vectors, ref, at):
        value = ref[...].astype(f32)
        value = jnp.pad(value, ((at, 8 - at - value.shape[0]), (0, LANES - value.shape[1])))
        return vectors + value

    for ref, at in ((norm_ref, 0), (gain_ref, 1), (bias_ref, 2), (taps_ref, 3)):
        vectors = put(vectors, ref, at)
    message_ref[rows:, :LANES] = vectors.astype(bf16)


def setup_kernel(
    where_ref, mine_ref, other_ref, heads_ref,
    shared_ref, norm_ref, taps_ref, channels_ref, head_rows_ref, pick_ref,
    gain_all, taps_all, held, *, n_taps, head_width,
):
    rank, plane = where_ref[0], where_ref[1]
    padded = shared_ref.shape[1]
    rows = norm_ref.shape[1] // 32
    block = 8 * rows
    rows_in, rows_out = norm_ref.shape[1] // 32, gain_all.shape[1] // 32
    piece = taps_all.shape[1] // 32
    inner = gain_all.shape[1]
    own = channels_ref.shape[1]
    for p in range(8):
        source = lax.bitwise_xor(rank, 2 * (p % 4) + p // 4)
        part_ref, top = (mine_ref, other_ref)[p // 4], p % 4 * (rows + 8)
        for o in range(4):
            at = pl.multiple_of(o * block + source * rows, 16)
            lanes = slice(o * padded, (o + 1) * padded)
            shared_ref[pl.ds(at, rows), :] = part_ref[top : top + rows, lanes]
            device = 8 * lax.bitwise_and(plane - o + 4, 3) + source
            held[device] = part_ref[top + rows : top + rows + 8, o * padded : o * padded + LANES].astype(f32)
    for i in range(32):
        vectors = held[i]
        norm_ref[:, i * rows_in : (i + 1) * rows_in] = vectors[0:1, :rows_in]
        gain_all[:, i * rows_out : (i + 1) * rows_out] = vectors[1:2, :rows_out]
        taps_all[:, i * piece : (i + 1) * piece] = vectors[:, :piece]
    taps_ref[...] = jnp.zeros_like(taps_ref)
    channels_ref[...] = jnp.zeros_like(channels_ref)
    taps_ref[0:n_taps, own:] = taps_all[3 : 3 + n_taps, inner:]
    taps_ref[n_taps : n_taps + 1, own:] = taps_all[2:3, inner:]
    for r in range(8):

        @pl.when(rank == r)
        def _(r=r):
            chip, core = r // 2, r % 2
            local, heads = iota((LANES, LANES), 0), iota((LANES, LANES), 1)
            chosen = jnp.zeros((LANES, LANES), jnp.bool_)
            for plane, at, start, count in local_slices(core, head_width):
                source = 3 * head_width * (4 * plane + chip) + start
                taps_ref[0:n_taps, at : at + count] = taps_all[3 : 3 + n_taps, source : source + count]
                taps_ref[n_taps : n_taps + 1, at : at + count] = taps_all[2:3, source : source + count]
                channels_ref[0:1, at : at + count] = gain_all[:, source : source + count]
                for j in range(count // head_width):
                    chosen |= (local == at // head_width + j) & (heads == source // head_width + j)
            pick_ref[...] = chosen.astype(f32)

    states = (padded - LANES) // 2
    chosen = pick_ref[...].astype(bf16)
    shared_ref[:, 2 * states :] = mm(shared_ref[:, 2 * states :], chosen, ((1,), (1,))).astype(bf16)
    head_rows = mm_exact(heads_ref[...], pick_ref[...], ((1,), (1,)))
    used = iota((1, LANES), 1) < own // head_width
    head_rows_ref[...] = jnp.zeros_like(head_rows_ref)
    head_rows_ref[0:1, :] = head_rows[0:1]
    head_rows_ref[1:2, :] = jnp.where(used, -jnp.exp(head_rows[1:2]), 0.0)
    channels_ref[1:2, :] = mm_exact(head_rows, head_map(own, head_width))[2:3]


def out_rows_kernel(where_ref, p0, p1, p2, p3, borrowed_ref, out_ref):
    rank, plane = where_ref[0], where_ref[1]
    core = lax.bitwise_and(rank, 1)
    rows = p0.shape[0]
    third = rows // 3
    for o, part in enumerate((p0, p1, p2, p3)):
        at_plane = lax.bitwise_and(plane - o + 4, 3)
        for k in range(2):
            for slices_plane, at, _, count in local_slices(k, 2 * third):

                @pl.when((core == k) & (at_plane == slices_plane))
                def _(o=o, part=part, k=k, at=at, count=count):
                    if count == rows + third and k == 0:
                        out_ref[at : at + rows, :] = part[...]
                        out_ref[at + rows : at + count, :] = borrowed_ref[o // 2]
                    elif count == rows + third:
                        out_ref[at : at + third, :] = borrowed_ref[o // 2]
                        out_ref[at + third : at + count, :] = part[...]
                    elif k == 0:
                        out_ref[at : at + count, :] = part[: 2 * third, :]
                    else:
                        out_ref[at : at + count, :] = part[third:, :]


def lend_kernel(where_ref, p0, p1, p2, p3, out_ref):
    core, plane = lax.bitwise_and(where_ref[0], 1), where_ref[1]
    third = out_ref.shape[1]
    odd = lax.bitwise_and(plane + 1 + core, 1)
    for o, part in enumerate((p0, p1, p2, p3)):
        for k in range(2):

            @pl.when((odd == o % 2) & (core == k))
            def _(o=o, part=part, k=k):
                out_ref[o // 2] = part[2 * third :, :] if k == 0 else part[:third, :]


def total_of(refs, rows=slice(None)):
    total = refs[0][rows].astype(f32)
    for ref in refs[1:]:
        total = total + ref[rows].astype(f32)
    return total


def as_row(column, count):
    return jnp.broadcast_to(column, (column.shape[0], LANES)).T[:1, :count]


def early_rows_kernel(p0, p1, p2, w_ref, gain_ref, gate_ref, out_ref, dot_ref):
    block = gate_ref.shape[0]
    rows = out_ref.shape[0]
    gate_ref[...] = total_of((p0, p1, p2), slice(0, block)).astype(bf16)
    for g in range(4):
        at = block + g * rows
        out_ref[:, g * block : (g + 1) * block] = total_of((p0, p1, p2), slice(at, at + rows))
    dot = jnp.sum(w_ref[...].astype(f32) * out_ref[...], axis=1, keepdims=True)
    dot_ref[...] = as_row(dot, rows) / gain_ref[...].astype(f32)


def late_rows_kernel(gate_ref, c0, c1, c2, c3, out_ref):
    own = gate_ref.shape[1]
    rows = out_ref.shape[1]
    for r in range(8):
        at = slice(r * rows, (r + 1) * rows)
        out_ref[r, :, :own] = gate_ref[at, :]
        out_ref[r, :, own:] = total_of((c0, c1, c2, c3), at).astype(bf16)


def columns_kernel(
    table_ref, w_gate_ref, w_conv_ref, w_step_ref, gain_ref, s0, s1, s2, s3,
    gate_ref, conv_ref, dot_ref, step_ref, taps_ref, bias_ref, step_bias_ref, decay_ref, skip_ref, *, head_width,
):
    group = 3 * head_width
    inner = 16 * group
    half = table_ref.shape[2] // 2
    for chip in range(4):
        for core in range(2):
            for plane, at, start, count in local_slices(core, head_width):
                to = slice(group * (4 * plane + chip) + start, group * (4 * plane + chip) + start + count)
                gate_ref[:, to] = table_ref[2 * chip + core, :, at : at + count].astype(f32)
                conv_ref[:, to] = table_ref[2 * chip + core, :, half + at : half + at + count].astype(f32)
    rows = gate_ref.shape[0]
    rest = conv_ref.shape[1] - inner
    shared = total_of((s0, s1, s2, s3))
    conv_ref[:, inner:] = shared[:rows, :rest]
    step_ref[...] = shared[:rows, rest : rest + step_ref.shape[1]]
    small = shared[rows:, :LANES] + shared[rows:, LANES : 2 * LANES]
    at = 0
    for ref in (taps_ref, bias_ref, step_bias_ref, decay_ref, skip_ref):
        ref[...] = small[at : at + ref.shape[0], : ref.shape[1]]
        at += ref.shape[0]
    total = jnp.sum(w_step_ref[...].astype(f32) * step_ref[...], axis=1, keepdims=True)
    for weight_ref, grad_ref in ((w_gate_ref, gate_ref), (w_conv_ref, conv_ref)):
        total = total + jnp.sum(weight_ref[...].astype(f32) * grad_ref[...], axis=1, keepdims=True)
    dot_ref[...] = as_row(total, rows) / gain_ref[...].astype(f32)


def tokens_out_kernel(
    where_ref, o0, o1, o2, o3, g0, g1, g2, g3, hidden_ref, cot_ref, sums_ref, norm_ref,
    output_ref, grad_ref, held, *, inner,
):
    rank, plane = where_ref[0], where_ref[1]
    tokens = hidden_ref[...].astype(f32)
    sums = jnp.concatenate([sums_ref[rank], jnp.zeros((LANES - 8, LANES), f32)], axis=0).T
    inv_gate = lax.rsqrt(sums[:, 0:1] / inner + norm_epsilon)
    output_ref[...] = (tokens + inv_gate * total_of((o0, o1, o2, o3))).astype(bf16)
    inv_rms = lax.rsqrt(jnp.mean(tokens * tokens, axis=1, keepdims=True) + norm_epsilon)
    width = tokens.shape[1]
    block = width // 4
    grad_ref[...] = total_of((g0, g1, g2, g3))
    for p in range(4):
        at = pl.multiple_of(block * lax.bitwise_and(plane - p + 4, 3), LANES)
        lanes = slice(p * block, (p + 1) * block)
        held[:, lanes] = grad_ref[:, pl.ds(at, block)] * norm_ref[:, lanes]
    grad_unit, unit = held[...], tokens * inv_rms
    mean = jnp.mean(grad_unit * unit, axis=1, keepdims=True)
    grad_ref[...] = cot_ref[...].astype(f32) + inv_rms * (grad_unit - unit * mean)


def once(kernel, inputs, outputs, where=None, scratch=()):
    specs = lambda shapes: [pl.BlockSpec(s, lambda *_, n=len(s): (0,) * n) for s in shapes]
    out_shape = [jax.ShapeDtypeStruct(shape, dtype) for shape, dtype in outputs]
    grid_spec = pltpu.PrefetchScalarGridSpec(
        num_scalar_prefetch=0 if where is None else 1,
        grid=(1,),
        in_specs=specs([a.shape for a in inputs]),
        out_specs=specs([shape for shape, _ in outputs]),
        scratch_shapes=list(scratch),
    )
    call = pl.pallas_call(kernel, out_shape=out_shape, grid_spec=grid_spec)
    return call(*([] if where is None else [where]), *inputs)


def hop(value, distance):
    count = lax.axis_size("seq")
    pairs = [(i, i ^ distance) for i in range(count)]
    return lax.ppermute(value, "seq", pairs)


def plane_hop(value, distance):
    count = lax.axis_size("batch")
    pairs = [(i, (i + distance) % count) for i in range(count)]
    return lax.ppermute(value, "batch", pairs)


def planes_gather(value, direct=False):
    one, three = plane_hop(value, 1), plane_hop(value, -1)
    two = plane_hop(value, 2) if direct else plane_hop(one, 1)
    return [value, one, two, three]


def planes_parts(blocks):
    near, far = plane_hop(blocks[1], -1), plane_hop(blocks[2], 1)
    sent = (blocks[3].astype(f32) + far.astype(f32)).astype(blocks[3].dtype)
    return [blocks[0], near, plane_hop(sent, 1)]


def planes_direct(blocks):
    return [blocks[0]] + [plane_hop(blocks[o], -o) for o in (1, 2, 3)]


def plane_gather(value):
    chips = [value] + [hop(value, distance) for distance in (2, 4, 6)]
    return chips + [hop(part, 1) for part in chips]


def small_gather(value):
    mine = jnp.concatenate([value] + [hop(value, distance) for distance in (2, 4, 6)])
    return mine, hop(mine, 1)


def plane_parts(mine, other):
    count = mine.shape[0] // 4
    other = hop(other, 1)
    half = []
    for j in range(4):
        rows = slice(j * count, (j + 1) * count)
        half.append((mine[rows].astype(f32) + other[rows].astype(f32)).astype(bf16))
    return half[:1] + [hop(half[j], 2 * j) for j in (1, 2, 3)]


def plane_total(value):
    value = value + hop(value, 1)
    return value + hop(value, 2) + hop(value, 4) + hop(value, 6)


def local_group(index, core, width):
    plane, at = jnp.zeros_like(index), jnp.zeros_like(index)
    for k in range(2):
        for slices_plane, first, start, count in local_slices(k, width):
            inside = (core == k) & (index >= first) & (index < first + count)
            plane = jnp.where(inside, slices_plane, plane)
            at = jnp.where(inside, index - first + start, at)
    return plane, at


def shared_back_kernel(where_ref, rows_ref, taps_ref, heads_ref, pick_ref, out_ref, *, head_width, piece, first_lane):
    rank, plane = where_ref[0], where_ref[1]
    rows = out_ref.shape[2] - 8
    local = taps_ref.shape[1]
    own = 6 * head_width
    inner = 8 * own
    core, chip = lax.bitwise_and(rank, 1), lax.shift_right_logical(rank, 1)
    at = iota((local, LANES), 0)
    at_plane, offset = local_group(at, core, head_width)
    column = jnp.where(at < own, 3 * head_width * (4 * at_plane + chip) + offset, inner + at - own)
    heads = mm_exact(heads_ref[...], pick_ref[...])
    heads = jnp.concatenate([jnp.zeros((5, LANES), f32), heads[:3]], axis=0)
    high, low = halves(taps_ref[...])
    both = jnp.concatenate([high, low], axis=0)
    target = LANES * (column // piece) + column % piece - iota((local, LANES), 1)
    head_halves = halves(heads)
    for o in range(4):
        first = 8 * lax.bitwise_and(plane - o + 4, 3)
        for r in range(8):
            chosen = (target == LANES * (first + r)).astype(bf16)
            spread = mm(both, chosen)
            place_at = place(r, rank)
            own_rows = slice((8 * o + r) * rows, (8 * o + r + 1) * rows)
            out_ref[place_at, o, :rows, : 2 * LANES] = rows_ref[own_rows, first_lane : first_lane + 2 * LANES]
            steps = mm(rows_ref[own_rows, first_lane + 2 * LANES :], pick_ref[...].astype(bf16))
            out_ref[place_at, o, :rows, 2 * LANES :] = steps.astype(bf16)
            for half in (0, 1):
                value = spread[8 * half : 8 * half + 8].astype(bf16) + head_halves[half]
                out_ref[place_at, o, rows:, half * LANES : (half + 1) * LANES] = value
            out_ref[place_at, o, rows:, 2 * LANES :] = jnp.zeros((8, out_ref.shape[3] - 2 * LANES), bf16)


def split_local(
    hidden,
    norm_gain,
    w_gate_in,
    w_conv_in,
    w_step,
    conv_weight,
    conv_bias,
    step_bias,
    decay_log,
    skip_gain,
    gate_gain,
    w_out,
    cotangent,
):
    plane, rank = lax.axis_index("batch"), lax.axis_index("seq")
    planes, ranks = lax.axis_size("batch"), lax.axis_size("seq")
    _, span, width = hidden.shape
    rows_in, inner = w_gate_in.shape
    channels = w_conv_in.shape[1]
    heads = w_step.shape[1]
    head_width = inner // heads
    states = (channels - inner) // 2
    taps = conv_weight.shape[0]
    own = inner // ranks
    rows_out = w_out.shape[0]
    tokens = ranks * span
    block = width // planes
    piece = conv_bias.shape[0]
    devices = planes * ranks
    padded = -(-(2 * states + heads) // LANES) * LANES
    local = own + 2 * states
    third = rows_out // 3
    fixed = None
    where = jnp.stack([rank, plane]).astype(jnp.int32)

    out_parts = planes_gather(w_out)
    cols, message = once(
        functools.partial(pack_kernel, head_width=head_width),
        [w_gate_in, w_conv_in, w_step, norm_gain[None], gate_gain[None], conv_bias[None], conv_weight],
        [((ranks, rows_in, 2 * own), bf16), ((rows_in + 8, padded), bf16)],
    )
    cols = lax.all_to_all(cols, "seq", 0, 0).reshape(ranks * rows_in, 2 * own)
    message = jnp.concatenate(planes_gather(message, True), axis=1)
    tokens_rel, cot_rel = plane_gather(hidden[0]), plane_gather(cotangent[0])
    shared_mine, shared_other = small_gather(message)
    conv_w, gate_w = planes_gather(cols[:, :own]), planes_gather(cols[:, own:], True)
    head_values = jnp.pad(jnp.stack([step_bias, decay_log, skip_gain]), ((0, 5), (0, LANES - heads)))
    shared_w, norm_full, taps_rows, channel_rows, head_rows, head_table = rows_call(
        functools.partial(setup_kernel, n_taps=taps, head_width=head_width),
        where,
        1,
        None,
        [(a, fixed) for a in (shared_mine, shared_other, head_values)],
        [
            ((width, padded), bf16, fixed),
            ((1, width), f32, fixed),
            ((8, local), f32, fixed),
            ((8, own), f32, fixed),
            ((8, LANES), f32, fixed),
            ((LANES, LANES), f32, fixed),
        ],
        [
            pltpu.VMEM((1, inner), f32),
            pltpu.VMEM((8, channels), f32),
            pltpu.VMEM((devices, 8, LANES), f32),
        ],
    )
    (lent_rows,) = once(lend_kernel, out_parts, [((2, third, width), bf16)], where)
    borrowed = hop(lent_rows, 1)
    (out_w,) = once(out_rows_kernel, [*out_parts, borrowed], [((own, width), bf16)], where)

    sizes = dict(n_taps=taps, head_width=head_width, states=states)
    rows = tokens // 4
    norm_full, out_w = lax.optimization_barrier((norm_full, out_w))
    normed, pre, raw, rest_w = rows_call(
        functools.partial(project_kernel, states=states),
        where,
        4,
        rows,
        [(a, fixed) for a in (*tokens_rel, norm_full, *conv_w, shared_w)],
        [
            ((tokens, width), bf16, each),
            ((tokens, local), bf16, each),
            ((tokens, LANES), f32, each),
            ((width, own + padded), bf16, fixed),
        ],
    )
    pre, raw = pre.reshape(ranks, span, local), raw.reshape(ranks, span, LANES)
    mixed, conv, inter, ssm, entering = spans_call(
        functools.partial(forward_kernel, **sizes),
        where,
        ranks,
        [(pre, relative), (raw, relative)]
        + [(a, fixed) for a in (taps_rows, head_rows, channel_rows)],
        [
            ((span, local), f32, in_time),
            ((span, local), bf16, in_time),
            ((span, own), f32, in_time),
            ((span, own), f32, relative),
            ((states, own), f32, in_time),
        ],
        [pltpu.VMEM((span + 8, local), f32), pltpu.VMEM((states, own), f32)],
    )
    ssm = ssm.reshape(tokens, own)
    gate, ngate, sums, part_mine, part_other, gate_all = rows_call(
        gate_kernel,
        where,
        4,
        rows,
        [(normed, each)]
        + [(a, fixed) for a in (*gate_w, *cot_rel, out_w, channel_rows)]
        + [(ssm, each)],
        [
            ((tokens, own), f32, each),
            ((tokens, own), f32, each),
            ((ranks, 8, LANES), f32, fixed),
            ((tokens // 2, width), bf16, lower),
            ((tokens // 2, width), bf16, upper),
            ((width, own), bf16, fixed),
        ],
        [pltpu.VMEM((rows, width), bf16)],
    )
    sums = plane_total(sums)
    out_own = plane_parts(part_mine, part_other)

    grad_y, grad_gate, projected, lent = rows_call(
        functools.partial(gate_back_kernel, inner=inner, third=third),
        where,
        4,
        rows,
        [(sums, fixed), (ssm, each), (gate, each), (ngate, each), (channel_rows, fixed)],
        [
            ((tokens, own), f32, each),
            ((tokens, own), bf16, each),
            ((tokens, own), bf16, each),
            ((tokens, LANES), bf16, each),
        ],
    )
    borrowed = hop(lent, 1)
    early = rows_call(
        functools.partial(early_grads_kernel, third=third),
        where,
        4,
        None,
        [(normed, Columns((tokens, block)))]
        + [(a, fixed) for a in (grad_gate, projected, borrowed, *cot_rel)],
        [((block + 4 * rows_out, block), bf16, fixed)] * 4,
        [
            pltpu.VMEM((tokens, width), bf16),
            pltpu.VMEM((tokens, own), bf16),
            pltpu.VMEM((own, width), bf16),
        ],
    )
    early = planes_parts(early)
    grad_rest, grad_taps, grad_heads = spans_call(
        functools.partial(backward_kernel, **sizes),
        where,
        ranks,
        [(grad_y.reshape(ranks, span, own), relative_reverse)]
        + [(a, in_reverse) for a in (inter, entering, conv)]
        + [(pre, relative_reverse), (mixed, in_reverse), (raw, relative_reverse)]
        + [(a, fixed) for a in (taps_rows, head_rows, channel_rows)],
        [
            ((span, own + padded), bf16, relative_reverse),
            ((8, local), f32, fixed),
            ((8, LANES), f32, fixed),
        ],
        [
            pltpu.VMEM((span + 8, local), f32),
            pltpu.VMEM((states, own), f32),
            pltpu.VMEM((states, own), f32),
        ],
    )
    grad_rest = grad_rest.reshape(tokens, own + padded)
    d_rest = jnp.dot(normed.T, grad_rest, preferred_element_type=f32).astype(bf16)
    d_conv = planes_direct([d_rest[o * block : (o + 1) * block, :own] for o in range(planes)])
    (d_shared,) = once(
        functools.partial(shared_back_kernel, head_width=head_width, piece=piece, first_lane=own),
        [d_rest, grad_taps, grad_heads, head_table],
        [((ranks, planes, rows_in + 8, padded), bf16)],
        where,
    )
    gate_all, d_shared = lax.optimization_barrier((gate_all, d_shared))
    mine, other = input_grad_call(grad_gate, grad_rest, gate_all, rest_w)
    grad_own = plane_parts(mine, other)
    d_shared = d_shared.reshape(2, ranks // 2 * planes, rows_in + 8, padded)
    d_shared = plane_parts(d_shared[0], d_shared[1])
    d_shared = sum(part.astype(f32) for part in d_shared)
    d_shared = planes_direct([d_shared[o] for o in range(planes)])

    d_gate, d_out, d_gain = once(
        early_rows_kernel,
        [*early, w_out, gate_gain[None]],
        [((block, own), bf16), ((rows_out, width), f32), ((1, rows_out), f32)],
    )
    (d_in,) = once(late_rows_kernel, [d_gate, *d_conv], [((ranks, rows_in, 2 * own), bf16)])
    d_in = lax.all_to_all(d_in, "seq", 0, 0)
    output, grad_hidden = once(
        functools.partial(tokens_out_kernel, inner=inner),
        [*out_own, *grad_own, hidden[0], cotangent[0], sums, norm_full],
        [((span, width), bf16), ((span, width), f32)],
        where,
        [pltpu.VMEM((span, width), f32)],
    )
    d_gate, d_conv, d_norm, d_step, *small = once(
        functools.partial(columns_kernel, head_width=head_width),
        [d_in, w_gate_in, w_conv_in, w_step, norm_gain[None], *d_shared],
        [
            ((rows_in, inner), f32),
            ((rows_in, channels), f32),
            ((1, rows_in), f32),
            ((rows_in, heads), f32),
            ((taps, piece), f32),
            ((1, piece), f32),
            ((1, heads), f32),
            ((1, heads), f32),
            ((1, heads), f32),
        ],
    )
    return (
        output[None],
        grad_hidden[None],
        d_norm[0],
        d_gate,
        d_conv,
        d_step,
        small[0],
        small[1][0],
        small[2][0],
        small[3][0],
        small[4][0],
        d_gain[0],
        d_out,
    )


def split_block(*args):
    return split_local(*args)


def solution(mesh):
    split = (mesh.shape["batch"], mesh.shape["seq"]) == (4, 8)
    body = split_block if split else local
    return jax.shard_map(
        body,
        mesh=mesh,
        in_specs=(
            P("batch", "seq", None),
            P(("batch", "seq")),
            P(("batch", "seq"), None),
            P(("batch", "seq"), None),
            P(("batch", "seq"), None),
            P(None, ("batch", "seq")),
            P(("batch", "seq")),
            P(),
            P(),
            P(),
            P(("batch", "seq")),
            P(("batch", "seq"), None),
            P("batch", "seq", None),
        ),
        out_specs=(
            P("batch", "seq", None),
            P("batch", "seq", None),
            P(("batch", "seq")),
            P(("batch", "seq"), None),
            P(("batch", "seq"), None),
            P(("batch", "seq"), None),
            P(None, ("batch", "seq")),
            P(("batch", "seq")),
            P(),
            P(),
            P(),
            P(("batch", "seq")),
            P(("batch", "seq"), None),
        ),
        check_vma=False,
    )
```

```python
import functools
import typing

import jax
import jax.numpy as jnp
from jax import lax
from jax.experimental import pallas as pl
from jax.experimental.pallas import tpu as pltpu
from jax.sharding import PartitionSpec as P

norm_epsilon = 1e-05


def shifted(value, axis, steps):
    count = lax.axis_size(axis)
    first, last = (max(0, -steps), min(count, count - steps))
    return lax.ppermute(value, axis, [(source, source + steps) for source in range(first, last)])


def prefix(array, axis, combine, identity, reverse):
    devices, place = (lax.axis_size(axis), lax.axis_index(axis))
    everything = jax.tree.map(lambda part: lax.all_gather(part, axis), array)
    start = jax.tree.map(
        lambda part, zero: jnp.broadcast_to(jnp.asarray(zero, part.dtype), part.shape),
        array,
        identity,
    )

    def hop(k, before):
        at = devices - 1 - k if reverse else k
        reached = at > place if reverse else at < place
        new = combine(before, jax.tree.map(lambda part: part[at], everything))
        return jax.tree.map(lambda a, b: jnp.where(reached, a, b), new, before)

    return lax.fori_loop(0, devices, hop, start)


def for_sending(array):
    return jax.tree.map(lambda a: a.astype(jnp.bfloat16) if a.dtype == jnp.float32 else a, array)


def narrow_product(pattern, former, latter):
    return jnp.einsum(pattern, former, latter, preferred_element_type=jnp.float32)


def wide_product(pattern, former, latter):
    return jnp.einsum(pattern, former, latter, precision=lax.Precision.HIGHEST)


def silu_slope(inputs):
    logistic = jax.nn.sigmoid(inputs)
    return logistic * (1.0 + inputs * (1.0 - logistic))


def upper_table(length):
    rows = lax.broadcasted_iota(jnp.int32, (length, length), 0)
    cols = lax.broadcasted_iota(jnp.int32, (length, length), 1)
    return (rows <= cols).astype(jnp.float32)


def running_total(step_size, head_rate):
    table = upper_table(step_size.shape[0])
    return jnp.dot((step_size * head_rate[None, :]).T, table, precision=lax.Precision.HIGHEST)


def span_parts(value_b, key_b, query_b, step_size, head_rate):
    length = step_size.shape[0]
    cumulative = running_total(step_size, head_rate)
    row_index = lax.broadcasted_iota(jnp.int32, (1, length, length), 1)
    col_index = lax.broadcasted_iota(jnp.int32, (1, length, length), 2)
    causal = row_index >= col_index
    spread = cumulative[:, :, None] - cumulative[:, None, :]
    decays = jnp.where(causal, jnp.exp(jnp.where(causal, spread, 0.0)), 0.0)
    affinity = jnp.dot(query_b, key_b.T, preferred_element_type=jnp.float32)
    step_rows = step_size.T
    scores = affinity[None] * decays * step_rows[:, None, :]
    mixing = scores.astype(jnp.bfloat16)
    within = narrow_product("hts,shp->thp", mixing, value_b)
    tail_decay = jnp.exp(cumulative[:, -1:] - cumulative) * step_rows
    weighted = (tail_decay.T[:, :, None] * value_b.astype(jnp.float32)).astype(jnp.bfloat16)
    span_state = narrow_product("shp,sn->hpn", weighted, key_b)
    total_decay = jnp.exp(cumulative[:, -1])
    return (within, span_state, total_decay, cumulative, decays, affinity, scores, mixing, weighted)


def span_inter(query_b, cumulative, carried):
    base = wide_product("tn,hpn->thp", query_b.astype(jnp.float32), carried)
    return jnp.exp(cumulative).T[:, :, None] * base


def carried_grad(query_b, cumulative, grad_y):
    scaled = grad_y * jnp.exp(cumulative).T[:, :, None]
    return wide_product("thp,tn->hpn", scaled, query_b.astype(jnp.float32))


def span_backward(
    value_b, key_b, query_b, step_size, carried, grad_y, grad_state, grad_total, head_rate
):
    parts = span_parts(value_b, key_b, query_b, step_size, head_rate)
    total_decay, cumulative, decays, affinity, scores, mixing, weighted = parts[2:]
    length = step_size.shape[0]
    query_f = query_b.astype(jnp.float32)
    key_f = key_b.astype(jnp.float32)
    value_f = value_b.astype(jnp.float32)
    step_rows = step_size.T
    growth = jnp.exp(cumulative)
    base = wide_product("tn,hpn->thp", query_f, carried)
    grad_cumul = growth * jnp.sum(grad_y * base, axis=2).T
    grad_query = wide_product("thp,hpn->tn", grad_y * growth.T[:, :, None], carried)
    grad_low = grad_y.astype(jnp.bfloat16)
    grad_mixing = narrow_product("thp,shp->hts", grad_low, value_b)
    grad_value = narrow_product("hts,thp->shp", mixing, grad_low)
    grad_affinity = jnp.sum(grad_mixing * decays * step_rows[:, None, :], axis=0)
    grad_steps = jnp.sum(grad_mixing * affinity[None] * decays, axis=1)
    through = grad_mixing * scores
    grad_cumul = grad_cumul + jnp.sum(through, axis=2) - jnp.sum(through, axis=1)
    grad_query = grad_query + wide_product("ts,sn->tn", grad_affinity, key_f)
    grad_key = wide_product("ts,tn->sn", grad_affinity, query_f)
    grad_weighted = wide_product("hpn,sn->shp", grad_state, key_f)
    grad_key = grad_key + wide_product("shp,hpn->sn", weighted.astype(jnp.float32), grad_state)
    grad_end = jnp.sum(grad_weighted * value_f, axis=2).T
    tail_only = jnp.exp(cumulative[:, -1:] - cumulative)
    grad_value = grad_value + grad_weighted * (tail_only * step_rows).T[:, :, None]
    grad_steps = grad_steps + grad_end * tail_only
    push = grad_end * tail_only * step_rows
    last_flag = lax.broadcasted_iota(jnp.int32, (1, length), 1) == length - 1
    last_term = (jnp.sum(push, axis=1) + grad_total * total_decay)[:, None]
    grad_cumul = grad_cumul - push + jnp.where(last_flag, last_term, 0.0)
    grad_log = jnp.dot(grad_cumul, upper_table(length).T, precision=lax.Precision.HIGHEST)
    grad_steps = grad_steps + grad_log * head_rate[:, None]
    grad_rate = jnp.sum(grad_log * step_rows, axis=1)
    return (grad_value, grad_key, grad_query, grad_steps.T, grad_rate)


def conv_apply(padded, kernel_f, bias_f, length):
    time_axis = padded.ndim - 2
    total = bias_f
    for offset in range(kernel_f.shape[0]):
        total = total + kernel_f[offset] * lax.slice_in_dim(
            padded, offset, offset + length, axis=time_axis
        )
    return total


def conv_back(grad_mixed, padded, kernel_f):
    length = grad_mixed.shape[-2]
    kernel_taps = kernel_f.shape[0]
    time_axis = grad_mixed.ndim - 2
    leading = tuple(range(grad_mixed.ndim - 1))
    grad_kernel = jnp.stack(
        [
            jnp.sum(
                grad_mixed * lax.slice_in_dim(padded, offset, offset + length, axis=time_axis),
                axis=leading,
            )
            for offset in range(kernel_taps)
        ]
    )
    grad_padded = jnp.zeros(padded.shape, jnp.float32)
    for offset in range(kernel_taps):
        widths = [(0, 0)] * grad_mixed.ndim
        widths[time_axis] = (offset, kernel_taps - 1 - offset)
        grad_padded = grad_padded + jnp.pad(grad_mixed * kernel_f[offset], widths)
    return (grad_kernel, grad_padded)


def combine_states(earlier, later):
    return (earlier[0] * later[0], later[0][:, :, None, None] * earlier[1] + later[1])


def local(
    hidden,
    norm_gain,
    w_gate_in,
    w_conv_in,
    w_step,
    conv_weight,
    conv_bias,
    step_bias,
    decay_log,
    skip_gain,
    gate_gain,
    w_out,
    cotangent,
):
    seq_count, length, model_width = hidden.shape
    gathered = (
        lax.all_gather(norm_gain, ("batch", "seq"), axis=0, tiled=True),
        lax.all_gather(w_gate_in, ("batch", "seq"), axis=0, tiled=True),
        lax.all_gather(w_conv_in, ("batch", "seq"), axis=0, tiled=True),
        lax.all_gather(w_step, ("batch", "seq"), axis=0, tiled=True),
        lax.all_gather(conv_weight, ("batch", "seq"), axis=1, tiled=True),
        lax.all_gather(conv_bias, ("batch", "seq"), axis=0, tiled=True),
        lax.all_gather(gate_gain, ("batch", "seq"), axis=0, tiled=True),
        lax.all_gather(w_out, ("batch", "seq"), axis=0, tiled=True),
    )
    (
        norm_full,
        gate_in_full,
        conv_in_full,
        step_full,
        kernel_full,
        bias_full,
        gain_full,
        out_full,
    ) = gathered
    inner_width = gate_in_full.shape[1]
    head_count = step_full.shape[1]
    head_width = inner_width // head_count
    channels = conv_in_full.shape[1]
    state_width = (channels - inner_width) // 2
    kernel_taps = kernel_full.shape[0]
    row_count = seq_count * length
    head_rate = -jnp.exp(decay_log)
    tokens_f = hidden.reshape(row_count, model_width).astype(jnp.float32)
    inv_rms = lax.rsqrt(jnp.mean(tokens_f * tokens_f, axis=1, keepdims=True) + norm_epsilon)
    unit = tokens_f * inv_rms
    normed = (unit * norm_full.astype(jnp.float32)[None]).astype(jnp.bfloat16)
    gate_pre = jnp.dot(normed, gate_in_full, preferred_element_type=jnp.float32)
    conv_pre = (
        jnp.dot(normed, conv_in_full, preferred_element_type=jnp.float32)
        .astype(jnp.bfloat16)
        .reshape(seq_count, length, channels)
    )
    raw_step = jnp.dot(normed, step_full, preferred_element_type=jnp.float32)
    rim = shifted(conv_pre[:, length - (kernel_taps - 1) :, :], "seq", 1)
    extended = jnp.concatenate([rim, conv_pre], axis=1).astype(jnp.float32)
    mixed_in = conv_apply(
        extended, kernel_full.astype(jnp.float32), bias_full.astype(jnp.float32), length
    )
    conv_out = jax.nn.silu(mixed_in).astype(jnp.bfloat16)
    value_b = conv_out[:, :, :inner_width].reshape(seq_count, length, head_count, head_width)
    key_b = conv_out[:, :, inner_width : inner_width + state_width]
    query_b = conv_out[:, :, inner_width + state_width :]
    step_size = jax.nn.softplus(raw_step + step_bias[None]).reshape(seq_count, length, head_count)

    def local_forward(value_piece, key_piece, query_piece, step_piece):
        parts = span_parts(value_piece, key_piece, query_piece, step_piece, head_rate)
        return (parts[0], parts[1], parts[2], parts[3])

    within, span_state, total_decay, cumulative = jax.vmap(local_forward)(
        value_b, key_b, query_b, step_size
    )
    identity = (jnp.ones_like(total_decay), jnp.zeros_like(span_state))
    _, carried = prefix((total_decay, span_state), "seq", combine_states, identity, False)
    inter = jax.vmap(span_inter)(query_b, cumulative, carried)
    value_f = value_b.astype(jnp.float32)
    ssm_out = within + inter + skip_gain[None, None, :, None] * value_f
    flat_out = ssm_out.reshape(row_count, inner_width)
    gate_silu = jax.nn.silu(gate_pre)
    gated = flat_out * gate_silu
    inv_gate = lax.rsqrt(jnp.mean(gated * gated, axis=1, keepdims=True) + norm_epsilon)
    normed_gate = gated * inv_gate
    projected_in = (normed_gate * gain_full.astype(jnp.float32)[None]).astype(jnp.bfloat16)
    output = (
        tokens_f + jnp.dot(projected_in, out_full, preferred_element_type=jnp.float32)
    ).astype(jnp.bfloat16)
    backward_weights = (
        lax.all_gather(norm_gain, ("batch", "seq"), axis=0, tiled=True),
        lax.all_gather(w_gate_in, ("batch", "seq"), axis=0, tiled=True),
        lax.all_gather(w_conv_in, ("batch", "seq"), axis=0, tiled=True),
        lax.all_gather(w_step, ("batch", "seq"), axis=0, tiled=True),
        lax.all_gather(conv_weight, ("batch", "seq"), axis=1, tiled=True),
        lax.all_gather(gate_gain, ("batch", "seq"), axis=0, tiled=True),
        lax.all_gather(w_out, ("batch", "seq"), axis=0, tiled=True),
    )
    norm_back, gate_in_back, conv_in_back, step_back, kernel_back, gain_back, out_back = (
        backward_weights
    )
    incoming = cotangent.reshape(row_count, model_width)
    grad_proj = jnp.dot(incoming, out_back.T, preferred_element_type=jnp.float32)
    grad_w_out = jnp.dot(projected_in.T, incoming, preferred_element_type=jnp.float32)
    grad_gate_gain = jnp.sum(grad_proj * normed_gate, axis=0)
    grad_ngate = grad_proj * gain_back.astype(jnp.float32)[None]
    grad_gated = inv_gate * (
        grad_ngate - normed_gate * jnp.mean(grad_ngate * normed_gate, axis=1, keepdims=True)
    )
    grad_flat = grad_gated * gate_silu
    grad_gate_pre = (grad_gated * flat_out * silu_slope(gate_pre)).astype(jnp.bfloat16)
    grad_ssm = grad_flat.reshape(seq_count, length, head_count, head_width)
    grad_skip = jnp.sum(grad_ssm * value_f, axis=(0, 1, 3))
    grad_carried = jax.vmap(carried_grad)(query_b, cumulative, grad_ssm)
    _, grad_state = prefix((total_decay, grad_carried), "seq", combine_states, identity, True)
    grad_total = jnp.sum(grad_state * carried, axis=(2, 3))

    def local_backward(
        value_piece,
        key_piece,
        query_piece,
        step_piece,
        carried_piece,
        grad_piece,
        state_piece,
        total_piece,
    ):
        return span_backward(
            value_piece,
            key_piece,
            query_piece,
            step_piece,
            carried_piece,
            grad_piece,
            state_piece,
            total_piece,
            head_rate,
        )

    grad_value, grad_key, grad_query, grad_steps, grad_rate = jax.vmap(local_backward)(
        value_b, key_b, query_b, step_size, carried, grad_ssm, grad_state, grad_total
    )
    grad_value = grad_value + grad_ssm * skip_gain[None, None, :, None]
    grad_conv_out = jnp.concatenate(
        [grad_value.reshape(seq_count, length, inner_width), grad_key, grad_query], axis=2
    )
    grad_mixed = grad_conv_out * silu_slope(mixed_in)
    grad_bias = jnp.sum(grad_mixed, axis=(0, 1))
    grad_kernel, grad_padded = conv_back(grad_mixed, extended, kernel_back.astype(jnp.float32))
    back_rim = shifted(for_sending(grad_padded[:, : kernel_taps - 1, :]), "seq", -1)
    grad_core = grad_padded[:, kernel_taps - 1 :, :]
    split_at = length - (kernel_taps - 1)
    grad_core = jnp.concatenate(
        [grad_core[:, :split_at], grad_core[:, split_at:] + back_rim], axis=1
    )
    grad_pre = grad_core.astype(jnp.bfloat16).reshape(row_count, channels)
    grad_raw = grad_steps.reshape(row_count, head_count) * jax.nn.sigmoid(
        raw_step + step_bias[None]
    )
    grad_step_bias = jnp.sum(grad_raw, axis=0)
    grad_raw_low = grad_raw.astype(jnp.bfloat16)
    grad_decay_log = jnp.sum(grad_rate, axis=0) * head_rate
    grad_w_gate_in = jnp.dot(normed.T, grad_gate_pre, preferred_element_type=jnp.float32)
    grad_w_conv_in = jnp.dot(normed.T, grad_pre, preferred_element_type=jnp.float32)
    grad_w_step = jnp.dot(normed.T, grad_raw_low, preferred_element_type=jnp.float32)
    grad_normed = jnp.dot(grad_gate_pre, gate_in_back.T, preferred_element_type=jnp.float32)
    grad_normed = grad_normed + jnp.dot(
        grad_pre, conv_in_back.T, preferred_element_type=jnp.float32
    )
    grad_normed = grad_normed + jnp.dot(
        grad_raw_low, step_back.T, preferred_element_type=jnp.float32
    )
    grad_norm_gain = jnp.sum(grad_normed * unit, axis=0)
    grad_unit = grad_normed * norm_back.astype(jnp.float32)[None]
    grad_tokens = inv_rms * (grad_unit - unit * jnp.mean(grad_unit * unit, axis=1, keepdims=True))
    grad_hidden = (incoming.astype(jnp.float32) + grad_tokens).reshape(
        seq_count, length, model_width
    )
    partial_grads = (
        grad_norm_gain,
        grad_w_gate_in,
        grad_w_conv_in,
        grad_w_step,
        grad_kernel,
        grad_bias,
        grad_gate_gain,
        grad_w_out,
    )
    shares = (
        lax.psum_scatter(partial_grads[0], ("batch", "seq"), scatter_dimension=0, tiled=True),
        lax.psum_scatter(partial_grads[1], ("batch", "seq"), scatter_dimension=0, tiled=True),
        lax.psum_scatter(partial_grads[2], ("batch", "seq"), scatter_dimension=0, tiled=True),
        lax.psum_scatter(partial_grads[3], ("batch", "seq"), scatter_dimension=0, tiled=True),
        lax.psum_scatter(partial_grads[4], ("batch", "seq"), scatter_dimension=1, tiled=True),
        lax.psum_scatter(partial_grads[5], ("batch", "seq"), scatter_dimension=0, tiled=True),
        lax.psum_scatter(partial_grads[6], ("batch", "seq"), scatter_dimension=0, tiled=True),
        lax.psum_scatter(partial_grads[7], ("batch", "seq"), scatter_dimension=0, tiled=True),
    )
    head_sums = lax.psum((grad_step_bias, grad_decay_log, grad_skip), ("batch", "seq"))
    return (
        output.reshape(seq_count, length, model_width),
        grad_hidden,
        shares[0],
        shares[1],
        shares[2],
        shares[3],
        shares[4],
        shares[5],
        head_sums[0],
        head_sums[1],
        head_sums[2],
        shares[6],
        shares[7],
    )


bf16 = jnp.bfloat16
f32 = jnp.float32
EXACT = lax.Precision.HIGHEST
LANES = 128


def granted(mebibytes):
    return pltpu.CompilerParams(vmem_limit_bytes=mebibytes << 20)


grant, wide_grant, whole_grant = granted(10), granted(18), granted(60)


def mm(former, latter, dims=((1,), (0,))):
    return lax.dot_general(former, latter, (dims, ((), ())), preferred_element_type=f32)


def mm_exact(former, latter, dims=((1,), (0,))):
    return lax.dot_general(
        former, latter, (dims, ((), ())), precision=EXACT, preferred_element_type=f32
    )


def halves(array):
    high = array.astype(bf16)
    return high, (array - high.astype(f32)).astype(bf16)


def iota(shape, axis):
    return lax.broadcasted_iota(jnp.int32, shape, axis)


def head_map(own, head_width):
    return (iota((LANES, own), 0) == iota((LANES, own), 1) // head_width).astype(f32)


def triangle_sum(table, array):
    high, low = halves(array)
    table = table.astype(bf16)
    return mm(jnp.concatenate([table, table], axis=1), jnp.concatenate([high, low], axis=0))


def twice(array):
    return jnp.concatenate([array, array], axis=1)


def stacked_halves(array):
    return jnp.concatenate(halves(array), axis=0)


def step_tables(raw, rate):
    span = raw.shape[0]
    step = jnp.maximum(raw, 0.0) + jnp.log1p(jnp.exp(-jnp.abs(raw)))
    return step, triangle_sum(iota((span, span), 0) >= iota((span, span), 1), step * rate)


def pair_masked(array, head_width):
    low = iota(array.shape, 1) < head_width
    zero = jnp.zeros_like(array)
    return jnp.concatenate([jnp.where(low, array, zero), jnp.where(low, zero, array)], axis=0)


def by_pair_lanes(array, pair, head_width):
    shape = (array.shape[0], 2 * head_width)
    first = jnp.broadcast_to(array[:, 2 * pair : 2 * pair + 1], shape)
    second = jnp.broadcast_to(array[:, 2 * pair + 1 : 2 * pair + 2], shape)
    return jnp.where(iota(shape, 1) < head_width, first, second)


def place(i, rank):
    m = lax.bitwise_xor(i, rank)
    return 4 * lax.bitwise_and(m, 1) + lax.shift_right_logical(m, 1)


def span_at(place_index, rank):
    m = 2 * lax.bitwise_and(place_index, 3) + lax.shift_right_logical(place_index, 2)
    return lax.bitwise_xor(m, rank)


def project_kernel(
    where_ref, t0, t1, t2, t3, t4, t5, t6, t7, gain_ref, w0, w1, w2, w3, shared_ref,
    normed_ref, pre_ref, raw_ref, weight_ref, *, states,
):
    step = pl.program_id(0)
    plane = where_ref[1]
    span, width = t0.shape
    own = w0.shape[1]
    block = width // 4

    @pl.when(step == 0)
    def _():
        for o, w in enumerate((w0, w1, w2, w3)):
            weight_ref[o * block : (o + 1) * block, :own] = w[...]
        weight_ref[:, own:] = shared_ref[...]

    parts = (t0, t1, t2, t3, t4, t5, t6, t7)
    for half in range(4):

        @pl.when(step == half)
        def _(half=half):
            for i in range(2):
                part = parts[2 * half + i]
                tokens = part[...].astype(f32)
                inv_rms = lax.rsqrt(jnp.mean(tokens * tokens, axis=1, keepdims=True) + norm_epsilon)
                for o in range(4):
                    at = pl.multiple_of(lax.bitwise_and(plane - o + 4, 3) * block, LANES)
                    value = part[:, pl.ds(at, block)].astype(f32) * inv_rms
                    value = (value * gain_ref[:, pl.ds(at, block)]).astype(bf16)
                    normed_ref[i * span : (i + 1) * span, o * block : (o + 1) * block] = value

    product = mm(normed_ref[...], weight_ref[...])
    local = own + 2 * states
    pre_ref[...] = product[:, :local].astype(bf16)
    raw_ref[...] = product[:, local:]


def forward_kernel(
    where_ref, pre_ref, raw_ref, taps_ref, heads_ref, rows_ref,
    mixed_ref, conv_ref, inter_ref, ssm_ref, state_ref,
    ext, state, *, n_taps, head_width, states,
):
    span, own = ssm_ref.shape[1:]

    @pl.when(pl.program_id(0) == 0)
    def _():
        ext[0:8, :] = jnp.zeros((8, ext.shape[1]), f32)
        state[...] = jnp.zeros_like(state)

    ext[8 : 8 + span, :] = pre_ref[0].astype(f32)
    mixed = taps_ref[n_taps : n_taps + 1, :]
    for k in range(n_taps):
        first = 8 - (n_taps - 1) + k
        mixed = mixed + taps_ref[k : k + 1, :] * ext[first : first + span, :]
    mixed_ref[0] = mixed
    ext[0:8, :] = ext[span : span + 8, :]
    conv = (mixed * jax.nn.sigmoid(mixed)).astype(bf16)
    conv_ref[0] = conv
    key, query = conv[:, own : own + states], conv[:, own + states :]
    step, cum = step_tables(raw_ref[0] + heads_ref[0:1, :], heads_ref[1:2, :])
    cum_t, step_t = cum.T, step.T
    affinity = mm(query, key, ((1,), (1,)))
    causal = iota((span, span), 0) >= iota((span, span), 1)
    entering = state[...]
    state_ref[0] = entering
    base = mm(twice(query), stacked_halves(entering))
    weighted, kept = [], []
    for pair in range(own // (2 * head_width)):
        lanes = slice(2 * pair * head_width, 2 * (pair + 1) * head_width)
        value = conv_ref[0, :, lanes]
        mixing = []
        for h in (2 * pair, 2 * pair + 1):
            decay = jnp.exp(jnp.where(causal, cum[:, h : h + 1] - cum_t[h : h + 1, :], -1e30))
            mixing.append((affinity * decay * step_t[h : h + 1, :]).astype(bf16))
        cum_pair = by_pair_lanes(cum, pair, head_width)
        growth = jnp.exp(cum_pair)
        tailed = jnp.exp(cum_pair[span - 1 : span, :] - cum_pair) * by_pair_lanes(step, pair, head_width)
        inter = growth * base[:, lanes]
        inter_ref[0, :, lanes] = inter
        value_f = value.astype(f32)
        within = mm(jnp.concatenate(mixing, axis=1), pair_masked(value, head_width))
        ssm_ref[0, :, lanes] = within + inter + rows_ref[1:2, lanes] * value_f
        weighted.append((tailed * value_f).astype(bf16))
        kept.append(growth[span - 1 : span, :])
    weighted, kept = jnp.concatenate(weighted, axis=1), jnp.concatenate(kept, axis=1)
    state[...] = kept * entering + mm(key, weighted, ((0,), (0,)))


def gate_kernel(
    where_ref, normed_ref, g0, g1, g2, g3, c0, c1, c2, c3, c4, c5, c6, c7,
    p0, p1, p2, p3, borrowed_ref, rows_ref, ssm_ref,
    gate_ref, ngate_ref, sums_ref, gated_ref, weight_ref, cot_ref, out_ref,
):
    step = pl.program_id(0)
    core, plane = lax.bitwise_and(where_ref[0], 1), where_ref[1]
    block = g0.shape[0]
    span = c0.shape[0]

    @pl.when(step == 0)
    def _():
        for o, w in enumerate((g0, g1, g2, g3)):
            weight_ref[o * block : (o + 1) * block, :] = w[...]
        for o, part in enumerate((p0, p1, p2, p3)):
            place_rows(out_ref, part, borrowed_ref, o, core, lax.bitwise_and(plane - o + 4, 3))

    parts = (c0, c1, c2, c3, c4, c5, c6, c7)
    for half in range(4):

        @pl.when(step == half)
        def _(half=half):
            for i in range(2):
                cot_ref[i * span : (i + 1) * span, :] = parts[2 * half + i][...]

    gate = mm(normed_ref[...], weight_ref[...])
    gate_ref[...] = gate
    gated = ssm_ref[...] * (gate * jax.nn.sigmoid(gate))
    gain = rows_ref[0:1, :]
    ngate = mm(cot_ref[...], out_ref[...], ((1,), (1,))) * gain
    ngate_ref[...] = ngate
    squares, cross = gated * gated, ngate * gated
    for i in range(2):
        rows = slice(i * span, (i + 1) * span)
        sums = []
        for product in (squares[rows], cross[rows]):
            folded = product[:, :LANES] + product[:, LANES : 2 * LANES] + product[:, 2 * LANES :]
            sums.append(jnp.sum(folded.T, axis=0, keepdims=True))
        row = iota((8, LANES), 0)
        sums_ref[span_at(2 * step + i, where_ref[0])] = jnp.where(row == 0, sums[0], sums[1])
    gated_ref[...] = (gated * gain).astype(bf16)


def out_part_kernel(where_ref, gated_ref, out_ref, mine_ref, other_ref):
    step = pl.program_id(0)
    part = mm(gated_ref[...], out_ref[...]).astype(bf16)

    @pl.when(step < 2)
    def _():
        mine_ref[...] = part

    @pl.when(step >= 2)
    def _():
        other_ref[...] = part


def gate_back_kernel(
    where_ref, sums_ref, ssm_ref, gate_ref, ngate_ref, rows_ref,
    grad_ref, grad_gate_ref, projected_ref, lent_ref, *, inner, third,
):
    step = pl.program_id(0)
    rows, own = ssm_ref.shape
    core = lax.bitwise_and(where_ref[0], 1)
    lent_ref[...] = jnp.zeros_like(lent_ref)
    span = LANES
    for i in range(rows // span):
        at = slice(i * span, (i + 1) * span)
        sums = sums_ref[span_at(rows // span * step + i, where_ref[0])]
        sums = jnp.concatenate([sums, jnp.zeros((LANES - 8, LANES), f32)], axis=0).T
        inv_gate = lax.rsqrt(sums[:, 0:1] / inner + norm_epsilon)
        mean = inv_gate * sums[:, 1:2] / inner
        inv_gate = jnp.broadcast_to(inv_gate, (span, own))
        ssm, gate = ssm_ref[at], gate_ref[at]
        logistic = jax.nn.sigmoid(gate)
        silu = gate * logistic
        normed = ssm * silu * inv_gate
        grad_gated = inv_gate * (ngate_ref[at] - normed * mean)
        grad_ref[at] = grad_gated * silu
        slope = logistic * (1.0 + gate * (1.0 - logistic))
        grad_gate_ref[at] = (grad_gated * ssm * slope).astype(bf16)
        projected_ref[at] = (normed * rows_ref[0:1, :]).astype(bf16)
    for k in range(2):

        @pl.when(core == k)
        def _(k=k):
            for plane, first, _, count in local_slices(k, 2 * third):
                if count == 4 * third:
                    source = first + 3 * third if k == 0 else first
                    to = plane // 2 * third
                    lent_ref[:, to : to + third] = projected_ref[:, source : source + third]


def gate_grad_kernel(where_ref, normed_ref, grad_gate_ref, b0, b1, b2, b3):
    total = mm(normed_ref[...], grad_gate_ref[...], ((0,), (0,))).astype(bf16)
    for o, out_ref in enumerate((b0, b1, b2, b3)):

        @pl.when(pl.program_id(0) == o)
        def _(out_ref=out_ref):
            out_ref[...] = total


def out_grad_kernel(
    where_ref, projected_ref, borrowed_ref, cot_ref, b0, b1, b2, b3, rows_ref, total_ref, *, third,
):
    step = pl.program_id(0)
    core, plane = lax.bitwise_and(where_ref[0], 1), where_ref[1]
    rows = 3 * third
    block = b0.shape[1]
    for k in range(2):

        @pl.when(core == k)
        def _(k=k):
            for at_plane, at, _, count in local_slices(k, 2 * third):
                to = at_plane * rows
                lent = slice(at_plane // 2 * third, (at_plane // 2 + 1) * third)
                if count == rows + third:
                    own_at = at if k == 0 else at + third
                    rows_ref[:, to : to + rows] = projected_ref[:, own_at : own_at + rows]
                elif k == 0:
                    rows_ref[:, to : to + count] = projected_ref[:, at : at + count]
                    rows_ref[:, to + count : to + rows] = borrowed_ref[:, lent]
                else:
                    rows_ref[:, to + third : to + rows] = projected_ref[:, at : at + count]
                    rows_ref[:, to : to + third] = borrowed_ref[:, lent]

    total = mm(rows_ref[...], cot_ref[...], ((0,), (0,)))

    @pl.when(step == 0)
    def _():
        total_ref[...] = total

    @pl.when(step == 1)
    def _():
        total_ref[...] += total
        for o, out_ref in enumerate((b0, b1, b2, b3)):
            first = pl.multiple_of(rows * lax.bitwise_and(plane - o + 4, 3), third)
            for g in range(4):
                own = total_ref[pl.ds(first, rows), g * block : (g + 1) * block]
                out_ref[g * rows : (g + 1) * rows, :] = own.astype(bf16)


def backward_kernel(
    where_ref, grad_ref, inter_ref, state_ref, conv_ref, pre_ref, mixed_ref, raw_ref,
    taps_ref, heads_ref, rows_ref,
    grad_pre_ref, grad_taps_ref, grad_heads_ref,
    ext, grad_state, next_state, *, n_taps, head_width, states,
):
    span, own = grad_ref.shape[1:]

    @pl.when(pl.program_id(0) == 0)
    def _():
        ext[span : span + 8, :] = jnp.zeros((8, ext.shape[1]), f32)
        grad_state[...] = jnp.zeros_like(grad_state)
        next_state[...] = jnp.zeros_like(next_state)
        grad_taps_ref[...] = jnp.zeros_like(grad_taps_ref)
        grad_heads_ref[...] = jnp.zeros_like(grad_heads_ref)

    key, query = conv_ref[0, :, own : own + states], conv_ref[0, :, own + states :]
    rate = heads_ref[1:2, :]
    raw = raw_ref[0] + heads_ref[0:1, :]
    step, cum = step_tables(raw, rate)
    cum_t, step_t = cum.T, step.T
    tail = jnp.exp(cum[span - 1 : span, :] - cum)
    affinity = mm(query, key, ((1,), (1,)))
    causal = iota((span, span), 0) >= iota((span, span), 1)
    after = grad_state[...]
    after_halves = stacked_halves(after)
    grad_weighted = mm(twice(key), after_halves)
    grad_affinity = jnp.zeros((span, span), f32)
    direct_t = jnp.zeros((span, span), f32)
    grad_cum = jnp.zeros((span, LANES), f32)
    row, lane = iota((span, span), 0), iota((span, LANES), 1)
    weighted, grown, grown_rest, kept = [], [], [], []
    products = [[], [], []]
    mixed = mixed_ref[0]
    logistic = jax.nn.sigmoid(mixed)
    slope = logistic * (1.0 + mixed * (1.0 - logistic))
    for pair in range(own // (2 * head_width)):
        lanes = slice(2 * pair * head_width, 2 * (pair + 1) * head_width)
        value, grad_y = conv_ref[0, :, lanes], grad_ref[0, :, lanes]
        value_f, grad_low = value.astype(f32), grad_y.astype(bf16)
        cum_pair = by_pair_lanes(cum, pair, head_width)
        growth = jnp.exp(cum_pair)
        tailed = jnp.exp(cum_pair[span - 1 : span, :] - cum_pair) * by_pair_lanes(step, pair, head_width)
        kept.append(growth[span - 1 : span, :])
        high, low = halves(grad_y * growth)
        grown.append(high)
        grown_rest.append(low)
        weighted.append((tailed * value_f).astype(bf16))
        grad_mixing = mm(grad_low, pair_masked(value, head_width), ((1,), (1,)))
        mixing = []
        for i in (0, 1):
            h = 2 * pair + i
            given = grad_mixing[:, i * span : (i + 1) * span]
            decay = jnp.exp(jnp.where(causal, cum[:, h : h + 1] - cum_t[h : h + 1, :], -1e30))
            grad_affinity = grad_affinity + given * decay * step_t[h : h + 1, :]
            table = affinity * decay
            scores = table * step_t[h : h + 1, :]
            mixing.append(scores.astype(bf16))
            direct_t = jnp.where(row == h, jnp.sum(given * table, axis=0, keepdims=True), direct_t)
            grad_cum = jnp.where(lane == h, jnp.sum(given * scores, axis=1, keepdims=True), grad_cum)
        grad_value = mm(jnp.concatenate(mixing, axis=0), pair_masked(grad_low, head_width), ((0,), (0,)))
        by_state = grad_weighted[:, lanes]
        grad_value = grad_value + tailed * by_state + rows_ref[1:2, lanes] * grad_y
        ext[0:span, lanes] = grad_value * slope[:, lanes]
        products[0].append(by_state * value_f)
        products[1].append(grad_y * inter_ref[0, :, lanes])
        products[2].append(jnp.sum(grad_y * value_f, axis=0, keepdims=True))
    weighted, grown = jnp.concatenate(weighted, axis=1), jnp.concatenate(grown, axis=1)
    grown_rest, kept = jnp.concatenate(grown_rest, axis=1), jnp.concatenate(kept, axis=1)
    grad_affinity = grad_affinity.astype(bf16)
    grad_query = mm(grown, state_ref[0].astype(bf16), ((1,), (1,))) + mm(grad_affinity, key)
    grad_key = mm(weighted, after_halves[:states], ((1,), (1,))) + mm(grad_affinity, query, ((0,), (0,)))
    ext[0:span, own : own + states] = grad_key * slope[:, own : own + states]
    ext[0:span, own + states :] = grad_query * slope[:, own + states :]
    to_lanes = head_map(own, head_width).astype(bf16)
    last = jnp.sum(after * next_state[...], axis=0, keepdims=True)
    by_head = jnp.concatenate(
        [
            jnp.concatenate(products[0], axis=1),
            jnp.concatenate(products[1], axis=1),
            jnp.broadcast_to(jnp.concatenate(products[2], axis=1), (8, own)),
            jnp.broadcast_to(last, (8, own)),
        ],
        axis=0,
    )
    high, low = halves(by_head)
    by_head = mm(high, to_lanes, ((1,), (1,))) + mm(low, to_lanes, ((1,), (1,)))
    direct = direct_t.T + by_head[:span] * tail
    grad_cum = grad_cum + by_head[span : 2 * span] - step * direct
    last = by_head[2 * span + 8 : 2 * span + 9]
    grad_cum = grad_cum + jnp.where(iota(grad_cum.shape, 0) == span - 1, last, 0.0)
    grad_log = triangle_sum(iota((span, span), 0) <= iota((span, span), 1), grad_cum)
    grad_raw = (direct + grad_log * rate) * jax.nn.sigmoid(raw)
    grad_heads_ref[0:1, :] += jnp.sum(grad_raw, axis=0, keepdims=True)
    grad_heads_ref[1:2, :] += jnp.sum(grad_log * step, axis=0, keepdims=True) * rate
    grad_heads_ref[2:3, :] += by_head[2 * span : 2 * span + 1]
    pre = pre_ref[0].astype(f32)
    grad_pre = jnp.zeros(pre.shape, f32)
    for k in range(n_taps):
        ahead = ext[n_taps - 1 - k : n_taps - 1 - k + span, :]
        grad_pre = grad_pre + ahead * taps_ref[k : k + 1, :]
        grad_taps_ref[k : k + 1, :] += jnp.sum(ahead * pre, axis=0, keepdims=True)
    grad_taps_ref[n_taps : n_taps + 1, :] += jnp.sum(ext[0:span, :], axis=0, keepdims=True)
    ext[span : span + 8, :] = ext[0:8, :]
    grad_pre_ref[0, :, : own + 2 * states] = grad_pre.astype(bf16)
    grad_pre_ref[0, :, own + 2 * states :] = grad_raw.astype(bf16)
    grad_state[...] = kept * after + mm(
        jnp.concatenate([query, query], axis=0), jnp.concatenate([grown, grown_rest], axis=0), ((0,), (0,))
    )
    next_state[...] = state_ref[0]


def input_grad_kernel(gate_ref, rest_ref, w_gate_ref, w_rest_ref, mine_ref, other_ref):
    half = mine_ref.shape[0]
    total = mm(gate_ref[...], w_gate_ref[...], ((1,), (1,))) + mm(rest_ref[...], w_rest_ref[...], ((1,), (1,)))
    mine_ref[...] = total[:half].astype(bf16)
    other_ref[...] = total[half:].astype(bf16)


def input_grad_call(gate, rest, w_gate, w_rest):
    half, width, block = gate.shape[0] // 2, w_gate.shape[0], w_gate.shape[0] // 3
    return pl.pallas_call(
        input_grad_kernel,
        out_shape=[jax.ShapeDtypeStruct((half, width), bf16)] * 2,
        grid=(3,),
        in_specs=[pl.BlockSpec(a.shape, lambda i: (0, 0)) for a in (gate, rest)]
        + [pl.BlockSpec((block, a.shape[1]), lambda i: (i, 0)) for a in (w_gate, w_rest)],
        out_specs=[pl.BlockSpec((half, block), lambda i: (0, i))] * 2,
        compiler_params=grant,
    )(gate, rest, w_gate, w_rest)


def by_span(shape, order):
    return pl.BlockSpec((1, *shape), lambda i, where: (order(i, where), 0, 0))


def spans_call(kernel, where, spans, inputs, outputs, scratch=()):
    in_specs = [
        by_span(a.shape[1:], order) if order else pl.BlockSpec(a.shape, lambda i, where, n=a.ndim: (0,) * n)
        for a, order in inputs
    ]
    out_specs = [
        by_span(shape, order) if order else pl.BlockSpec(shape, lambda i, where, n=len(shape): (0,) * n)
        for shape, _, order in outputs
    ]
    out_shape = [
        jax.ShapeDtypeStruct(
            (spans, *shape) if order else shape, dtype
        )
        for shape, dtype, order in outputs
    ]
    return pl.pallas_call(
        kernel,
        out_shape=out_shape,
        grid_spec=pltpu.PrefetchScalarGridSpec(
            num_scalar_prefetch=1,
            grid=(spans,),
            in_specs=in_specs,
            out_specs=out_specs,
            scratch_shapes=list(scratch),
        ),
        compiler_params=grant,
    )(where, *[a for a, _ in inputs])


def in_time(i, where):
    return i


def in_reverse(i, where):
    return 7 - i


def relative(i, where):
    return place(i, where[0])


def relative_reverse(i, where):
    return place(7 - i, where[0])


class Part(typing.NamedTuple):
    shape: tuple
    at: tuple


class Columns(typing.NamedTuple):
    shape: tuple
    first: int = 0


def rows_call(kernel, where, steps, rows, inputs, outputs, scratch=(), params=grant):
    def spec(shape, index):
        if isinstance(index, Part):
            return pl.BlockSpec(index.shape, lambda i, where: index.at)
        if isinstance(index, Columns):
            return pl.BlockSpec(index.shape, lambda i, where: (0, index.first + i))
        if index is None:
            return pl.BlockSpec(shape, lambda i, where, n=len(shape): (0,) * n)
        return pl.BlockSpec((rows, *shape[1:]), lambda i, where: (index(i), 0))

    return pl.pallas_call(
        kernel,
        out_shape=[jax.ShapeDtypeStruct(shape, dtype) for shape, dtype, _ in outputs],
        grid_spec=pltpu.PrefetchScalarGridSpec(
            num_scalar_prefetch=1,
            grid=(steps,),
            in_specs=[spec(a.shape, index) for a, index in inputs],
            out_specs=[spec(shape, index) for shape, _, index in outputs],
            scratch_shapes=list(scratch),
        ),
        compiler_params=params,
    )(where, *[a for a, _ in inputs])


def each(i):
    return i


def halves_swapped(i):
    return 1 - i


def lower(i):
    return lax.min(i, 1)


def upper(i):
    return lax.max(i - 2, 0)


def local_slices(core, width):
    at, slices = 0, []
    for plane in range(4):
        count = 2 * width if plane % 2 == core else width
        slices.append((plane, at, 0 if core == 0 else 3 * width - count, count))
        at += count
    return slices


def pack_kernel(
    gate_ref, conv_ref, step_ref, norm_ref, gain_ref, bias_ref, taps_ref,
    cols_ref, message_ref, *, head_width,
):
    inner = gate_ref.shape[1]
    group = 3 * head_width
    for chip in range(4):
        for core in range(2):
            for plane, at, start, count in local_slices(core, head_width):
                source = group * (4 * plane + chip) + start
                for first, ref in ((0, conv_ref), (cols_ref.shape[2] // 2, gate_ref)):
                    to = slice(first + at, first + at + count)
                    cols_ref[2 * chip + core, :, to] = ref[:, source : source + count]
    rest = conv_ref.shape[1] - inner
    rows = gate_ref.shape[0]
    message_ref[...] = jnp.zeros_like(message_ref)
    message_ref[:rows, :rest] = conv_ref[:, inner:]
    message_ref[:rows, rest : rest + step_ref.shape[1]] = step_ref[...]
    vectors = jnp.zeros((8, LANES), f32)

    def put(vectors, ref, at):
        value = ref[...].astype(f32)
        value = jnp.pad(value, ((at, 8 - at - value.shape[0]), (0, LANES - value.shape[1])))
        return vectors + value

    for ref, at in ((norm_ref, 0), (gain_ref, 1), (bias_ref, 2), (taps_ref, 3)):
        vectors = put(vectors, ref, at)
    message_ref[rows:, :LANES] = vectors.astype(bf16)


def setup_kernel(
    where_ref, s0, s1, s2, s3, s4, s5, s6, s7, heads_ref,
    shared_ref, norm_ref, taps_ref, channels_ref, head_rows_ref, pick_ref,
    gain_all, taps_all, held, *, n_taps, head_width,
):
    rank, plane = where_ref[0], where_ref[1]
    padded = shared_ref.shape[1]
    rows = norm_ref.shape[1] // 32
    block = 8 * rows
    rows_in, rows_out = norm_ref.shape[1] // 32, gain_all.shape[1] // 32
    piece = taps_all.shape[1] // 32
    inner = gain_all.shape[1]
    own = channels_ref.shape[1]
    for p in range(8):
        source = lax.bitwise_xor(rank, 2 * (p % 4) + p // 4)
        part_ref = (s0, s1, s2, s3, s4, s5, s6, s7)[p]
        for o in range(4):
            at = pl.multiple_of(o * block + source * rows, 16)
            lanes = slice(o * padded, (o + 1) * padded)
            shared_ref[pl.ds(at, rows), :] = part_ref[:rows, lanes]
            device = 8 * lax.bitwise_and(plane - o + 4, 3) + source
            held[device] = part_ref[rows : rows + 8, o * padded : o * padded + LANES].astype(f32)
    for i in range(32):
        vectors = held[i]
        norm_ref[:, i * rows_in : (i + 1) * rows_in] = vectors[0:1, :rows_in]
        gain_all[:, i * rows_out : (i + 1) * rows_out] = vectors[1:2, :rows_out]
        taps_all[:, i * piece : (i + 1) * piece] = vectors[:, :piece]
    taps_ref[...] = jnp.zeros_like(taps_ref)
    channels_ref[...] = jnp.zeros_like(channels_ref)
    taps_ref[0:n_taps, own:] = taps_all[3 : 3 + n_taps, inner:]
    taps_ref[n_taps : n_taps + 1, own:] = taps_all[2:3, inner:]
    for r in range(8):

        @pl.when(rank == r)
        def _(r=r):
            chip, core = r // 2, r % 2
            local, heads = iota((LANES, LANES), 0), iota((LANES, LANES), 1)
            chosen = jnp.zeros((LANES, LANES), jnp.bool_)
            for plane, at, start, count in local_slices(core, head_width):
                source = 3 * head_width * (4 * plane + chip) + start
                taps_ref[0:n_taps, at : at + count] = taps_all[3 : 3 + n_taps, source : source + count]
                taps_ref[n_taps : n_taps + 1, at : at + count] = taps_all[2:3, source : source + count]
                channels_ref[0:1, at : at + count] = gain_all[:, source : source + count]
                for j in range(count // head_width):
                    chosen |= (local == at // head_width + j) & (heads == source // head_width + j)
            pick_ref[...] = chosen.astype(f32)

    states = (padded - LANES) // 2
    chosen = pick_ref[...].astype(bf16)
    shared_ref[:, 2 * states :] = mm(shared_ref[:, 2 * states :], chosen, ((1,), (1,))).astype(bf16)
    head_rows = mm_exact(heads_ref[...], pick_ref[...], ((1,), (1,)))
    used = iota((1, LANES), 1) < own // head_width
    head_rows_ref[...] = jnp.zeros_like(head_rows_ref)
    head_rows_ref[0:1, :] = head_rows[0:1]
    head_rows_ref[1:2, :] = jnp.where(used, -jnp.exp(head_rows[1:2]), 0.0)
    channels_ref[1:2, :] = mm_exact(head_rows, head_map(own, head_width))[2:3]


def lend_kernel(where_ref, p0, p1, p2, p3, out_ref):
    core = lax.bitwise_and(where_ref[0], 1)
    third = out_ref.shape[1]
    for o, part in enumerate((p0, p1, p2, p3)):
        for k in range(2):

            @pl.when(core == k)
            def _(o=o, part=part, k=k):
                out_ref[o] = part[2 * third :, :] if k == 0 else part[:third, :]


def place_rows(out_ref, part_ref, borrowed_ref, o, core, at_plane):
    rows = part_ref.shape[0]
    third = rows // 3
    for k in range(2):
        for slices_plane, at, _, count in local_slices(k, 2 * third):

            @pl.when((core == k) & (at_plane == slices_plane))
            def _(k=k, at=at, count=count):
                if count == rows + third and k == 0:
                    out_ref[at : at + rows, :] = part_ref[...]
                    out_ref[at + rows : at + count, :] = borrowed_ref[o]
                elif count == rows + third:
                    out_ref[at : at + third, :] = borrowed_ref[o]
                    out_ref[at + third : at + count, :] = part_ref[...]
                elif k == 0:
                    out_ref[at : at + count, :] = part_ref[: 2 * third, :]
                else:
                    out_ref[at : at + count, :] = part_ref[third:, :]


def total_of(refs, rows=slice(None)):
    total = refs[0][rows].astype(f32)
    for ref in refs[1:]:
        total = total + ref[rows].astype(f32)
    return total


def as_row(column, count):
    return jnp.broadcast_to(column, (column.shape[0], LANES)).T[:1, :count]


def early_rows_kernel(p0, p1, p2, w_ref, gain_ref, out_ref, dot_ref):
    rows = out_ref.shape[0]
    block = p0.shape[1]
    for g in range(4):
        at = slice(g * rows, (g + 1) * rows)
        out_ref[:, g * block : (g + 1) * block] = total_of((p0, p1, p2), at)
    dot = jnp.sum(w_ref[...].astype(f32) * out_ref[...], axis=1, keepdims=True)
    dot_ref[...] = as_row(dot, rows) / gain_ref[...].astype(f32)


def late_rows_kernel(g0, g1, g2, c0, c1, c2, out_ref):
    own = g0.shape[1]
    rows = out_ref.shape[1]
    for r in range(8):
        at = slice(r * rows, (r + 1) * rows)
        out_ref[r, :, :own] = total_of((g0, g1, g2), at).astype(bf16)
        out_ref[r, :, own:] = total_of((c0, c1, c2), at).astype(bf16)


def columns_kernel(
    table_ref, w_gate_ref, w_conv_ref, w_step_ref, gain_ref, s0, s1, s2, s3,
    gate_ref, conv_ref, dot_ref, step_ref, taps_ref, bias_ref, step_bias_ref, decay_ref, skip_ref, *, head_width,
):
    group = 3 * head_width
    inner = 16 * group
    half = table_ref.shape[2] // 2
    for chip in range(4):
        for core in range(2):
            for plane, at, start, count in local_slices(core, head_width):
                to = slice(group * (4 * plane + chip) + start, group * (4 * plane + chip) + start + count)
                gate_ref[:, to] = table_ref[2 * chip + core, :, at : at + count].astype(f32)
                conv_ref[:, to] = table_ref[2 * chip + core, :, half + at : half + at + count].astype(f32)
    rows = gate_ref.shape[0]
    rest = conv_ref.shape[1] - inner
    shared = total_of((s0, s1, s2, s3))
    conv_ref[:, inner:] = shared[:rows, :rest]
    step_ref[...] = shared[:rows, rest : rest + step_ref.shape[1]]
    small = shared[rows:, :LANES] + shared[rows:, LANES : 2 * LANES]
    at = 0
    for ref in (taps_ref, bias_ref, step_bias_ref, decay_ref, skip_ref):
        ref[...] = small[at : at + ref.shape[0], : ref.shape[1]]
        at += ref.shape[0]
    total = jnp.sum(w_step_ref[...].astype(f32) * step_ref[...], axis=1, keepdims=True)
    for weight_ref, grad_ref in ((w_gate_ref, gate_ref), (w_conv_ref, conv_ref)):
        total = total + jnp.sum(weight_ref[...].astype(f32) * grad_ref[...], axis=1, keepdims=True)
    dot_ref[...] = as_row(total, rows) / gain_ref[...].astype(f32)


def tokens_out_kernel(
    where_ref, o0, o1, o2, o3, g0, g1, g2, g3, hidden_ref, cot_ref, sums_ref, norm_ref,
    output_ref, grad_ref, held, *, inner,
):
    rank, plane = where_ref[0], where_ref[1]
    tokens = hidden_ref[...].astype(f32)
    sums = jnp.concatenate([sums_ref[rank], jnp.zeros((LANES - 8, LANES), f32)], axis=0).T
    inv_gate = lax.rsqrt(sums[:, 0:1] / inner + norm_epsilon)
    output_ref[...] = (tokens + inv_gate * total_of((o0, o1, o2, o3))).astype(bf16)
    inv_rms = lax.rsqrt(jnp.mean(tokens * tokens, axis=1, keepdims=True) + norm_epsilon)
    width = tokens.shape[1]
    block = width // 4
    grad_ref[...] = total_of((g0, g1, g2, g3))
    for p in range(4):
        at = pl.multiple_of(block * lax.bitwise_and(plane - p + 4, 3), LANES)
        lanes = slice(p * block, (p + 1) * block)
        held[:, lanes] = grad_ref[:, pl.ds(at, block)] * norm_ref[:, lanes]
    grad_unit, unit = held[...], tokens * inv_rms
    mean = jnp.mean(grad_unit * unit, axis=1, keepdims=True)
    grad_ref[...] = cot_ref[...].astype(f32) + inv_rms * (grad_unit - unit * mean)


def once(kernel, inputs, outputs, where=None, scratch=(), params=grant):
    specs = lambda shapes: [pl.BlockSpec(s, lambda *_, n=len(s): (0,) * n) for s in shapes]
    out_shape = [jax.ShapeDtypeStruct(shape, dtype) for shape, dtype in outputs]
    grid_spec = pltpu.PrefetchScalarGridSpec(
        num_scalar_prefetch=0 if where is None else 1,
        grid=(1,),
        in_specs=specs([a.shape for a in inputs]),
        out_specs=specs([shape for shape, _ in outputs]),
        scratch_shapes=list(scratch),
    )
    call = pl.pallas_call(kernel, out_shape=out_shape, grid_spec=grid_spec, compiler_params=params)
    return call(*([] if where is None else [where]), *inputs)


def hop(value, distance):
    count = lax.axis_size("seq")
    pairs = [(i, i ^ distance) for i in range(count)]
    return lax.ppermute(value, "seq", pairs)


def plane_hop(value, distance):
    count = lax.axis_size("batch")
    pairs = [(i, (i + distance) % count) for i in range(count)]
    return lax.ppermute(value, "batch", pairs)


def planes_gather(value, direct=False):
    one, three = plane_hop(value, 1), plane_hop(value, -1)
    two = plane_hop(value, 2) if direct else plane_hop(one, 1)
    return [value, one, two, three]


def planes_parts(blocks):
    near, far = plane_hop(blocks[1], -1), plane_hop(blocks[2], 1)
    sent = (blocks[3].astype(f32) + far.astype(f32)).astype(blocks[3].dtype)
    return [blocks[0], near, plane_hop(sent, 1)]


def planes_direct(blocks):
    return [blocks[0]] + [plane_hop(blocks[o], -o) for o in (1, 2, 3)]


def plane_gather(value):
    chips = [value] + [hop(value, distance) for distance in (2, 4, 6)]
    return chips + [hop(part, 1) for part in chips]


def plane_parts(mine, other):
    count = mine.shape[0] // 4
    other = hop(other, 1)
    half = []
    for j in range(4):
        rows = slice(j * count, (j + 1) * count)
        half.append((mine[rows].astype(f32) + other[rows].astype(f32)).astype(bf16))
    return half[:1] + [hop(half[j], 2 * j) for j in (1, 2, 3)]


def plane_total(value):
    value = value + hop(value, 1)
    return value + hop(value, 2) + hop(value, 4) + hop(value, 6)


def local_group(index, core, width):
    plane, at = jnp.zeros_like(index), jnp.zeros_like(index)
    for k in range(2):
        for slices_plane, first, start, count in local_slices(k, width):
            inside = (core == k) & (index >= first) & (index < first + count)
            plane = jnp.where(inside, slices_plane, plane)
            at = jnp.where(inside, index - first + start, at)
    return plane, at


def shared_back_kernel(where_ref, rows_ref, taps_ref, heads_ref, pick_ref, mine_ref, other_ref, *, head_width, piece):
    rank, plane = where_ref[0], where_ref[1]
    rows = mine_ref.shape[2] - 8
    local = taps_ref.shape[1]
    own = 6 * head_width
    inner = 8 * own
    core, chip = lax.bitwise_and(rank, 1), lax.shift_right_logical(rank, 1)
    at = iota((local, LANES), 0)
    at_plane, offset = local_group(at, core, head_width)
    column = jnp.where(at < own, 3 * head_width * (4 * at_plane + chip) + offset, inner + at - own)
    heads = mm_exact(heads_ref[...], pick_ref[...])
    heads = jnp.concatenate([jnp.zeros((5, LANES), f32), heads[:3]], axis=0)
    high, low = halves(taps_ref[...])
    both = jnp.concatenate([high, low], axis=0)
    target = LANES * (column // piece) + column % piece - iota((local, LANES), 1)
    head_halves = halves(heads)
    for o in range(4):
        first = 8 * lax.bitwise_and(plane - o + 4, 3)
        for p in range(8):
            r = lax.bitwise_xor(rank, 2 * (p % 4) + p // 4)
            out_ref, q = (mine_ref, other_ref)[p // 4], p % 4
            chosen = (target == LANES * (first + r)).astype(bf16)
            spread = mm(both, chosen)
            own_rows = rows_ref[pl.ds(pl.multiple_of((8 * o + r) * rows, 16), rows), :]
            out_ref[q, o, :rows, : 2 * LANES] = own_rows[:, : 2 * LANES]
            out_ref[q, o, :rows, 2 * LANES :] = mm(own_rows[:, 2 * LANES :], pick_ref[...].astype(bf16)).astype(bf16)
            for half in (0, 1):
                value = spread[8 * half : 8 * half + 8].astype(bf16) + head_halves[half]
                out_ref[q, o, rows:, half * LANES : (half + 1) * LANES] = value
            out_ref[q, o, rows:, 2 * LANES :] = jnp.zeros((8, out_ref.shape[3] - 2 * LANES), bf16)


def split_local(
    hidden,
    norm_gain,
    w_gate_in,
    w_conv_in,
    w_step,
    conv_weight,
    conv_bias,
    step_bias,
    decay_log,
    skip_gain,
    gate_gain,
    w_out,
    cotangent,
):
    plane, rank = lax.axis_index("batch"), lax.axis_index("seq")
    planes, ranks = lax.axis_size("batch"), lax.axis_size("seq")
    _, span, width = hidden.shape
    rows_in, inner = w_gate_in.shape
    channels = w_conv_in.shape[1]
    heads = w_step.shape[1]
    head_width = inner // heads
    states = (channels - inner) // 2
    taps = conv_weight.shape[0]
    own = inner // ranks
    rows_out = w_out.shape[0]
    tokens = ranks * span
    block = width // planes
    piece = conv_bias.shape[0]
    devices = planes * ranks
    padded = -(-(2 * states + heads) // LANES) * LANES
    local = own + 2 * states
    third = rows_out // 3
    fixed = None
    where = jnp.stack([rank, plane]).astype(jnp.int32)

    out_parts = planes_gather(w_out)
    cols, message = once(
        functools.partial(pack_kernel, head_width=head_width),
        [w_gate_in, w_conv_in, w_step, norm_gain[None], gate_gain[None], conv_bias[None], conv_weight],
        [((ranks, rows_in, 2 * own), bf16), ((rows_in + 8, padded), bf16)],
        params=whole_grant,
    )
    cols = lax.all_to_all(cols, "seq", 0, 0).reshape(ranks * rows_in, 2 * own)
    message = jnp.concatenate(planes_gather(message, True), axis=1)
    message = [hidden[0], message, jnp.zeros((span // 2 - rows_in - 8, width), bf16)]
    tokens_rel, cot_rel = plane_gather(jnp.concatenate(message)), plane_gather(cotangent[0])
    token_part, shared_part = Part((span, width), (0, 0)), Part((span // 2, width), (2, 0))
    conv_w, gate_w = planes_gather(cols[:, :own]), planes_gather(cols[:, own:])
    head_values = jnp.pad(jnp.stack([step_bias, decay_log, skip_gain]), ((0, 5), (0, LANES - heads)))
    shared_w, norm_full, taps_rows, channel_rows, head_rows, head_table = rows_call(
        functools.partial(setup_kernel, n_taps=taps, head_width=head_width),
        where,
        1,
        None,
        [(a, shared_part) for a in tokens_rel] + [(head_values, fixed)],
        [
            ((width, padded), bf16, fixed),
            ((1, width), f32, fixed),
            ((8, local), f32, fixed),
            ((8, own), f32, fixed),
            ((8, LANES), f32, fixed),
            ((LANES, LANES), f32, fixed),
        ],
        [
            pltpu.VMEM((1, inner), f32),
            pltpu.VMEM((8, channels), f32),
            pltpu.VMEM((devices, 8, LANES), f32),
        ],
    )
    (lent_rows,) = once(lend_kernel, out_parts, [((planes, third, width), bf16)], where)
    out_borrowed = hop(lent_rows, 1)

    sizes = dict(n_taps=taps, head_width=head_width, states=states)
    rows = tokens // 4
    normed, pre, raw, rest_w = rows_call(
        functools.partial(project_kernel, states=states),
        where,
        4,
        rows,
        [(a, token_part) for a in tokens_rel]
        + [(a, fixed) for a in (norm_full, *conv_w, shared_w)],
        [
            ((tokens, width), bf16, each),
            ((tokens, local), bf16, each),
            ((tokens, LANES), f32, each),
            ((width, own + padded), bf16, fixed),
        ],
        params=wide_grant,
    )
    pre, raw = pre.reshape(ranks, span, local), raw.reshape(ranks, span, LANES)
    mixed, conv, inter, ssm, entering = spans_call(
        functools.partial(forward_kernel, **sizes),
        where,
        ranks,
        [(pre, relative), (raw, relative)]
        + [(a, fixed) for a in (taps_rows, head_rows, channel_rows)],
        [
            ((span, local), f32, in_time),
            ((span, local), bf16, in_time),
            ((span, own), f32, in_time),
            ((span, own), f32, relative),
            ((states, own), f32, in_time),
        ],
        [pltpu.VMEM((span + 8, local), f32), pltpu.VMEM((states, own), f32)],
    )
    ssm = ssm.reshape(tokens, own)
    gate, ngate, sums, gated, gate_all, cot, out_w = rows_call(
        gate_kernel,
        where,
        4,
        rows,
        [(normed, each)]
        + [(a, fixed) for a in (*gate_w, *cot_rel, *out_parts, out_borrowed, channel_rows)]
        + [(ssm, each)],
        [
            ((tokens, own), f32, each),
            ((tokens, own), f32, each),
            ((ranks, 8, LANES), f32, fixed),
            ((tokens, own), bf16, each),
            ((width, own), bf16, fixed),
            ((tokens, width), bf16, each),
            ((own, width), bf16, fixed),
        ],
        params=wide_grant,
    )
    sums = plane_total(sums)
    part_mine, part_other = rows_call(
        out_part_kernel,
        where,
        4,
        rows,
        [(gated, each), (out_w, fixed)],
        [((tokens // 2, width), bf16, lower), ((tokens // 2, width), bf16, upper)],
    )
    out_own = plane_parts(part_mine, part_other)

    grad_y, grad_gate, projected, lent = rows_call(
        functools.partial(gate_back_kernel, inner=inner, third=third),
        where,
        4,
        rows,
        [(sums, fixed), (ssm, each), (gate, each), (ngate, each), (channel_rows, fixed)],
        [
            ((tokens, own), f32, each),
            ((tokens, own), bf16, each),
            ((tokens, own), bf16, each),
            ((tokens, LANES), bf16, each),
        ],
    )
    borrowed = hop(lent, 1)
    d_gate = rows_call(
        gate_grad_kernel,
        where,
        planes,
        None,
        [(normed, Columns((tokens, block))), (grad_gate, fixed)],
        [((block, own), bf16, fixed)] * 4,
    )
    d_gate = planes_parts(d_gate)
    d_out = rows_call(
        functools.partial(out_grad_kernel, third=third),
        where,
        2,
        tokens // 2,
        [(projected, each), (borrowed, halves_swapped), (cot, each)],
        [((4 * rows_out, block), bf16, fixed)] * 4,
        [pltpu.VMEM((tokens // 2, own), bf16), pltpu.VMEM((own, width), f32)],
    )
    d_out = planes_parts(d_out)
    grad_rest, grad_taps, grad_heads = spans_call(
        functools.partial(backward_kernel, **sizes),
        where,
        ranks,
        [(grad_y.reshape(ranks, span, own), relative_reverse)]
        + [(a, in_reverse) for a in (inter, entering, conv)]
        + [(pre, relative_reverse), (mixed, in_reverse), (raw, relative_reverse)]
        + [(a, fixed) for a in (taps_rows, head_rows, channel_rows)],
        [
            ((span, own + padded), bf16, relative_reverse),
            ((8, local), f32, fixed),
            ((8, LANES), f32, fixed),
        ],
        [
            pltpu.VMEM((span + 8, local), f32),
            pltpu.VMEM((states, own), f32),
            pltpu.VMEM((states, own), f32),
        ],
    )
    grad_rest = grad_rest.reshape(tokens, own + padded)
    d_rest = jnp.dot(normed.T, grad_rest, preferred_element_type=f32).astype(bf16)
    d_conv = planes_parts([d_rest[o * block : (o + 1) * block, :own] for o in range(planes)])
    d_shared = rows_call(
        functools.partial(shared_back_kernel, head_width=head_width, piece=piece),
        where,
        1,
        None,
        [(d_rest, Columns((width, padded), own // padded))]
        + [(a, fixed) for a in (grad_taps, grad_heads, head_table)],
        [((ranks // 2, planes, rows_in + 8, padded), bf16, fixed)] * 2,
    )
    gate_all, *d_shared = lax.optimization_barrier((gate_all, *d_shared))
    mine, other = input_grad_call(grad_gate, grad_rest, gate_all, rest_w)
    grad_own = plane_parts(mine, other)
    d_shared = [a.reshape(ranks // 2 * planes, rows_in + 8, padded) for a in d_shared]
    d_shared = plane_parts(d_shared[0], d_shared[1])
    d_shared = sum(part.astype(f32) for part in d_shared)
    d_shared = planes_direct([d_shared[o] for o in range(planes)])

    d_out, d_gain = once(
        early_rows_kernel,
        [*d_out, w_out, gate_gain[None]],
        [((rows_out, width), f32), ((1, rows_out), f32)],
    )
    (d_in,) = once(late_rows_kernel, [*d_gate, *d_conv], [((ranks, rows_in, 2 * own), bf16)])
    d_in = lax.all_to_all(d_in, "seq", 0, 0)
    output, grad_hidden = once(
        functools.partial(tokens_out_kernel, inner=inner),
        [*out_own, *grad_own, hidden[0], cotangent[0], sums, norm_full],
        [((span, width), bf16), ((span, width), f32)],
        where,
        [pltpu.VMEM((span, width), f32)],
    )
    d_gate, d_conv, d_norm, d_step, *small = once(
        functools.partial(columns_kernel, head_width=head_width),
        [d_in, w_gate_in, w_conv_in, w_step, norm_gain[None], *d_shared],
        [
            ((rows_in, inner), f32),
            ((rows_in, channels), f32),
            ((1, rows_in), f32),
            ((rows_in, heads), f32),
            ((taps, piece), f32),
            ((1, piece), f32),
            ((1, heads), f32),
            ((1, heads), f32),
            ((1, heads), f32),
        ],
    )
    return (
        output[None],
        grad_hidden[None],
        d_norm[0],
        d_gate,
        d_conv,
        d_step,
        small[0],
        small[1][0],
        small[2][0],
        small[3][0],
        small[4][0],
        d_gain[0],
        d_out,
    )


def split_block(*args):
    return split_local(*args)


def solution(mesh):
    split = (mesh.shape["batch"], mesh.shape["seq"]) == (4, 8)
    body = split_block if split else local
    return jax.shard_map(
        body,
        mesh=mesh,
        in_specs=(
            P("batch", "seq", None),
            P(("batch", "seq")),
            P(("batch", "seq"), None),
            P(("batch", "seq"), None),
            P(("batch", "seq"), None),
            P(None, ("batch", "seq")),
            P(("batch", "seq")),
            P(),
            P(),
            P(),
            P(("batch", "seq")),
            P(("batch", "seq"), None),
            P("batch", "seq", None),
        ),
        out_specs=(
            P("batch", "seq", None),
            P("batch", "seq", None),
            P(("batch", "seq")),
            P(("batch", "seq"), None),
            P(("batch", "seq"), None),
            P(("batch", "seq"), None),
            P(None, ("batch", "seq")),
            P(("batch", "seq")),
            P(),
            P(),
            P(),
            P(("batch", "seq")),
            P(("batch", "seq"), None),
        ),
        check_vma=False,
    )
```

```python
import functools
import typing

import jax
import jax.numpy as jnp
from jax import lax
from jax.experimental import pallas as pl
from jax.experimental.pallas import tpu as pltpu
from jax.sharding import PartitionSpec as P

norm_epsilon = 1e-05


def shifted(value, axis, steps):
    count = lax.axis_size(axis)
    first, last = (max(0, -steps), min(count, count - steps))
    return lax.ppermute(value, axis, [(source, source + steps) for source in range(first, last)])


def prefix(array, axis, combine, identity, reverse):
    devices, place = (lax.axis_size(axis), lax.axis_index(axis))
    everything = jax.tree.map(lambda part: lax.all_gather(part, axis), array)
    start = jax.tree.map(
        lambda part, zero: jnp.broadcast_to(jnp.asarray(zero, part.dtype), part.shape),
        array,
        identity,
    )

    def hop(k, before):
        at = devices - 1 - k if reverse else k
        reached = at > place if reverse else at < place
        new = combine(before, jax.tree.map(lambda part: part[at], everything))
        return jax.tree.map(lambda a, b: jnp.where(reached, a, b), new, before)

    return lax.fori_loop(0, devices, hop, start)


def for_sending(array):
    return jax.tree.map(lambda a: a.astype(jnp.bfloat16) if a.dtype == jnp.float32 else a, array)


def narrow_product(pattern, former, latter):
    return jnp.einsum(pattern, former, latter, preferred_element_type=jnp.float32)


def wide_product(pattern, former, latter):
    return jnp.einsum(pattern, former, latter, precision=lax.Precision.HIGHEST)


def silu_slope(inputs):
    logistic = jax.nn.sigmoid(inputs)
    return logistic * (1.0 + inputs * (1.0 - logistic))


def upper_table(length):
    rows = lax.broadcasted_iota(jnp.int32, (length, length), 0)
    cols = lax.broadcasted_iota(jnp.int32, (length, length), 1)
    return (rows <= cols).astype(jnp.float32)


def running_total(step_size, head_rate):
    table = upper_table(step_size.shape[0])
    return jnp.dot((step_size * head_rate[None, :]).T, table, precision=lax.Precision.HIGHEST)


def span_parts(value_b, key_b, query_b, step_size, head_rate):
    length = step_size.shape[0]
    cumulative = running_total(step_size, head_rate)
    row_index = lax.broadcasted_iota(jnp.int32, (1, length, length), 1)
    col_index = lax.broadcasted_iota(jnp.int32, (1, length, length), 2)
    causal = row_index >= col_index
    spread = cumulative[:, :, None] - cumulative[:, None, :]
    decays = jnp.where(causal, jnp.exp(jnp.where(causal, spread, 0.0)), 0.0)
    affinity = jnp.dot(query_b, key_b.T, preferred_element_type=jnp.float32)
    step_rows = step_size.T
    scores = affinity[None] * decays * step_rows[:, None, :]
    mixing = scores.astype(jnp.bfloat16)
    within = narrow_product("hts,shp->thp", mixing, value_b)
    tail_decay = jnp.exp(cumulative[:, -1:] - cumulative) * step_rows
    weighted = (tail_decay.T[:, :, None] * value_b.astype(jnp.float32)).astype(jnp.bfloat16)
    span_state = narrow_product("shp,sn->hpn", weighted, key_b)
    total_decay = jnp.exp(cumulative[:, -1])
    return (within, span_state, total_decay, cumulative, decays, affinity, scores, mixing, weighted)


def span_inter(query_b, cumulative, carried):
    base = wide_product("tn,hpn->thp", query_b.astype(jnp.float32), carried)
    return jnp.exp(cumulative).T[:, :, None] * base


def carried_grad(query_b, cumulative, grad_y):
    scaled = grad_y * jnp.exp(cumulative).T[:, :, None]
    return wide_product("thp,tn->hpn", scaled, query_b.astype(jnp.float32))


def span_backward(
    value_b, key_b, query_b, step_size, carried, grad_y, grad_state, grad_total, head_rate
):
    parts = span_parts(value_b, key_b, query_b, step_size, head_rate)
    total_decay, cumulative, decays, affinity, scores, mixing, weighted = parts[2:]
    length = step_size.shape[0]
    query_f = query_b.astype(jnp.float32)
    key_f = key_b.astype(jnp.float32)
    value_f = value_b.astype(jnp.float32)
    step_rows = step_size.T
    growth = jnp.exp(cumulative)
    base = wide_product("tn,hpn->thp", query_f, carried)
    grad_cumul = growth * jnp.sum(grad_y * base, axis=2).T
    grad_query = wide_product("thp,hpn->tn", grad_y * growth.T[:, :, None], carried)
    grad_low = grad_y.astype(jnp.bfloat16)
    grad_mixing = narrow_product("thp,shp->hts", grad_low, value_b)
    grad_value = narrow_product("hts,thp->shp", mixing, grad_low)
    grad_affinity = jnp.sum(grad_mixing * decays * step_rows[:, None, :], axis=0)
    grad_steps = jnp.sum(grad_mixing * affinity[None] * decays, axis=1)
    through = grad_mixing * scores
    grad_cumul = grad_cumul + jnp.sum(through, axis=2) - jnp.sum(through, axis=1)
    grad_query = grad_query + wide_product("ts,sn->tn", grad_affinity, key_f)
    grad_key = wide_product("ts,tn->sn", grad_affinity, query_f)
    grad_weighted = wide_product("hpn,sn->shp", grad_state, key_f)
    grad_key = grad_key + wide_product("shp,hpn->sn", weighted.astype(jnp.float32), grad_state)
    grad_end = jnp.sum(grad_weighted * value_f, axis=2).T
    tail_only = jnp.exp(cumulative[:, -1:] - cumulative)
    grad_value = grad_value + grad_weighted * (tail_only * step_rows).T[:, :, None]
    grad_steps = grad_steps + grad_end * tail_only
    push = grad_end * tail_only * step_rows
    last_flag = lax.broadcasted_iota(jnp.int32, (1, length), 1) == length - 1
    last_term = (jnp.sum(push, axis=1) + grad_total * total_decay)[:, None]
    grad_cumul = grad_cumul - push + jnp.where(last_flag, last_term, 0.0)
    grad_log = jnp.dot(grad_cumul, upper_table(length).T, precision=lax.Precision.HIGHEST)
    grad_steps = grad_steps + grad_log * head_rate[:, None]
    grad_rate = jnp.sum(grad_log * step_rows, axis=1)
    return (grad_value, grad_key, grad_query, grad_steps.T, grad_rate)


def conv_apply(padded, kernel_f, bias_f, length):
    time_axis = padded.ndim - 2
    total = bias_f
    for offset in range(kernel_f.shape[0]):
        total = total + kernel_f[offset] * lax.slice_in_dim(
            padded, offset, offset + length, axis=time_axis
        )
    return total


def conv_back(grad_mixed, padded, kernel_f):
    length = grad_mixed.shape[-2]
    kernel_taps = kernel_f.shape[0]
    time_axis = grad_mixed.ndim - 2
    leading = tuple(range(grad_mixed.ndim - 1))
    grad_kernel = jnp.stack(
        [
            jnp.sum(
                grad_mixed * lax.slice_in_dim(padded, offset, offset + length, axis=time_axis),
                axis=leading,
            )
            for offset in range(kernel_taps)
        ]
    )
    grad_padded = jnp.zeros(padded.shape, jnp.float32)
    for offset in range(kernel_taps):
        widths = [(0, 0)] * grad_mixed.ndim
        widths[time_axis] = (offset, kernel_taps - 1 - offset)
        grad_padded = grad_padded + jnp.pad(grad_mixed * kernel_f[offset], widths)
    return (grad_kernel, grad_padded)


def combine_states(earlier, later):
    return (earlier[0] * later[0], later[0][:, :, None, None] * earlier[1] + later[1])


def local(
    hidden,
    norm_gain,
    w_gate_in,
    w_conv_in,
    w_step,
    conv_weight,
    conv_bias,
    step_bias,
    decay_log,
    skip_gain,
    gate_gain,
    w_out,
    cotangent,
):
    seq_count, length, model_width = hidden.shape
    gathered = (
        lax.all_gather(norm_gain, ("batch", "seq"), axis=0, tiled=True),
        lax.all_gather(w_gate_in, ("batch", "seq"), axis=0, tiled=True),
        lax.all_gather(w_conv_in, ("batch", "seq"), axis=0, tiled=True),
        lax.all_gather(w_step, ("batch", "seq"), axis=0, tiled=True),
        lax.all_gather(conv_weight, ("batch", "seq"), axis=1, tiled=True),
        lax.all_gather(conv_bias, ("batch", "seq"), axis=0, tiled=True),
        lax.all_gather(gate_gain, ("batch", "seq"), axis=0, tiled=True),
        lax.all_gather(w_out, ("batch", "seq"), axis=0, tiled=True),
    )
    (
        norm_full,
        gate_in_full,
        conv_in_full,
        step_full,
        kernel_full,
        bias_full,
        gain_full,
        out_full,
    ) = gathered
    inner_width = gate_in_full.shape[1]
    head_count = step_full.shape[1]
    head_width = inner_width // head_count
    channels = conv_in_full.shape[1]
    state_width = (channels - inner_width) // 2
    kernel_taps = kernel_full.shape[0]
    row_count = seq_count * length
    head_rate = -jnp.exp(decay_log)
    tokens_f = hidden.reshape(row_count, model_width).astype(jnp.float32)
    inv_rms = lax.rsqrt(jnp.mean(tokens_f * tokens_f, axis=1, keepdims=True) + norm_epsilon)
    unit = tokens_f * inv_rms
    normed = (unit * norm_full.astype(jnp.float32)[None]).astype(jnp.bfloat16)
    gate_pre = jnp.dot(normed, gate_in_full, preferred_element_type=jnp.float32)
    conv_pre = (
        jnp.dot(normed, conv_in_full, preferred_element_type=jnp.float32)
        .astype(jnp.bfloat16)
        .reshape(seq_count, length, channels)
    )
    raw_step = jnp.dot(normed, step_full, preferred_element_type=jnp.float32)
    rim = shifted(conv_pre[:, length - (kernel_taps - 1) :, :], "seq", 1)
    extended = jnp.concatenate([rim, conv_pre], axis=1).astype(jnp.float32)
    mixed_in = conv_apply(
        extended, kernel_full.astype(jnp.float32), bias_full.astype(jnp.float32), length
    )
    conv_out = jax.nn.silu(mixed_in).astype(jnp.bfloat16)
    value_b = conv_out[:, :, :inner_width].reshape(seq_count, length, head_count, head_width)
    key_b = conv_out[:, :, inner_width : inner_width + state_width]
    query_b = conv_out[:, :, inner_width + state_width :]
    step_size = jax.nn.softplus(raw_step + step_bias[None]).reshape(seq_count, length, head_count)

    def local_forward(value_piece, key_piece, query_piece, step_piece):
        parts = span_parts(value_piece, key_piece, query_piece, step_piece, head_rate)
        return (parts[0], parts[1], parts[2], parts[3])

    within, span_state, total_decay, cumulative = jax.vmap(local_forward)(
        value_b, key_b, query_b, step_size
    )
    identity = (jnp.ones_like(total_decay), jnp.zeros_like(span_state))
    _, carried = prefix((total_decay, span_state), "seq", combine_states, identity, False)
    inter = jax.vmap(span_inter)(query_b, cumulative, carried)
    value_f = value_b.astype(jnp.float32)
    ssm_out = within + inter + skip_gain[None, None, :, None] * value_f
    flat_out = ssm_out.reshape(row_count, inner_width)
    gate_silu = jax.nn.silu(gate_pre)
    gated = flat_out * gate_silu
    inv_gate = lax.rsqrt(jnp.mean(gated * gated, axis=1, keepdims=True) + norm_epsilon)
    normed_gate = gated * inv_gate
    projected_in = (normed_gate * gain_full.astype(jnp.float32)[None]).astype(jnp.bfloat16)
    output = (
        tokens_f + jnp.dot(projected_in, out_full, preferred_element_type=jnp.float32)
    ).astype(jnp.bfloat16)
    backward_weights = (
        lax.all_gather(norm_gain, ("batch", "seq"), axis=0, tiled=True),
        lax.all_gather(w_gate_in, ("batch", "seq"), axis=0, tiled=True),
        lax.all_gather(w_conv_in, ("batch", "seq"), axis=0, tiled=True),
        lax.all_gather(w_step, ("batch", "seq"), axis=0, tiled=True),
        lax.all_gather(conv_weight, ("batch", "seq"), axis=1, tiled=True),
        lax.all_gather(gate_gain, ("batch", "seq"), axis=0, tiled=True),
        lax.all_gather(w_out, ("batch", "seq"), axis=0, tiled=True),
    )
    norm_back, gate_in_back, conv_in_back, step_back, kernel_back, gain_back, out_back = (
        backward_weights
    )
    incoming = cotangent.reshape(row_count, model_width)
    grad_proj = jnp.dot(incoming, out_back.T, preferred_element_type=jnp.float32)
    grad_w_out = jnp.dot(projected_in.T, incoming, preferred_element_type=jnp.float32)
    grad_gate_gain = jnp.sum(grad_proj * normed_gate, axis=0)
    grad_ngate = grad_proj * gain_back.astype(jnp.float32)[None]
    grad_gated = inv_gate * (
        grad_ngate - normed_gate * jnp.mean(grad_ngate * normed_gate, axis=1, keepdims=True)
    )
    grad_flat = grad_gated * gate_silu
    grad_gate_pre = (grad_gated * flat_out * silu_slope(gate_pre)).astype(jnp.bfloat16)
    grad_ssm = grad_flat.reshape(seq_count, length, head_count, head_width)
    grad_skip = jnp.sum(grad_ssm * value_f, axis=(0, 1, 3))
    grad_carried = jax.vmap(carried_grad)(query_b, cumulative, grad_ssm)
    _, grad_state = prefix((total_decay, grad_carried), "seq", combine_states, identity, True)
    grad_total = jnp.sum(grad_state * carried, axis=(2, 3))

    def local_backward(
        value_piece,
        key_piece,
        query_piece,
        step_piece,
        carried_piece,
        grad_piece,
        state_piece,
        total_piece,
    ):
        return span_backward(
            value_piece,
            key_piece,
            query_piece,
            step_piece,
            carried_piece,
            grad_piece,
            state_piece,
            total_piece,
            head_rate,
        )

    grad_value, grad_key, grad_query, grad_steps, grad_rate = jax.vmap(local_backward)(
        value_b, key_b, query_b, step_size, carried, grad_ssm, grad_state, grad_total
    )
    grad_value = grad_value + grad_ssm * skip_gain[None, None, :, None]
    grad_conv_out = jnp.concatenate(
        [grad_value.reshape(seq_count, length, inner_width), grad_key, grad_query], axis=2
    )
    grad_mixed = grad_conv_out * silu_slope(mixed_in)
    grad_bias = jnp.sum(grad_mixed, axis=(0, 1))
    grad_kernel, grad_padded = conv_back(grad_mixed, extended, kernel_back.astype(jnp.float32))
    back_rim = shifted(for_sending(grad_padded[:, : kernel_taps - 1, :]), "seq", -1)
    grad_core = grad_padded[:, kernel_taps - 1 :, :]
    split_at = length - (kernel_taps - 1)
    grad_core = jnp.concatenate(
        [grad_core[:, :split_at], grad_core[:, split_at:] + back_rim], axis=1
    )
    grad_pre = grad_core.astype(jnp.bfloat16).reshape(row_count, channels)
    grad_raw = grad_steps.reshape(row_count, head_count) * jax.nn.sigmoid(
        raw_step + step_bias[None]
    )
    grad_step_bias = jnp.sum(grad_raw, axis=0)
    grad_raw_low = grad_raw.astype(jnp.bfloat16)
    grad_decay_log = jnp.sum(grad_rate, axis=0) * head_rate
    grad_w_gate_in = jnp.dot(normed.T, grad_gate_pre, preferred_element_type=jnp.float32)
    grad_w_conv_in = jnp.dot(normed.T, grad_pre, preferred_element_type=jnp.float32)
    grad_w_step = jnp.dot(normed.T, grad_raw_low, preferred_element_type=jnp.float32)
    grad_normed = jnp.dot(grad_gate_pre, gate_in_back.T, preferred_element_type=jnp.float32)
    grad_normed = grad_normed + jnp.dot(
        grad_pre, conv_in_back.T, preferred_element_type=jnp.float32
    )
    grad_normed = grad_normed + jnp.dot(
        grad_raw_low, step_back.T, preferred_element_type=jnp.float32
    )
    grad_norm_gain = jnp.sum(grad_normed * unit, axis=0)
    grad_unit = grad_normed * norm_back.astype(jnp.float32)[None]
    grad_tokens = inv_rms * (grad_unit - unit * jnp.mean(grad_unit * unit, axis=1, keepdims=True))
    grad_hidden = (incoming.astype(jnp.float32) + grad_tokens).reshape(
        seq_count, length, model_width
    )
    partial_grads = (
        grad_norm_gain,
        grad_w_gate_in,
        grad_w_conv_in,
        grad_w_step,
        grad_kernel,
        grad_bias,
        grad_gate_gain,
        grad_w_out,
    )
    shares = (
        lax.psum_scatter(partial_grads[0], ("batch", "seq"), scatter_dimension=0, tiled=True),
        lax.psum_scatter(partial_grads[1], ("batch", "seq"), scatter_dimension=0, tiled=True),
        lax.psum_scatter(partial_grads[2], ("batch", "seq"), scatter_dimension=0, tiled=True),
        lax.psum_scatter(partial_grads[3], ("batch", "seq"), scatter_dimension=0, tiled=True),
        lax.psum_scatter(partial_grads[4], ("batch", "seq"), scatter_dimension=1, tiled=True),
        lax.psum_scatter(partial_grads[5], ("batch", "seq"), scatter_dimension=0, tiled=True),
        lax.psum_scatter(partial_grads[6], ("batch", "seq"), scatter_dimension=0, tiled=True),
        lax.psum_scatter(partial_grads[7], ("batch", "seq"), scatter_dimension=0, tiled=True),
    )
    head_sums = lax.psum((grad_step_bias, grad_decay_log, grad_skip), ("batch", "seq"))
    return (
        output.reshape(seq_count, length, model_width),
        grad_hidden,
        shares[0],
        shares[1],
        shares[2],
        shares[3],
        shares[4],
        shares[5],
        head_sums[0],
        head_sums[1],
        head_sums[2],
        shares[6],
        shares[7],
    )


bf16 = jnp.bfloat16
f32 = jnp.float32
EXACT = lax.Precision.HIGHEST
LANES = 128


def granted(mebibytes):
    return pltpu.CompilerParams(vmem_limit_bytes=mebibytes << 20)


grant, wide_grant, whole_grant = granted(10), granted(18), granted(60)


def mm(former, latter, dims=((1,), (0,))):
    return lax.dot_general(former, latter, (dims, ((), ())), preferred_element_type=f32)


def mm_exact(former, latter, dims=((1,), (0,))):
    return lax.dot_general(
        former, latter, (dims, ((), ())), precision=EXACT, preferred_element_type=f32
    )


def halves(array):
    high = array.astype(bf16)
    return high, (array - high.astype(f32)).astype(bf16)


def iota(shape, axis):
    return lax.broadcasted_iota(jnp.int32, shape, axis)


def head_map(own, head_width):
    return (iota((LANES, own), 0) == iota((LANES, own), 1) // head_width).astype(f32)


def triangle_sum(table, array):
    high, low = halves(array)
    table = table.astype(bf16)
    return mm(jnp.concatenate([table, table], axis=1), jnp.concatenate([high, low], axis=0))


def twice(array):
    return jnp.concatenate([array, array], axis=1)


def stacked_halves(array):
    return jnp.concatenate(halves(array), axis=0)


def step_tables(raw, rate):
    span = raw.shape[0]
    step = jnp.maximum(raw, 0.0) + jnp.log1p(jnp.exp(-jnp.abs(raw)))
    return step, triangle_sum(iota((span, span), 0) >= iota((span, span), 1), step * rate)


def pair_masked(array, head_width):
    low = iota(array.shape, 1) < head_width
    zero = jnp.zeros_like(array)
    return jnp.concatenate([jnp.where(low, array, zero), jnp.where(low, zero, array)], axis=0)


def by_pair_lanes(array, pair, head_width):
    shape = (array.shape[0], 2 * head_width)
    first = jnp.broadcast_to(array[:, 2 * pair : 2 * pair + 1], shape)
    second = jnp.broadcast_to(array[:, 2 * pair + 1 : 2 * pair + 2], shape)
    return jnp.where(iota(shape, 1) < head_width, first, second)


def place(i, rank):
    m = lax.bitwise_xor(i, rank)
    return 4 * lax.bitwise_and(m, 1) + lax.shift_right_logical(m, 1)


def span_at(place_index, rank):
    m = 2 * lax.bitwise_and(place_index, 3) + lax.shift_right_logical(place_index, 2)
    return lax.bitwise_xor(m, rank)


def project_kernel(
    where_ref, t0, t1, t2, t3, t4, t5, t6, t7, gain_ref, w0, w1, w2, w3, shared_ref,
    normed_ref, pre_ref, raw_ref, weight_ref, *, states,
):
    step = pl.program_id(0)
    plane = where_ref[1]
    span, width = t0.shape
    own = w0.shape[1]
    block = width // 4

    @pl.when(step == 0)
    def _():
        for o, w in enumerate((w0, w1, w2, w3)):
            weight_ref[o * block : (o + 1) * block, :own] = w[...]
        weight_ref[:, own:] = shared_ref[...]

    parts = (t0, t1, t2, t3, t4, t5, t6, t7)
    for half in range(4):

        @pl.when(step == half)
        def _(half=half):
            for i in range(2):
                part = parts[2 * half + i]
                tokens = part[...].astype(f32)
                inv_rms = lax.rsqrt(jnp.mean(tokens * tokens, axis=1, keepdims=True) + norm_epsilon)
                for o in range(4):
                    at = pl.multiple_of(lax.bitwise_and(plane - o + 4, 3) * block, LANES)
                    value = part[:, pl.ds(at, block)].astype(f32) * inv_rms
                    value = (value * gain_ref[:, pl.ds(at, block)]).astype(bf16)
                    normed_ref[i * span : (i + 1) * span, o * block : (o + 1) * block] = value

    product = mm(normed_ref[...], weight_ref[...])
    local = own + 2 * states
    pre_ref[...] = product[:, :local].astype(bf16)
    raw_ref[...] = product[:, local:]


def forward_kernel(
    where_ref, pre_ref, raw_ref, taps_ref, heads_ref, rows_ref,
    mixed_ref, conv_ref, inter_ref, ssm_ref, state_ref,
    ext, state, *, n_taps, head_width, states,
):
    span, own = ssm_ref.shape[1:]

    @pl.when(pl.program_id(0) == 0)
    def _():
        ext[0:8, :] = jnp.zeros((8, ext.shape[1]), f32)
        state[...] = jnp.zeros_like(state)

    ext[8 : 8 + span, :] = pre_ref[0].astype(f32)
    mixed = taps_ref[n_taps : n_taps + 1, :]
    for k in range(n_taps):
        first = 8 - (n_taps - 1) + k
        mixed = mixed + taps_ref[k : k + 1, :] * ext[first : first + span, :]
    mixed_ref[0] = mixed
    ext[0:8, :] = ext[span : span + 8, :]
    conv = (mixed * jax.nn.sigmoid(mixed)).astype(bf16)
    conv_ref[0] = conv
    key, query = conv[:, own : own + states], conv[:, own + states :]
    step, cum = step_tables(raw_ref[0] + heads_ref[0:1, :], heads_ref[1:2, :])
    cum_t, step_t = cum.T, step.T
    affinity = mm(query, key, ((1,), (1,)))
    causal = iota((span, span), 0) >= iota((span, span), 1)
    entering = state[...]
    state_ref[0] = entering
    base = mm(twice(query), stacked_halves(entering))
    weighted, kept = [], []
    for pair in range(own // (2 * head_width)):
        lanes = slice(2 * pair * head_width, 2 * (pair + 1) * head_width)
        value = conv_ref[0, :, lanes]
        mixing = []
        for h in (2 * pair, 2 * pair + 1):
            decay = jnp.exp(jnp.where(causal, cum[:, h : h + 1] - cum_t[h : h + 1, :], -1e30))
            mixing.append((affinity * decay * step_t[h : h + 1, :]).astype(bf16))
        cum_pair = by_pair_lanes(cum, pair, head_width)
        growth = jnp.exp(cum_pair)
        tailed = jnp.exp(cum_pair[span - 1 : span, :] - cum_pair) * by_pair_lanes(step, pair, head_width)
        inter = growth * base[:, lanes]
        inter_ref[0, :, lanes] = inter
        value_f = value.astype(f32)
        within = mm(jnp.concatenate(mixing, axis=1), pair_masked(value, head_width))
        ssm_ref[0, :, lanes] = within + inter + rows_ref[1:2, lanes] * value_f
        weighted.append((tailed * value_f).astype(bf16))
        kept.append(growth[span - 1 : span, :])
    weighted, kept = jnp.concatenate(weighted, axis=1), jnp.concatenate(kept, axis=1)
    state[...] = kept * entering + mm(key, weighted, ((0,), (0,)))


def gate_kernel(
    where_ref, normed_ref, g0, g1, g2, g3, c0, c1, c2, c3, c4, c5, c6, c7,
    p0, p1, p2, p3, borrowed_ref, rows_ref, ssm_ref,
    gate_ref, ngate_ref, sums_ref, gated_ref, weight_ref, cot_ref, out_ref,
):
    step = pl.program_id(0)
    core, plane = lax.bitwise_and(where_ref[0], 1), where_ref[1]
    block = g0.shape[0]
    span = c0.shape[0]

    @pl.when(step == 0)
    def _():
        for o, w in enumerate((g0, g1, g2, g3)):
            weight_ref[o * block : (o + 1) * block, :] = w[...]
        for o, part in enumerate((p0, p1, p2, p3)):
            place_rows(out_ref, part, borrowed_ref, o, core, lax.bitwise_and(plane - o + 4, 3))

    parts = (c0, c1, c2, c3, c4, c5, c6, c7)
    for half in range(4):

        @pl.when(step == half)
        def _(half=half):
            for i in range(2):
                cot_ref[i * span : (i + 1) * span, :] = parts[2 * half + i][...]

    gate = mm(normed_ref[...], weight_ref[...])
    gate_ref[...] = gate
    gated = ssm_ref[...] * (gate * jax.nn.sigmoid(gate))
    gain = rows_ref[0:1, :]
    ngate = mm(cot_ref[...], out_ref[...], ((1,), (1,))) * gain
    ngate_ref[...] = ngate
    squares, cross = gated * gated, ngate * gated
    for i in range(2):
        rows = slice(i * span, (i + 1) * span)
        sums = []
        for product in (squares[rows], cross[rows]):
            folded = product[:, :LANES] + product[:, LANES : 2 * LANES] + product[:, 2 * LANES :]
            sums.append(jnp.sum(folded.T, axis=0, keepdims=True))
        row = iota((8, LANES), 0)
        sums_ref[span_at(2 * step + i, where_ref[0])] = jnp.where(row == 0, sums[0], sums[1])
    gated_ref[...] = (gated * gain).astype(bf16)


def out_part_kernel(where_ref, gated_ref, out_ref, mine_ref, other_ref):
    step = pl.program_id(0)
    part = mm(gated_ref[...], out_ref[...]).astype(bf16)

    @pl.when(step < 2)
    def _():
        mine_ref[...] = part

    @pl.when(step >= 2)
    def _():
        other_ref[...] = part


def gate_back_kernel(
    where_ref, sums_ref, ssm_ref, gate_ref, ngate_ref, rows_ref,
    grad_ref, grad_gate_ref, projected_ref, lent_ref, *, inner, third,
):
    step = pl.program_id(0)
    rows, own = ssm_ref.shape
    core = lax.bitwise_and(where_ref[0], 1)
    lent_ref[...] = jnp.zeros_like(lent_ref)
    span = LANES
    for i in range(rows // span):
        at = slice(i * span, (i + 1) * span)
        sums = sums_ref[span_at(rows // span * step + i, where_ref[0])]
        sums = jnp.concatenate([sums, jnp.zeros((LANES - 8, LANES), f32)], axis=0).T
        inv_gate = lax.rsqrt(sums[:, 0:1] / inner + norm_epsilon)
        mean = inv_gate * sums[:, 1:2] / inner
        inv_gate = jnp.broadcast_to(inv_gate, (span, own))
        ssm, gate = ssm_ref[at], gate_ref[at]
        logistic = jax.nn.sigmoid(gate)
        silu = gate * logistic
        normed = ssm * silu * inv_gate
        grad_gated = inv_gate * (ngate_ref[at] - normed * mean)
        grad_ref[at] = grad_gated * silu
        slope = logistic * (1.0 + gate * (1.0 - logistic))
        grad_gate_ref[at] = (grad_gated * ssm * slope).astype(bf16)
        projected_ref[at] = (normed * rows_ref[0:1, :]).astype(bf16)
    for k in range(2):

        @pl.when(core == k)
        def _(k=k):
            for plane, first, _, count in local_slices(k, 2 * third):
                if count == 4 * third:
                    source = first + 3 * third if k == 0 else first
                    to = plane // 2 * third
                    lent_ref[:, to : to + third] = projected_ref[:, source : source + third]


def gate_grad_kernel(where_ref, normed_ref, grad_gate_ref, b0, b1, b2, b3):
    total = mm(normed_ref[...], grad_gate_ref[...], ((0,), (0,))).astype(bf16)
    for o, out_ref in enumerate((b0, b1, b2, b3)):

        @pl.when(pl.program_id(0) == o)
        def _(out_ref=out_ref):
            out_ref[...] = total


def out_grad_kernel(
    where_ref, projected_ref, borrowed_ref, cot_ref, b0, b1, b2, b3, rows_ref, total_ref, *, third,
):
    step = pl.program_id(0)
    core, plane = lax.bitwise_and(where_ref[0], 1), where_ref[1]
    rows = 3 * third
    block = b0.shape[1]
    for k in range(2):

        @pl.when(core == k)
        def _(k=k):
            for at_plane, at, _, count in local_slices(k, 2 * third):
                to = at_plane * rows
                lent = slice(at_plane // 2 * third, (at_plane // 2 + 1) * third)
                if count == rows + third:
                    own_at = at if k == 0 else at + third
                    rows_ref[:, to : to + rows] = projected_ref[:, own_at : own_at + rows]
                elif k == 0:
                    rows_ref[:, to : to + count] = projected_ref[:, at : at + count]
                    rows_ref[:, to + count : to + rows] = borrowed_ref[:, lent]
                else:
                    rows_ref[:, to + third : to + rows] = projected_ref[:, at : at + count]
                    rows_ref[:, to : to + third] = borrowed_ref[:, lent]

    total = mm(rows_ref[...], cot_ref[...], ((0,), (0,)))

    @pl.when(step == 0)
    def _():
        total_ref[...] = total

    @pl.when(step == 1)
    def _():
        total_ref[...] += total
        for o, out_ref in enumerate((b0, b1, b2, b3)):
            first = pl.multiple_of(rows * lax.bitwise_and(plane - o + 4, 3), third)
            for g in range(4):
                own = total_ref[pl.ds(first, rows), g * block : (g + 1) * block]
                out_ref[g * rows : (g + 1) * rows, :] = own.astype(bf16)


def backward_kernel(
    where_ref, grad_ref, inter_ref, state_ref, conv_ref, pre_ref, mixed_ref, raw_ref,
    taps_ref, heads_ref, rows_ref,
    grad_pre_ref, grad_taps_ref, grad_heads_ref,
    ext, grad_state, next_state, *, n_taps, head_width, states,
):
    span, own = grad_ref.shape[1:]

    @pl.when(pl.program_id(0) == 0)
    def _():
        ext[span : span + 8, :] = jnp.zeros((8, ext.shape[1]), f32)
        grad_state[...] = jnp.zeros_like(grad_state)
        next_state[...] = jnp.zeros_like(next_state)
        grad_taps_ref[...] = jnp.zeros_like(grad_taps_ref)
        grad_heads_ref[...] = jnp.zeros_like(grad_heads_ref)

    key, query = conv_ref[0, :, own : own + states], conv_ref[0, :, own + states :]
    rate = heads_ref[1:2, :]
    raw = raw_ref[0] + heads_ref[0:1, :]
    step, cum = step_tables(raw, rate)
    cum_t, step_t = cum.T, step.T
    tail = jnp.exp(cum[span - 1 : span, :] - cum)
    affinity = mm(query, key, ((1,), (1,)))
    causal = iota((span, span), 0) >= iota((span, span), 1)
    after = grad_state[...]
    after_halves = stacked_halves(after)
    grad_weighted = mm(twice(key), after_halves)
    grad_affinity = jnp.zeros((span, span), f32)
    direct_t = jnp.zeros((span, span), f32)
    grad_cum = jnp.zeros((span, LANES), f32)
    row, lane = iota((span, span), 0), iota((span, LANES), 1)
    weighted, grown, grown_rest, kept = [], [], [], []
    products = [[], [], []]
    mixed = mixed_ref[0]
    logistic = jax.nn.sigmoid(mixed)
    slope = logistic * (1.0 + mixed * (1.0 - logistic))
    for pair in range(own // (2 * head_width)):
        lanes = slice(2 * pair * head_width, 2 * (pair + 1) * head_width)
        value, grad_y = conv_ref[0, :, lanes], grad_ref[0, :, lanes]
        value_f, grad_low = value.astype(f32), grad_y.astype(bf16)
        cum_pair = by_pair_lanes(cum, pair, head_width)
        growth = jnp.exp(cum_pair)
        tailed = jnp.exp(cum_pair[span - 1 : span, :] - cum_pair) * by_pair_lanes(step, pair, head_width)
        kept.append(growth[span - 1 : span, :])
        high, low = halves(grad_y * growth)
        grown.append(high)
        grown_rest.append(low)
        weighted.append((tailed * value_f).astype(bf16))
        grad_mixing = mm(grad_low, pair_masked(value, head_width), ((1,), (1,)))
        mixing = []
        for i in (0, 1):
            h = 2 * pair + i
            given = grad_mixing[:, i * span : (i + 1) * span]
            decay = jnp.exp(jnp.where(causal, cum[:, h : h + 1] - cum_t[h : h + 1, :], -1e30))
            grad_affinity = grad_affinity + given * decay * step_t[h : h + 1, :]
            table = affinity * decay
            scores = table * step_t[h : h + 1, :]
            mixing.append(scores.astype(bf16))
            direct_t = jnp.where(row == h, jnp.sum(given * table, axis=0, keepdims=True), direct_t)
            grad_cum = jnp.where(lane == h, jnp.sum(given * scores, axis=1, keepdims=True), grad_cum)
        grad_value = mm(jnp.concatenate(mixing, axis=0), pair_masked(grad_low, head_width), ((0,), (0,)))
        by_state = grad_weighted[:, lanes]
        grad_value = grad_value + tailed * by_state + rows_ref[1:2, lanes] * grad_y
        ext[0:span, lanes] = grad_value * slope[:, lanes]
        products[0].append(by_state * value_f)
        products[1].append(grad_y * inter_ref[0, :, lanes])
        products[2].append(jnp.sum(grad_y * value_f, axis=0, keepdims=True))
    weighted, grown = jnp.concatenate(weighted, axis=1), jnp.concatenate(grown, axis=1)
    grown_rest, kept = jnp.concatenate(grown_rest, axis=1), jnp.concatenate(kept, axis=1)
    grad_affinity = grad_affinity.astype(bf16)
    grad_query = mm(grown, state_ref[0].astype(bf16), ((1,), (1,))) + mm(grad_affinity, key)
    grad_key = mm(weighted, after_halves[:states], ((1,), (1,))) + mm(grad_affinity, query, ((0,), (0,)))
    ext[0:span, own : own + states] = grad_key * slope[:, own : own + states]
    ext[0:span, own + states :] = grad_query * slope[:, own + states :]
    to_lanes = head_map(own, head_width).astype(bf16)
    last = jnp.sum(after * next_state[...], axis=0, keepdims=True)
    by_head = jnp.concatenate(
        [
            jnp.concatenate(products[0], axis=1),
            jnp.concatenate(products[1], axis=1),
            jnp.broadcast_to(jnp.concatenate(products[2], axis=1), (8, own)),
            jnp.broadcast_to(last, (8, own)),
        ],
        axis=0,
    )
    high, low = halves(by_head)
    by_head = mm(high, to_lanes, ((1,), (1,))) + mm(low, to_lanes, ((1,), (1,)))
    direct = direct_t.T + by_head[:span] * tail
    grad_cum = grad_cum + by_head[span : 2 * span] - step * direct
    last = by_head[2 * span + 8 : 2 * span + 9]
    grad_cum = grad_cum + jnp.where(iota(grad_cum.shape, 0) == span - 1, last, 0.0)
    grad_log = triangle_sum(iota((span, span), 0) <= iota((span, span), 1), grad_cum)
    grad_raw = (direct + grad_log * rate) * jax.nn.sigmoid(raw)
    grad_heads_ref[0:1, :] += jnp.sum(grad_raw, axis=0, keepdims=True)
    grad_heads_ref[1:2, :] += jnp.sum(grad_log * step, axis=0, keepdims=True) * rate
    grad_heads_ref[2:3, :] += by_head[2 * span : 2 * span + 1]
    pre = pre_ref[0].astype(f32)
    grad_pre = jnp.zeros(pre.shape, f32)
    for k in range(n_taps):
        ahead = ext[n_taps - 1 - k : n_taps - 1 - k + span, :]
        grad_pre = grad_pre + ahead * taps_ref[k : k + 1, :]
        grad_taps_ref[k : k + 1, :] += jnp.sum(ahead * pre, axis=0, keepdims=True)
    grad_taps_ref[n_taps : n_taps + 1, :] += jnp.sum(ext[0:span, :], axis=0, keepdims=True)
    ext[span : span + 8, :] = ext[0:8, :]
    grad_pre_ref[0, :, : own + 2 * states] = grad_pre.astype(bf16)
    grad_pre_ref[0, :, own + 2 * states :] = grad_raw.astype(bf16)
    grad_state[...] = kept * after + mm(
        jnp.concatenate([query, query], axis=0), jnp.concatenate([grown, grown_rest], axis=0), ((0,), (0,))
    )
    next_state[...] = state_ref[0]


def input_grad_kernel(gate_ref, rest_ref, w_gate_ref, w_rest_ref, mine_ref, other_ref):
    half = mine_ref.shape[0]
    total = mm(gate_ref[...], w_gate_ref[...], ((1,), (1,))) + mm(rest_ref[...], w_rest_ref[...], ((1,), (1,)))
    mine_ref[...] = total[:half].astype(bf16)
    other_ref[...] = total[half:].astype(bf16)


def input_grad_call(gate, rest, w_gate, w_rest):
    half, width, block = gate.shape[0] // 2, w_gate.shape[0], w_gate.shape[0] // 3
    return pl.pallas_call(
        input_grad_kernel,
        out_shape=[jax.ShapeDtypeStruct((half, width), bf16)] * 2,
        grid=(3,),
        in_specs=[pl.BlockSpec(a.shape, lambda i: (0, 0)) for a in (gate, rest)]
        + [pl.BlockSpec((block, a.shape[1]), lambda i: (i, 0)) for a in (w_gate, w_rest)],
        out_specs=[pl.BlockSpec((half, block), lambda i: (0, i))] * 2,
        compiler_params=grant,
    )(gate, rest, w_gate, w_rest)


def by_span(shape, order):
    return pl.BlockSpec((1, *shape), lambda i, where: (order(i, where), 0, 0))


def spans_call(kernel, where, spans, inputs, outputs, scratch=()):
    in_specs = [
        by_span(a.shape[1:], order) if order else pl.BlockSpec(a.shape, lambda i, where, n=a.ndim: (0,) * n)
        for a, order in inputs
    ]
    out_specs = [
        by_span(shape, order) if order else pl.BlockSpec(shape, lambda i, where, n=len(shape): (0,) * n)
        for shape, _, order in outputs
    ]
    out_shape = [
        jax.ShapeDtypeStruct(
            (spans, *shape) if order else shape, dtype
        )
        for shape, dtype, order in outputs
    ]
    return pl.pallas_call(
        kernel,
        out_shape=out_shape,
        grid_spec=pltpu.PrefetchScalarGridSpec(
            num_scalar_prefetch=1,
            grid=(spans,),
            in_specs=in_specs,
            out_specs=out_specs,
            scratch_shapes=list(scratch),
        ),
        compiler_params=grant,
    )(where, *[a for a, _ in inputs])


def in_time(i, where):
    return i


def in_reverse(i, where):
    return 7 - i


def relative(i, where):
    return place(i, where[0])


def relative_reverse(i, where):
    return place(7 - i, where[0])


class Columns(typing.NamedTuple):
    shape: tuple
    first: int = 0


def rows_call(kernel, where, steps, rows, inputs, outputs, scratch=(), params=grant):
    def spec(shape, index):
        if isinstance(index, Columns):
            return pl.BlockSpec(index.shape, lambda i, where: (0, index.first + i))
        if index is None:
            return pl.BlockSpec(shape, lambda i, where, n=len(shape): (0,) * n)
        return pl.BlockSpec((rows, *shape[1:]), lambda i, where: (index(i), 0))

    return pl.pallas_call(
        kernel,
        out_shape=[jax.ShapeDtypeStruct(shape, dtype) for shape, dtype, _ in outputs],
        grid_spec=pltpu.PrefetchScalarGridSpec(
            num_scalar_prefetch=1,
            grid=(steps,),
            in_specs=[spec(a.shape, index) for a, index in inputs],
            out_specs=[spec(shape, index) for shape, _, index in outputs],
            scratch_shapes=list(scratch),
        ),
        compiler_params=params,
    )(where, *[a for a, _ in inputs])


def each(i):
    return i


def halves_swapped(i):
    return 1 - i


def lower(i):
    return lax.min(i, 1)


def upper(i):
    return lax.max(i - 2, 0)


def local_slices(core, width):
    at, slices = 0, []
    for plane in range(4):
        count = 2 * width if plane % 2 == core else width
        slices.append((plane, at, 0 if core == 0 else 3 * width - count, count))
        at += count
    return slices


def pack_kernel(
    gate_ref, conv_ref, step_ref, norm_ref, gain_ref, bias_ref, taps_ref,
    cols_ref, message_ref, *, head_width,
):
    inner = gate_ref.shape[1]
    group = 3 * head_width
    for chip in range(4):
        for core in range(2):
            for plane, at, start, count in local_slices(core, head_width):
                source = group * (4 * plane + chip) + start
                for first, ref in ((0, conv_ref), (cols_ref.shape[2] // 2, gate_ref)):
                    to = slice(first + at, first + at + count)
                    cols_ref[2 * chip + core, :, to] = ref[:, source : source + count]
    rest = conv_ref.shape[1] - inner
    rows = gate_ref.shape[0]
    message_ref[...] = jnp.zeros_like(message_ref)
    message_ref[:rows, :rest] = conv_ref[:, inner:]
    message_ref[:rows, rest : rest + step_ref.shape[1]] = step_ref[...]
    vectors = jnp.zeros((8, LANES), f32)

    def put(vectors, ref, at):
        value = ref[...].astype(f32)
        value = jnp.pad(value, ((at, 8 - at - value.shape[0]), (0, LANES - value.shape[1])))
        return vectors + value

    for ref, at in ((norm_ref, 0), (gain_ref, 1), (bias_ref, 2), (taps_ref, 3)):
        vectors = put(vectors, ref, at)
    message_ref[rows:, :LANES] = vectors.astype(bf16)


def setup_kernel(
    where_ref, mine_ref, other_ref, heads_ref,
    shared_ref, norm_ref, taps_ref, channels_ref, head_rows_ref, pick_ref,
    gain_all, taps_all, held, *, n_taps, head_width,
):
    rank, plane = where_ref[0], where_ref[1]
    padded = shared_ref.shape[1]
    rows = norm_ref.shape[1] // 32
    block = 8 * rows
    rows_in, rows_out = norm_ref.shape[1] // 32, gain_all.shape[1] // 32
    piece = taps_all.shape[1] // 32
    inner = gain_all.shape[1]
    own = channels_ref.shape[1]
    for p in range(8):
        source = lax.bitwise_xor(rank, 2 * (p % 4) + p // 4)
        part_ref, top = (mine_ref, other_ref)[p // 4], p % 4 * (rows + 8)
        for o in range(4):
            at = pl.multiple_of(o * block + source * rows, 16)
            lanes = slice(o * padded, (o + 1) * padded)
            shared_ref[pl.ds(at, rows), :] = part_ref[top : top + rows, lanes]
            device = 8 * lax.bitwise_and(plane - o + 4, 3) + source
            held[device] = part_ref[top + rows : top + rows + 8, o * padded : o * padded + LANES].astype(f32)
    for i in range(32):
        vectors = held[i]
        norm_ref[:, i * rows_in : (i + 1) * rows_in] = vectors[0:1, :rows_in]
        gain_all[:, i * rows_out : (i + 1) * rows_out] = vectors[1:2, :rows_out]
        taps_all[:, i * piece : (i + 1) * piece] = vectors[:, :piece]
    taps_ref[...] = jnp.zeros_like(taps_ref)
    channels_ref[...] = jnp.zeros_like(channels_ref)
    taps_ref[0:n_taps, own:] = taps_all[3 : 3 + n_taps, inner:]
    taps_ref[n_taps : n_taps + 1, own:] = taps_all[2:3, inner:]
    for r in range(8):

        @pl.when(rank == r)
        def _(r=r):
            chip, core = r // 2, r % 2
            local, heads = iota((LANES, LANES), 0), iota((LANES, LANES), 1)
            chosen = jnp.zeros((LANES, LANES), jnp.bool_)
            for plane, at, start, count in local_slices(core, head_width):
                source = 3 * head_width * (4 * plane + chip) + start
                taps_ref[0:n_taps, at : at + count] = taps_all[3 : 3 + n_taps, source : source + count]
                taps_ref[n_taps : n_taps + 1, at : at + count] = taps_all[2:3, source : source + count]
                channels_ref[0:1, at : at + count] = gain_all[:, source : source + count]
                for j in range(count // head_width):
                    chosen |= (local == at // head_width + j) & (heads == source // head_width + j)
            pick_ref[...] = chosen.astype(f32)

    states = (padded - LANES) // 2
    chosen = pick_ref[...].astype(bf16)
    shared_ref[:, 2 * states :] = mm(shared_ref[:, 2 * states :], chosen, ((1,), (1,))).astype(bf16)
    head_rows = mm_exact(heads_ref[...], pick_ref[...], ((1,), (1,)))
    used = iota((1, LANES), 1) < own // head_width
    head_rows_ref[...] = jnp.zeros_like(head_rows_ref)
    head_rows_ref[0:1, :] = head_rows[0:1]
    head_rows_ref[1:2, :] = jnp.where(used, -jnp.exp(head_rows[1:2]), 0.0)
    channels_ref[1:2, :] = mm_exact(head_rows, head_map(own, head_width))[2:3]


def lend_kernel(where_ref, p0, p1, p2, p3, out_ref):
    core = lax.bitwise_and(where_ref[0], 1)
    third = out_ref.shape[1]
    for o, part in enumerate((p0, p1, p2, p3)):
        for k in range(2):

            @pl.when(core == k)
            def _(o=o, part=part, k=k):
                out_ref[o] = part[2 * third :, :] if k == 0 else part[:third, :]


def place_rows(out_ref, part_ref, borrowed_ref, o, core, at_plane):
    rows = part_ref.shape[0]
    third = rows // 3
    for k in range(2):
        for slices_plane, at, _, count in local_slices(k, 2 * third):

            @pl.when((core == k) & (at_plane == slices_plane))
            def _(k=k, at=at, count=count):
                if count == rows + third and k == 0:
                    out_ref[at : at + rows, :] = part_ref[...]
                    out_ref[at + rows : at + count, :] = borrowed_ref[o]
                elif count == rows + third:
                    out_ref[at : at + third, :] = borrowed_ref[o]
                    out_ref[at + third : at + count, :] = part_ref[...]
                elif k == 0:
                    out_ref[at : at + count, :] = part_ref[: 2 * third, :]
                else:
                    out_ref[at : at + count, :] = part_ref[third:, :]


def total_of(refs, rows=slice(None)):
    total = refs[0][rows].astype(f32)
    for ref in refs[1:]:
        total = total + ref[rows].astype(f32)
    return total


def as_row(column, count):
    return jnp.broadcast_to(column, (column.shape[0], LANES)).T[:1, :count]


def early_rows_kernel(p0, p1, p2, w_ref, gain_ref, out_ref, dot_ref):
    rows = out_ref.shape[0]
    block = p0.shape[1]
    for g in range(4):
        at = slice(g * rows, (g + 1) * rows)
        out_ref[:, g * block : (g + 1) * block] = total_of((p0, p1, p2), at)
    dot = jnp.sum(w_ref[...].astype(f32) * out_ref[...], axis=1, keepdims=True)
    dot_ref[...] = as_row(dot, rows) / gain_ref[...].astype(f32)


def late_rows_kernel(g0, g1, g2, c0, c1, c2, out_ref):
    own = g0.shape[1]
    rows = out_ref.shape[1]
    for r in range(8):
        at = slice(r * rows, (r + 1) * rows)
        out_ref[r, :, :own] = total_of((g0, g1, g2), at).astype(bf16)
        out_ref[r, :, own:] = total_of((c0, c1, c2), at).astype(bf16)


def columns_kernel(
    table_ref, w_gate_ref, w_conv_ref, w_step_ref, gain_ref, s0, s1, s2, s3,
    gate_ref, conv_ref, dot_ref, step_ref, taps_ref, bias_ref, step_bias_ref, decay_ref, skip_ref, *, head_width,
):
    group = 3 * head_width
    inner = 16 * group
    half = table_ref.shape[2] // 2
    for chip in range(4):
        for core in range(2):
            for plane, at, start, count in local_slices(core, head_width):
                to = slice(group * (4 * plane + chip) + start, group * (4 * plane + chip) + start + count)
                gate_ref[:, to] = table_ref[2 * chip + core, :, at : at + count].astype(f32)
                conv_ref[:, to] = table_ref[2 * chip + core, :, half + at : half + at + count].astype(f32)
    rows = gate_ref.shape[0]
    rest = conv_ref.shape[1] - inner
    shared = total_of((s0, s1, s2, s3))
    conv_ref[:, inner:] = shared[:rows, :rest]
    step_ref[...] = shared[:rows, rest : rest + step_ref.shape[1]]
    small = shared[rows:, :LANES] + shared[rows:, LANES : 2 * LANES]
    at = 0
    for ref in (taps_ref, bias_ref, step_bias_ref, decay_ref, skip_ref):
        ref[...] = small[at : at + ref.shape[0], : ref.shape[1]]
        at += ref.shape[0]
    total = jnp.sum(w_step_ref[...].astype(f32) * step_ref[...], axis=1, keepdims=True)
    for weight_ref, grad_ref in ((w_gate_ref, gate_ref), (w_conv_ref, conv_ref)):
        total = total + jnp.sum(weight_ref[...].astype(f32) * grad_ref[...], axis=1, keepdims=True)
    dot_ref[...] = as_row(total, rows) / gain_ref[...].astype(f32)


def tokens_out_kernel(
    where_ref, o0, o1, o2, o3, g0, g1, g2, g3, hidden_ref, cot_ref, sums_ref, norm_ref,
    output_ref, grad_ref, held, *, inner,
):
    rank, plane = where_ref[0], where_ref[1]
    tokens = hidden_ref[...].astype(f32)
    sums = jnp.concatenate([sums_ref[rank], jnp.zeros((LANES - 8, LANES), f32)], axis=0).T
    inv_gate = lax.rsqrt(sums[:, 0:1] / inner + norm_epsilon)
    output_ref[...] = (tokens + inv_gate * total_of((o0, o1, o2, o3))).astype(bf16)
    inv_rms = lax.rsqrt(jnp.mean(tokens * tokens, axis=1, keepdims=True) + norm_epsilon)
    width = tokens.shape[1]
    block = width // 4
    grad_ref[...] = total_of((g0, g1, g2, g3))
    for p in range(4):
        at = pl.multiple_of(block * lax.bitwise_and(plane - p + 4, 3), LANES)
        lanes = slice(p * block, (p + 1) * block)
        held[:, lanes] = grad_ref[:, pl.ds(at, block)] * norm_ref[:, lanes]
    grad_unit, unit = held[...], tokens * inv_rms
    mean = jnp.mean(grad_unit * unit, axis=1, keepdims=True)
    grad_ref[...] = cot_ref[...].astype(f32) + inv_rms * (grad_unit - unit * mean)


def once(kernel, inputs, outputs, where=None, scratch=(), params=grant):
    specs = lambda shapes: [pl.BlockSpec(s, lambda *_, n=len(s): (0,) * n) for s in shapes]
    out_shape = [jax.ShapeDtypeStruct(shape, dtype) for shape, dtype in outputs]
    grid_spec = pltpu.PrefetchScalarGridSpec(
        num_scalar_prefetch=0 if where is None else 1,
        grid=(1,),
        in_specs=specs([a.shape for a in inputs]),
        out_specs=specs([shape for shape, _ in outputs]),
        scratch_shapes=list(scratch),
    )
    call = pl.pallas_call(kernel, out_shape=out_shape, grid_spec=grid_spec, compiler_params=params)
    return call(*([] if where is None else [where]), *inputs)


def hop(value, distance):
    count = lax.axis_size("seq")
    pairs = [(i, i ^ distance) for i in range(count)]
    return lax.ppermute(value, "seq", pairs)


def plane_hop(value, distance):
    count = lax.axis_size("batch")
    pairs = [(i, (i + distance) % count) for i in range(count)]
    return lax.ppermute(value, "batch", pairs)


def planes_gather(value, direct=False):
    one, three = plane_hop(value, 1), plane_hop(value, -1)
    two = plane_hop(value, 2) if direct else plane_hop(one, 1)
    return [value, one, two, three]


def planes_parts(blocks):
    near, far = plane_hop(blocks[1], -1), plane_hop(blocks[2], 1)
    sent = (blocks[3].astype(f32) + far.astype(f32)).astype(blocks[3].dtype)
    return [blocks[0], near, plane_hop(sent, 1)]


def planes_direct(blocks):
    return [blocks[0]] + [plane_hop(blocks[o], -o) for o in (1, 2, 3)]


def plane_gather(value):
    chips = [value] + [hop(value, distance) for distance in (2, 4, 6)]
    return chips + [hop(part, 1) for part in chips]


def small_gather(value):
    parts = [value] + [hop(value, distance) for distance in (2, 4, 6)]
    mine = jnp.concatenate(parts)
    return mine, hop(mine, 1)


def plane_parts(mine, other):
    count = mine.shape[0] // 4
    other = hop(other, 1)
    half = []
    for j in range(4):
        rows = slice(j * count, (j + 1) * count)
        half.append((mine[rows].astype(f32) + other[rows].astype(f32)).astype(bf16))
    return half[:1] + [hop(half[j], 2 * j) for j in (1, 2, 3)]


def plane_total(value):
    value = value + hop(value, 1)
    return value + hop(value, 2) + hop(value, 4) + hop(value, 6)


def local_group(index, core, width):
    plane, at = jnp.zeros_like(index), jnp.zeros_like(index)
    for k in range(2):
        for slices_plane, first, start, count in local_slices(k, width):
            inside = (core == k) & (index >= first) & (index < first + count)
            plane = jnp.where(inside, slices_plane, plane)
            at = jnp.where(inside, index - first + start, at)
    return plane, at


def shared_back_kernel(where_ref, rows_ref, taps_ref, heads_ref, pick_ref, mine_ref, other_ref, *, head_width, piece):
    rank, plane = where_ref[0], where_ref[1]
    rows = mine_ref.shape[2] - 8
    local = taps_ref.shape[1]
    own = 6 * head_width
    inner = 8 * own
    core, chip = lax.bitwise_and(rank, 1), lax.shift_right_logical(rank, 1)
    at = iota((local, LANES), 0)
    at_plane, offset = local_group(at, core, head_width)
    column = jnp.where(at < own, 3 * head_width * (4 * at_plane + chip) + offset, inner + at - own)
    heads = mm_exact(heads_ref[...], pick_ref[...])
    heads = jnp.concatenate([jnp.zeros((5, LANES), f32), heads[:3]], axis=0)
    high, low = halves(taps_ref[...])
    both = jnp.concatenate([high, low], axis=0)
    target = LANES * (column // piece) + column % piece - iota((local, LANES), 1)
    head_halves = halves(heads)
    for o in range(4):
        first = 8 * lax.bitwise_and(plane - o + 4, 3)
        for p in range(8):
            r = lax.bitwise_xor(rank, 2 * (p % 4) + p // 4)
            out_ref, q = (mine_ref, other_ref)[p // 4], p % 4
            chosen = (target == LANES * (first + r)).astype(bf16)
            spread = mm(both, chosen)
            own_rows = rows_ref[pl.ds(pl.multiple_of((8 * o + r) * rows, 16), rows), :]
            out_ref[q, o, :rows, : 2 * LANES] = own_rows[:, : 2 * LANES]
            out_ref[q, o, :rows, 2 * LANES :] = mm(own_rows[:, 2 * LANES :], pick_ref[...].astype(bf16)).astype(bf16)
            for half in (0, 1):
                value = spread[8 * half : 8 * half + 8].astype(bf16) + head_halves[half]
                out_ref[q, o, rows:, half * LANES : (half + 1) * LANES] = value
            out_ref[q, o, rows:, 2 * LANES :] = jnp.zeros((8, out_ref.shape[3] - 2 * LANES), bf16)


def split_local(
    hidden,
    norm_gain,
    w_gate_in,
    w_conv_in,
    w_step,
    conv_weight,
    conv_bias,
    step_bias,
    decay_log,
    skip_gain,
    gate_gain,
    w_out,
    cotangent,
):
    plane, rank = lax.axis_index("batch"), lax.axis_index("seq")
    planes, ranks = lax.axis_size("batch"), lax.axis_size("seq")
    _, span, width = hidden.shape
    rows_in, inner = w_gate_in.shape
    channels = w_conv_in.shape[1]
    heads = w_step.shape[1]
    head_width = inner // heads
    states = (channels - inner) // 2
    taps = conv_weight.shape[0]
    own = inner // ranks
    rows_out = w_out.shape[0]
    tokens = ranks * span
    block = width // planes
    piece = conv_bias.shape[0]
    devices = planes * ranks
    padded = -(-(2 * states + heads) // LANES) * LANES
    local = own + 2 * states
    third = rows_out // 3
    fixed = None
    where = jnp.stack([rank, plane]).astype(jnp.int32)

    out_parts = planes_gather(w_out)
    cols, message = once(
        functools.partial(pack_kernel, head_width=head_width),
        [w_gate_in, w_conv_in, w_step, norm_gain[None], gate_gain[None], conv_bias[None], conv_weight],
        [((ranks, rows_in, 2 * own), bf16), ((rows_in + 8, padded), bf16)],
        params=whole_grant,
    )
    cols = lax.all_to_all(cols, "seq", 0, 0).reshape(ranks * rows_in, 2 * own)
    message = planes_gather(message, True)
    message = jnp.concatenate(message, axis=1)
    tokens_rel, cot_rel = plane_gather(hidden[0]), plane_gather(cotangent[0])
    shared_mine, shared_other = small_gather(message)
    conv_cols, gate_cols = cols[:, :own], cols[:, own:]
    conv_w, gate_w = planes_gather(conv_cols), planes_gather(gate_cols)
    head_values = jnp.pad(jnp.stack([step_bias, decay_log, skip_gain]), ((0, 5), (0, LANES - heads)))
    shared_w, norm_full, taps_rows, channel_rows, head_rows, head_table = rows_call(
        functools.partial(setup_kernel, n_taps=taps, head_width=head_width),
        where,
        1,
        None,
        [(a, fixed) for a in (shared_mine, shared_other, head_values)],
        [
            ((width, padded), bf16, fixed),
            ((1, width), f32, fixed),
            ((8, local), f32, fixed),
            ((8, own), f32, fixed),
            ((8, LANES), f32, fixed),
            ((LANES, LANES), f32, fixed),
        ],
        [
            pltpu.VMEM((1, inner), f32),
            pltpu.VMEM((8, channels), f32),
            pltpu.VMEM((devices, 8, LANES), f32),
        ],
    )
    (lent_rows,) = once(lend_kernel, out_parts, [((planes, third, width), bf16)], where)
    out_borrowed = hop(lent_rows, 1)

    sizes = dict(n_taps=taps, head_width=head_width, states=states)
    rows = tokens // 4
    normed, pre, raw, rest_w = rows_call(
        functools.partial(project_kernel, states=states),
        where,
        4,
        rows,
        [(a, fixed) for a in (*tokens_rel, norm_full, *conv_w, shared_w)],
        [
            ((tokens, width), bf16, each),
            ((tokens, local), bf16, each),
            ((tokens, LANES), f32, each),
            ((width, own + padded), bf16, fixed),
        ],
        params=wide_grant,
    )
    pre, raw = pre.reshape(ranks, span, local), raw.reshape(ranks, span, LANES)
    mixed, conv, inter, ssm, entering = spans_call(
        functools.partial(forward_kernel, **sizes),
        where,
        ranks,
        [(pre, relative), (raw, relative)]
        + [(a, fixed) for a in (taps_rows, head_rows, channel_rows)],
        [
            ((span, local), f32, in_time),
            ((span, local), bf16, in_time),
            ((span, own), f32, in_time),
            ((span, own), f32, relative),
            ((states, own), f32, in_time),
        ],
        [pltpu.VMEM((span + 8, local), f32), pltpu.VMEM((states, own), f32)],
    )
    ssm = ssm.reshape(tokens, own)
    gate, ngate, sums, gated, gate_all, cot, out_w = rows_call(
        gate_kernel,
        where,
        4,
        rows,
        [(normed, each)]
        + [(a, fixed) for a in (*gate_w, *cot_rel, *out_parts, out_borrowed, channel_rows)]
        + [(ssm, each)],
        [
            ((tokens, own), f32, each),
            ((tokens, own), f32, each),
            ((ranks, 8, LANES), f32, fixed),
            ((tokens, own), bf16, each),
            ((width, own), bf16, fixed),
            ((tokens, width), bf16, each),
            ((own, width), bf16, fixed),
        ],
        params=wide_grant,
    )
    sums = plane_total(sums)
    part_mine, part_other = rows_call(
        out_part_kernel,
        where,
        4,
        rows,
        [(gated, each), (out_w, fixed)],
        [((tokens // 2, width), bf16, lower), ((tokens // 2, width), bf16, upper)],
    )
    out_own = plane_parts(part_mine, part_other)

    grad_y, grad_gate, projected, lent = rows_call(
        functools.partial(gate_back_kernel, inner=inner, third=third),
        where,
        4,
        rows,
        [(sums, fixed), (ssm, each), (gate, each), (ngate, each), (channel_rows, fixed)],
        [
            ((tokens, own), f32, each),
            ((tokens, own), bf16, each),
            ((tokens, own), bf16, each),
            ((tokens, LANES), bf16, each),
        ],
    )
    borrowed = hop(lent, 1)
    d_gate = rows_call(
        gate_grad_kernel,
        where,
        planes,
        None,
        [(normed, Columns((tokens, block))), (grad_gate, fixed)],
        [((block, own), bf16, fixed)] * 4,
    )
    d_gate = planes_parts(d_gate)
    d_out = rows_call(
        functools.partial(out_grad_kernel, third=third),
        where,
        2,
        tokens // 2,
        [(projected, each), (borrowed, halves_swapped), (cot, each)],
        [((4 * rows_out, block), bf16, fixed)] * 4,
        [pltpu.VMEM((tokens // 2, own), bf16), pltpu.VMEM((own, width), f32)],
    )
    d_out = planes_parts(d_out)
    grad_rest, grad_taps, grad_heads = spans_call(
        functools.partial(backward_kernel, **sizes),
        where,
        ranks,
        [(grad_y.reshape(ranks, span, own), relative_reverse)]
        + [(a, in_reverse) for a in (inter, entering, conv)]
        + [(pre, relative_reverse), (mixed, in_reverse), (raw, relative_reverse)]
        + [(a, fixed) for a in (taps_rows, head_rows, channel_rows)],
        [
            ((span, own + padded), bf16, relative_reverse),
            ((8, local), f32, fixed),
            ((8, LANES), f32, fixed),
        ],
        [
            pltpu.VMEM((span + 8, local), f32),
            pltpu.VMEM((states, own), f32),
            pltpu.VMEM((states, own), f32),
        ],
    )
    grad_rest = grad_rest.reshape(tokens, own + padded)
    d_rest = jnp.dot(normed.T, grad_rest, preferred_element_type=f32).astype(bf16)
    d_conv = planes_parts([d_rest[o * block : (o + 1) * block, :own] for o in range(planes)])
    d_shared = rows_call(
        functools.partial(shared_back_kernel, head_width=head_width, piece=piece),
        where,
        1,
        None,
        [(d_rest, Columns((width, padded), own // padded))]
        + [(a, fixed) for a in (grad_taps, grad_heads, head_table)],
        [((ranks // 2, planes, rows_in + 8, padded), bf16, fixed)] * 2,
    )
    gate_all, *d_shared = lax.optimization_barrier((gate_all, *d_shared))
    mine, other = input_grad_call(grad_gate, grad_rest, gate_all, rest_w)
    grad_own = plane_parts(mine, other)
    d_shared = [a.reshape(ranks // 2 * planes, rows_in + 8, padded) for a in d_shared]
    d_shared = plane_parts(d_shared[0], d_shared[1])
    d_shared = sum(part.astype(f32) for part in d_shared)
    d_shared = planes_direct([d_shared[o] for o in range(planes)])

    d_out, d_gain = once(
        early_rows_kernel,
        [*d_out, w_out, gate_gain[None]],
        [((rows_out, width), f32), ((1, rows_out), f32)],
    )
    (d_in,) = once(late_rows_kernel, [*d_gate, *d_conv], [((ranks, rows_in, 2 * own), bf16)])
    d_in = lax.all_to_all(d_in, "seq", 0, 0)
    output, grad_hidden = once(
        functools.partial(tokens_out_kernel, inner=inner),
        [*out_own, *grad_own, hidden[0], cotangent[0], sums, norm_full],
        [((span, width), bf16), ((span, width), f32)],
        where,
        [pltpu.VMEM((span, width), f32)],
        params=whole_grant,
    )
    d_gate, d_conv, d_norm, d_step, *small = once(
        functools.partial(columns_kernel, head_width=head_width),
        [d_in, w_gate_in, w_conv_in, w_step, norm_gain[None], *d_shared],
        [
            ((rows_in, inner), f32),
            ((rows_in, channels), f32),
            ((1, rows_in), f32),
            ((rows_in, heads), f32),
            ((taps, piece), f32),
            ((1, piece), f32),
            ((1, heads), f32),
            ((1, heads), f32),
            ((1, heads), f32),
        ],
    )
    return (
        output[None],
        grad_hidden[None],
        d_norm[0],
        d_gate,
        d_conv,
        d_step,
        small[0],
        small[1][0],
        small[2][0],
        small[3][0],
        small[4][0],
        d_gain[0],
        d_out,
    )


def split_block(*args):
    return split_local(*args)


def solution(mesh):
    split = (mesh.shape["batch"], mesh.shape["seq"]) == (4, 8)
    body = split_block if split else local
    return jax.shard_map(
        body,
        mesh=mesh,
        in_specs=(
            P("batch", "seq", None),
            P(("batch", "seq")),
            P(("batch", "seq"), None),
            P(("batch", "seq"), None),
            P(("batch", "seq"), None),
            P(None, ("batch", "seq")),
            P(("batch", "seq")),
            P(),
            P(),
            P(),
            P(("batch", "seq")),
            P(("batch", "seq"), None),
            P("batch", "seq", None),
        ),
        out_specs=(
            P("batch", "seq", None),
            P("batch", "seq", None),
            P(("batch", "seq")),
            P(("batch", "seq"), None),
            P(("batch", "seq"), None),
            P(("batch", "seq"), None),
            P(None, ("batch", "seq")),
            P(("batch", "seq")),
            P(),
            P(),
            P(),
            P(("batch", "seq")),
            P(("batch", "seq"), None),
        ),
        check_vma=False,
    )
```

```python
import functools
import typing

import jax
import jax.numpy as jnp
from jax import lax
from jax.experimental import pallas as pl
from jax.experimental.pallas import tpu as pltpu
from jax.sharding import PartitionSpec as P

norm_epsilon = 1e-05


def shifted(value, axis, steps):
    count = lax.axis_size(axis)
    first, last = (max(0, -steps), min(count, count - steps))
    return lax.ppermute(value, axis, [(source, source + steps) for source in range(first, last)])


def prefix(array, axis, combine, identity, reverse):
    devices, place = (lax.axis_size(axis), lax.axis_index(axis))
    everything = jax.tree.map(lambda part: lax.all_gather(part, axis), array)
    start = jax.tree.map(
        lambda part, zero: jnp.broadcast_to(jnp.asarray(zero, part.dtype), part.shape),
        array,
        identity,
    )

    def hop(k, before):
        at = devices - 1 - k if reverse else k
        reached = at > place if reverse else at < place
        new = combine(before, jax.tree.map(lambda part: part[at], everything))
        return jax.tree.map(lambda a, b: jnp.where(reached, a, b), new, before)

    return lax.fori_loop(0, devices, hop, start)


def for_sending(array):
    return jax.tree.map(lambda a: a.astype(jnp.bfloat16) if a.dtype == jnp.float32 else a, array)


def narrow_product(pattern, former, latter):
    return jnp.einsum(pattern, former, latter, preferred_element_type=jnp.float32)


def wide_product(pattern, former, latter):
    return jnp.einsum(pattern, former, latter, precision=lax.Precision.HIGHEST)


def silu_slope(inputs):
    logistic = jax.nn.sigmoid(inputs)
    return logistic * (1.0 + inputs * (1.0 - logistic))


def upper_table(length):
    rows = lax.broadcasted_iota(jnp.int32, (length, length), 0)
    cols = lax.broadcasted_iota(jnp.int32, (length, length), 1)
    return (rows <= cols).astype(jnp.float32)


def running_total(step_size, head_rate):
    table = upper_table(step_size.shape[0])
    return jnp.dot((step_size * head_rate[None, :]).T, table, precision=lax.Precision.HIGHEST)


def span_parts(value_b, key_b, query_b, step_size, head_rate):
    length = step_size.shape[0]
    cumulative = running_total(step_size, head_rate)
    row_index = lax.broadcasted_iota(jnp.int32, (1, length, length), 1)
    col_index = lax.broadcasted_iota(jnp.int32, (1, length, length), 2)
    causal = row_index >= col_index
    spread = cumulative[:, :, None] - cumulative[:, None, :]
    decays = jnp.where(causal, jnp.exp(jnp.where(causal, spread, 0.0)), 0.0)
    affinity = jnp.dot(query_b, key_b.T, preferred_element_type=jnp.float32)
    step_rows = step_size.T
    scores = affinity[None] * decays * step_rows[:, None, :]
    mixing = scores.astype(jnp.bfloat16)
    within = narrow_product("hts,shp->thp", mixing, value_b)
    tail_decay = jnp.exp(cumulative[:, -1:] - cumulative) * step_rows
    weighted = (tail_decay.T[:, :, None] * value_b.astype(jnp.float32)).astype(jnp.bfloat16)
    span_state = narrow_product("shp,sn->hpn", weighted, key_b)
    total_decay = jnp.exp(cumulative[:, -1])
    return (within, span_state, total_decay, cumulative, decays, affinity, scores, mixing, weighted)


def span_inter(query_b, cumulative, carried):
    base = wide_product("tn,hpn->thp", query_b.astype(jnp.float32), carried)
    return jnp.exp(cumulative).T[:, :, None] * base


def carried_grad(query_b, cumulative, grad_y):
    scaled = grad_y * jnp.exp(cumulative).T[:, :, None]
    return wide_product("thp,tn->hpn", scaled, query_b.astype(jnp.float32))


def span_backward(
    value_b, key_b, query_b, step_size, carried, grad_y, grad_state, grad_total, head_rate
):
    parts = span_parts(value_b, key_b, query_b, step_size, head_rate)
    total_decay, cumulative, decays, affinity, scores, mixing, weighted = parts[2:]
    length = step_size.shape[0]
    query_f = query_b.astype(jnp.float32)
    key_f = key_b.astype(jnp.float32)
    value_f = value_b.astype(jnp.float32)
    step_rows = step_size.T
    growth = jnp.exp(cumulative)
    base = wide_product("tn,hpn->thp", query_f, carried)
    grad_cumul = growth * jnp.sum(grad_y * base, axis=2).T
    grad_query = wide_product("thp,hpn->tn", grad_y * growth.T[:, :, None], carried)
    grad_low = grad_y.astype(jnp.bfloat16)
    grad_mixing = narrow_product("thp,shp->hts", grad_low, value_b)
    grad_value = narrow_product("hts,thp->shp", mixing, grad_low)
    grad_affinity = jnp.sum(grad_mixing * decays * step_rows[:, None, :], axis=0)
    grad_steps = jnp.sum(grad_mixing * affinity[None] * decays, axis=1)
    through = grad_mixing * scores
    grad_cumul = grad_cumul + jnp.sum(through, axis=2) - jnp.sum(through, axis=1)
    grad_query = grad_query + wide_product("ts,sn->tn", grad_affinity, key_f)
    grad_key = wide_product("ts,tn->sn", grad_affinity, query_f)
    grad_weighted = wide_product("hpn,sn->shp", grad_state, key_f)
    grad_key = grad_key + wide_product("shp,hpn->sn", weighted.astype(jnp.float32), grad_state)
    grad_end = jnp.sum(grad_weighted * value_f, axis=2).T
    tail_only = jnp.exp(cumulative[:, -1:] - cumulative)
    grad_value = grad_value + grad_weighted * (tail_only * step_rows).T[:, :, None]
    grad_steps = grad_steps + grad_end * tail_only
    push = grad_end * tail_only * step_rows
    last_flag = lax.broadcasted_iota(jnp.int32, (1, length), 1) == length - 1
    last_term = (jnp.sum(push, axis=1) + grad_total * total_decay)[:, None]
    grad_cumul = grad_cumul - push + jnp.where(last_flag, last_term, 0.0)
    grad_log = jnp.dot(grad_cumul, upper_table(length).T, precision=lax.Precision.HIGHEST)
    grad_steps = grad_steps + grad_log * head_rate[:, None]
    grad_rate = jnp.sum(grad_log * step_rows, axis=1)
    return (grad_value, grad_key, grad_query, grad_steps.T, grad_rate)


def conv_apply(padded, kernel_f, bias_f, length):
    time_axis = padded.ndim - 2
    total = bias_f
    for offset in range(kernel_f.shape[0]):
        total = total + kernel_f[offset] * lax.slice_in_dim(
            padded, offset, offset + length, axis=time_axis
        )
    return total


def conv_back(grad_mixed, padded, kernel_f):
    length = grad_mixed.shape[-2]
    kernel_taps = kernel_f.shape[0]
    time_axis = grad_mixed.ndim - 2
    leading = tuple(range(grad_mixed.ndim - 1))
    grad_kernel = jnp.stack(
        [
            jnp.sum(
                grad_mixed * lax.slice_in_dim(padded, offset, offset + length, axis=time_axis),
                axis=leading,
            )
            for offset in range(kernel_taps)
        ]
    )
    grad_padded = jnp.zeros(padded.shape, jnp.float32)
    for offset in range(kernel_taps):
        widths = [(0, 0)] * grad_mixed.ndim
        widths[time_axis] = (offset, kernel_taps - 1 - offset)
        grad_padded = grad_padded + jnp.pad(grad_mixed * kernel_f[offset], widths)
    return (grad_kernel, grad_padded)


def combine_states(earlier, later):
    return (earlier[0] * later[0], later[0][:, :, None, None] * earlier[1] + later[1])


def local(
    hidden,
    norm_gain,
    w_gate_in,
    w_conv_in,
    w_step,
    conv_weight,
    conv_bias,
    step_bias,
    decay_log,
    skip_gain,
    gate_gain,
    w_out,
    cotangent,
):
    seq_count, length, model_width = hidden.shape
    gathered = (
        lax.all_gather(norm_gain, ("batch", "seq"), axis=0, tiled=True),
        lax.all_gather(w_gate_in, ("batch", "seq"), axis=0, tiled=True),
        lax.all_gather(w_conv_in, ("batch", "seq"), axis=0, tiled=True),
        lax.all_gather(w_step, ("batch", "seq"), axis=0, tiled=True),
        lax.all_gather(conv_weight, ("batch", "seq"), axis=1, tiled=True),
        lax.all_gather(conv_bias, ("batch", "seq"), axis=0, tiled=True),
        lax.all_gather(gate_gain, ("batch", "seq"), axis=0, tiled=True),
        lax.all_gather(w_out, ("batch", "seq"), axis=0, tiled=True),
    )
    (
        norm_full,
        gate_in_full,
        conv_in_full,
        step_full,
        kernel_full,
        bias_full,
        gain_full,
        out_full,
    ) = gathered
    inner_width = gate_in_full.shape[1]
    head_count = step_full.shape[1]
    head_width = inner_width // head_count
    channels = conv_in_full.shape[1]
    state_width = (channels - inner_width) // 2
    kernel_taps = kernel_full.shape[0]
    row_count = seq_count * length
    head_rate = -jnp.exp(decay_log)
    tokens_f = hidden.reshape(row_count, model_width).astype(jnp.float32)
    inv_rms = lax.rsqrt(jnp.mean(tokens_f * tokens_f, axis=1, keepdims=True) + norm_epsilon)
    unit = tokens_f * inv_rms
    normed = (unit * norm_full.astype(jnp.float32)[None]).astype(jnp.bfloat16)
    gate_pre = jnp.dot(normed, gate_in_full, preferred_element_type=jnp.float32)
    conv_pre = (
        jnp.dot(normed, conv_in_full, preferred_element_type=jnp.float32)
        .astype(jnp.bfloat16)
        .reshape(seq_count, length, channels)
    )
    raw_step = jnp.dot(normed, step_full, preferred_element_type=jnp.float32)
    rim = shifted(conv_pre[:, length - (kernel_taps - 1) :, :], "seq", 1)
    extended = jnp.concatenate([rim, conv_pre], axis=1).astype(jnp.float32)
    mixed_in = conv_apply(
        extended, kernel_full.astype(jnp.float32), bias_full.astype(jnp.float32), length
    )
    conv_out = jax.nn.silu(mixed_in).astype(jnp.bfloat16)
    value_b = conv_out[:, :, :inner_width].reshape(seq_count, length, head_count, head_width)
    key_b = conv_out[:, :, inner_width : inner_width + state_width]
    query_b = conv_out[:, :, inner_width + state_width :]
    step_size = jax.nn.softplus(raw_step + step_bias[None]).reshape(seq_count, length, head_count)

    def local_forward(value_piece, key_piece, query_piece, step_piece):
        parts = span_parts(value_piece, key_piece, query_piece, step_piece, head_rate)
        return (parts[0], parts[1], parts[2], parts[3])

    within, span_state, total_decay, cumulative = jax.vmap(local_forward)(
        value_b, key_b, query_b, step_size
    )
    identity = (jnp.ones_like(total_decay), jnp.zeros_like(span_state))
    _, carried = prefix((total_decay, span_state), "seq", combine_states, identity, False)
    inter = jax.vmap(span_inter)(query_b, cumulative, carried)
    value_f = value_b.astype(jnp.float32)
    ssm_out = within + inter + skip_gain[None, None, :, None] * value_f
    flat_out = ssm_out.reshape(row_count, inner_width)
    gate_silu = jax.nn.silu(gate_pre)
    gated = flat_out * gate_silu
    inv_gate = lax.rsqrt(jnp.mean(gated * gated, axis=1, keepdims=True) + norm_epsilon)
    normed_gate = gated * inv_gate
    projected_in = (normed_gate * gain_full.astype(jnp.float32)[None]).astype(jnp.bfloat16)
    output = (
        tokens_f + jnp.dot(projected_in, out_full, preferred_element_type=jnp.float32)
    ).astype(jnp.bfloat16)
    backward_weights = (
        lax.all_gather(norm_gain, ("batch", "seq"), axis=0, tiled=True),
        lax.all_gather(w_gate_in, ("batch", "seq"), axis=0, tiled=True),
        lax.all_gather(w_conv_in, ("batch", "seq"), axis=0, tiled=True),
        lax.all_gather(w_step, ("batch", "seq"), axis=0, tiled=True),
        lax.all_gather(conv_weight, ("batch", "seq"), axis=1, tiled=True),
        lax.all_gather(gate_gain, ("batch", "seq"), axis=0, tiled=True),
        lax.all_gather(w_out, ("batch", "seq"), axis=0, tiled=True),
    )
    norm_back, gate_in_back, conv_in_back, step_back, kernel_back, gain_back, out_back = (
        backward_weights
    )
    incoming = cotangent.reshape(row_count, model_width)
    grad_proj = jnp.dot(incoming, out_back.T, preferred_element_type=jnp.float32)
    grad_w_out = jnp.dot(projected_in.T, incoming, preferred_element_type=jnp.float32)
    grad_gate_gain = jnp.sum(grad_proj * normed_gate, axis=0)
    grad_ngate = grad_proj * gain_back.astype(jnp.float32)[None]
    grad_gated = inv_gate * (
        grad_ngate - normed_gate * jnp.mean(grad_ngate * normed_gate, axis=1, keepdims=True)
    )
    grad_flat = grad_gated * gate_silu
    grad_gate_pre = (grad_gated * flat_out * silu_slope(gate_pre)).astype(jnp.bfloat16)
    grad_ssm = grad_flat.reshape(seq_count, length, head_count, head_width)
    grad_skip = jnp.sum(grad_ssm * value_f, axis=(0, 1, 3))
    grad_carried = jax.vmap(carried_grad)(query_b, cumulative, grad_ssm)
    _, grad_state = prefix((total_decay, grad_carried), "seq", combine_states, identity, True)
    grad_total = jnp.sum(grad_state * carried, axis=(2, 3))

    def local_backward(
        value_piece,
        key_piece,
        query_piece,
        step_piece,
        carried_piece,
        grad_piece,
        state_piece,
        total_piece,
    ):
        return span_backward(
            value_piece,
            key_piece,
            query_piece,
            step_piece,
            carried_piece,
            grad_piece,
            state_piece,
            total_piece,
            head_rate,
        )

    grad_value, grad_key, grad_query, grad_steps, grad_rate = jax.vmap(local_backward)(
        value_b, key_b, query_b, step_size, carried, grad_ssm, grad_state, grad_total
    )
    grad_value = grad_value + grad_ssm * skip_gain[None, None, :, None]
    grad_conv_out = jnp.concatenate(
        [grad_value.reshape(seq_count, length, inner_width), grad_key, grad_query], axis=2
    )
    grad_mixed = grad_conv_out * silu_slope(mixed_in)
    grad_bias = jnp.sum(grad_mixed, axis=(0, 1))
    grad_kernel, grad_padded = conv_back(grad_mixed, extended, kernel_back.astype(jnp.float32))
    back_rim = shifted(for_sending(grad_padded[:, : kernel_taps - 1, :]), "seq", -1)
    grad_core = grad_padded[:, kernel_taps - 1 :, :]
    split_at = length - (kernel_taps - 1)
    grad_core = jnp.concatenate(
        [grad_core[:, :split_at], grad_core[:, split_at:] + back_rim], axis=1
    )
    grad_pre = grad_core.astype(jnp.bfloat16).reshape(row_count, channels)
    grad_raw = grad_steps.reshape(row_count, head_count) * jax.nn.sigmoid(
        raw_step + step_bias[None]
    )
    grad_step_bias = jnp.sum(grad_raw, axis=0)
    grad_raw_low = grad_raw.astype(jnp.bfloat16)
    grad_decay_log = jnp.sum(grad_rate, axis=0) * head_rate
    grad_w_gate_in = jnp.dot(normed.T, grad_gate_pre, preferred_element_type=jnp.float32)
    grad_w_conv_in = jnp.dot(normed.T, grad_pre, preferred_element_type=jnp.float32)
    grad_w_step = jnp.dot(normed.T, grad_raw_low, preferred_element_type=jnp.float32)
    grad_normed = jnp.dot(grad_gate_pre, gate_in_back.T, preferred_element_type=jnp.float32)
    grad_normed = grad_normed + jnp.dot(
        grad_pre, conv_in_back.T, preferred_element_type=jnp.float32
    )
    grad_normed = grad_normed + jnp.dot(
        grad_raw_low, step_back.T, preferred_element_type=jnp.float32
    )
    grad_norm_gain = jnp.sum(grad_normed * unit, axis=0)
    grad_unit = grad_normed * norm_back.astype(jnp.float32)[None]
    grad_tokens = inv_rms * (grad_unit - unit * jnp.mean(grad_unit * unit, axis=1, keepdims=True))
    grad_hidden = (incoming.astype(jnp.float32) + grad_tokens).reshape(
        seq_count, length, model_width
    )
    partial_grads = (
        grad_norm_gain,
        grad_w_gate_in,
        grad_w_conv_in,
        grad_w_step,
        grad_kernel,
        grad_bias,
        grad_gate_gain,
        grad_w_out,
    )
    shares = (
        lax.psum_scatter(partial_grads[0], ("batch", "seq"), scatter_dimension=0, tiled=True),
        lax.psum_scatter(partial_grads[1], ("batch", "seq"), scatter_dimension=0, tiled=True),
        lax.psum_scatter(partial_grads[2], ("batch", "seq"), scatter_dimension=0, tiled=True),
        lax.psum_scatter(partial_grads[3], ("batch", "seq"), scatter_dimension=0, tiled=True),
        lax.psum_scatter(partial_grads[4], ("batch", "seq"), scatter_dimension=1, tiled=True),
        lax.psum_scatter(partial_grads[5], ("batch", "seq"), scatter_dimension=0, tiled=True),
        lax.psum_scatter(partial_grads[6], ("batch", "seq"), scatter_dimension=0, tiled=True),
        lax.psum_scatter(partial_grads[7], ("batch", "seq"), scatter_dimension=0, tiled=True),
    )
    head_sums = lax.psum((grad_step_bias, grad_decay_log, grad_skip), ("batch", "seq"))
    return (
        output.reshape(seq_count, length, model_width),
        grad_hidden,
        shares[0],
        shares[1],
        shares[2],
        shares[3],
        shares[4],
        shares[5],
        head_sums[0],
        head_sums[1],
        head_sums[2],
        shares[6],
        shares[7],
    )


bf16 = jnp.bfloat16
f32 = jnp.float32
EXACT = lax.Precision.HIGHEST
LANES = 128


def granted(mebibytes):
    return pltpu.CompilerParams(vmem_limit_bytes=mebibytes << 20)


grant, wide_grant, whole_grant = granted(10), granted(18), granted(60)


def mm(former, latter, dims=((1,), (0,))):
    return lax.dot_general(former, latter, (dims, ((), ())), preferred_element_type=f32)


def mm_exact(former, latter, dims=((1,), (0,))):
    return lax.dot_general(
        former, latter, (dims, ((), ())), precision=EXACT, preferred_element_type=f32
    )


def halves(array):
    high = array.astype(bf16)
    return high, (array - high.astype(f32)).astype(bf16)


def iota(shape, axis):
    return lax.broadcasted_iota(jnp.int32, shape, axis)


def head_map(own, head_width):
    return (iota((LANES, own), 0) == iota((LANES, own), 1) // head_width).astype(f32)


def triangle_sum(table, array):
    high, low = halves(array)
    table = table.astype(bf16)
    return mm(jnp.concatenate([table, table], axis=1), jnp.concatenate([high, low], axis=0))


def twice(array):
    return jnp.concatenate([array, array], axis=1)


def stacked_halves(array):
    return jnp.concatenate(halves(array), axis=0)


def step_tables(raw, rate):
    span = raw.shape[0]
    step = jnp.maximum(raw, 0.0) + jnp.log1p(jnp.exp(-jnp.abs(raw)))
    return step, triangle_sum(iota((span, span), 0) >= iota((span, span), 1), step * rate)


def pair_masked(array, head_width):
    low = iota(array.shape, 1) < head_width
    zero = jnp.zeros_like(array)
    return jnp.concatenate([jnp.where(low, array, zero), jnp.where(low, zero, array)], axis=0)


def by_pair_lanes(array, pair, head_width):
    shape = (array.shape[0], 2 * head_width)
    first = jnp.broadcast_to(array[:, 2 * pair : 2 * pair + 1], shape)
    second = jnp.broadcast_to(array[:, 2 * pair + 1 : 2 * pair + 2], shape)
    return jnp.where(iota(shape, 1) < head_width, first, second)


def place(i, rank):
    m = lax.bitwise_xor(i, rank)
    return 4 * lax.bitwise_and(m, 1) + lax.shift_right_logical(m, 1)


def span_at(place_index, rank):
    m = 2 * lax.bitwise_and(place_index, 3) + lax.shift_right_logical(place_index, 2)
    return lax.bitwise_xor(m, rank)


def project_kernel(
    where_ref, t0, t1, t2, t3, t4, t5, t6, t7, gain_ref, w0, w1, w2, w3, shared_ref,
    normed_ref, pre_ref, raw_ref, weight_ref, *, states,
):
    step = pl.program_id(0)
    plane = where_ref[1]
    span, width = t0.shape
    own = w0.shape[1]
    block = width // 4

    @pl.when(step == 0)
    def _():
        for o, w in enumerate((w0, w1, w2, w3)):
            weight_ref[o * block : (o + 1) * block, :own] = w[...]
        weight_ref[:, own:] = shared_ref[...]

    parts = (t0, t1, t2, t3, t4, t5, t6, t7)
    for half in range(4):

        @pl.when(step == half)
        def _(half=half):
            for i in range(2):
                part = parts[2 * half + i]
                tokens = part[...].astype(f32)
                inv_rms = lax.rsqrt(jnp.mean(tokens * tokens, axis=1, keepdims=True) + norm_epsilon)
                for o in range(4):
                    at = pl.multiple_of(lax.bitwise_and(plane - o + 4, 3) * block, LANES)
                    value = part[:, pl.ds(at, block)].astype(f32) * inv_rms
                    value = (value * gain_ref[:, pl.ds(at, block)]).astype(bf16)
                    normed_ref[i * span : (i + 1) * span, o * block : (o + 1) * block] = value

    product = mm(normed_ref[...], weight_ref[...])
    local = own + 2 * states
    pre_ref[...] = product[:, :local].astype(bf16)
    raw_ref[...] = product[:, local:]


def forward_kernel(
    where_ref, pre_ref, raw_ref, taps_ref, heads_ref, rows_ref,
    mixed_ref, conv_ref, inter_ref, ssm_ref, state_ref,
    ext, state, *, n_taps, head_width, states,
):
    span, own = ssm_ref.shape[1:]

    @pl.when(pl.program_id(0) == 0)
    def _():
        ext[0:8, :] = jnp.zeros((8, ext.shape[1]), f32)
        state[...] = jnp.zeros_like(state)

    ext[8 : 8 + span, :] = pre_ref[0].astype(f32)
    mixed = taps_ref[n_taps : n_taps + 1, :]
    for k in range(n_taps):
        first = 8 - (n_taps - 1) + k
        mixed = mixed + taps_ref[k : k + 1, :] * ext[first : first + span, :]
    mixed_ref[0] = mixed
    ext[0:8, :] = ext[span : span + 8, :]
    conv = (mixed * jax.nn.sigmoid(mixed)).astype(bf16)
    conv_ref[0] = conv
    key, query = conv[:, own : own + states], conv[:, own + states :]
    step, cum = step_tables(raw_ref[0] + heads_ref[0:1, :], heads_ref[1:2, :])
    cum_t, step_t = cum.T, step.T
    affinity = mm(query, key, ((1,), (1,)))
    causal = iota((span, span), 0) >= iota((span, span), 1)
    entering = state[...]
    state_ref[0] = entering
    base = mm(twice(query), stacked_halves(entering))
    weighted, kept = [], []
    for pair in range(own // (2 * head_width)):
        lanes = slice(2 * pair * head_width, 2 * (pair + 1) * head_width)
        value = conv_ref[0, :, lanes]
        mixing = []
        for h in (2 * pair, 2 * pair + 1):
            decay = jnp.exp(jnp.where(causal, cum[:, h : h + 1] - cum_t[h : h + 1, :], -1e30))
            mixing.append((affinity * decay * step_t[h : h + 1, :]).astype(bf16))
        cum_pair = by_pair_lanes(cum, pair, head_width)
        growth = jnp.exp(cum_pair)
        tailed = jnp.exp(cum_pair[span - 1 : span, :] - cum_pair) * by_pair_lanes(step, pair, head_width)
        inter = growth * base[:, lanes]
        inter_ref[0, :, lanes] = inter
        value_f = value.astype(f32)
        within = mm(jnp.concatenate(mixing, axis=1), pair_masked(value, head_width))
        ssm_ref[0, :, lanes] = within + inter + rows_ref[1:2, lanes] * value_f
        weighted.append((tailed * value_f).astype(bf16))
        kept.append(growth[span - 1 : span, :])
    weighted, kept = jnp.concatenate(weighted, axis=1), jnp.concatenate(kept, axis=1)
    state[...] = kept * entering + mm(key, weighted, ((0,), (0,)))


def gate_kernel(
    where_ref, normed_ref, g0, g1, g2, g3, c0, c1, c2, c3, c4, c5, c6, c7,
    p0, p1, p2, p3, borrowed_ref, rows_ref, ssm_ref,
    gate_ref, ngate_ref, sums_ref, gated_ref, weight_ref, cot_ref, out_ref,
):
    step = pl.program_id(0)
    core, plane = lax.bitwise_and(where_ref[0], 1), where_ref[1]
    block = g0.shape[0]
    span = c0.shape[0]

    @pl.when(step == 0)
    def _():
        for o, w in enumerate((g0, g1, g2, g3)):
            weight_ref[o * block : (o + 1) * block, :] = w[...]
        for o, part in enumerate((p0, p1, p2, p3)):
            place_rows(out_ref, part, borrowed_ref, o, core, lax.bitwise_and(plane - o + 4, 3))

    parts = (c0, c1, c2, c3, c4, c5, c6, c7)
    for half in range(4):

        @pl.when(step == half)
        def _(half=half):
            for i in range(2):
                cot_ref[i * span : (i + 1) * span, :] = parts[2 * half + i][...]

    gate = mm(normed_ref[...], weight_ref[...])
    gate_ref[...] = gate
    gated = ssm_ref[...] * (gate * jax.nn.sigmoid(gate))
    gain = rows_ref[0:1, :]
    ngate = mm(cot_ref[...], out_ref[...], ((1,), (1,))) * gain
    ngate_ref[...] = ngate
    squares, cross = gated * gated, ngate * gated
    for i in range(2):
        rows = slice(i * span, (i + 1) * span)
        sums = []
        for product in (squares[rows], cross[rows]):
            folded = product[:, :LANES] + product[:, LANES : 2 * LANES] + product[:, 2 * LANES :]
            sums.append(jnp.sum(folded.T, axis=0, keepdims=True))
        row = iota((8, LANES), 0)
        sums_ref[span_at(2 * step + i, where_ref[0])] = jnp.where(row == 0, sums[0], sums[1])
    gated_ref[...] = (gated * gain).astype(bf16)


def out_part_kernel(where_ref, gated_ref, out_ref, mine_ref, other_ref):
    step = pl.program_id(0)
    part = mm(gated_ref[...], out_ref[...]).astype(bf16)

    @pl.when(step < 2)
    def _():
        mine_ref[...] = part

    @pl.when(step >= 2)
    def _():
        other_ref[...] = part


def gate_back_kernel(
    where_ref, sums_ref, ssm_ref, gate_ref, ngate_ref, rows_ref,
    grad_ref, grad_gate_ref, projected_ref, lent_ref, *, inner, third,
):
    step = pl.program_id(0)
    rows, own = ssm_ref.shape
    core = lax.bitwise_and(where_ref[0], 1)
    lent_ref[...] = jnp.zeros_like(lent_ref)
    span = LANES
    for i in range(rows // span):
        at = slice(i * span, (i + 1) * span)
        sums = sums_ref[span_at(rows // span * step + i, where_ref[0])]
        sums = jnp.concatenate([sums, jnp.zeros((LANES - 8, LANES), f32)], axis=0).T
        inv_gate = lax.rsqrt(sums[:, 0:1] / inner + norm_epsilon)
        mean = inv_gate * sums[:, 1:2] / inner
        inv_gate = jnp.broadcast_to(inv_gate, (span, own))
        ssm, gate = ssm_ref[at], gate_ref[at]
        logistic = jax.nn.sigmoid(gate)
        silu = gate * logistic
        normed = ssm * silu * inv_gate
        grad_gated = inv_gate * (ngate_ref[at] - normed * mean)
        grad_ref[at] = grad_gated * silu
        slope = logistic * (1.0 + gate * (1.0 - logistic))
        grad_gate_ref[at] = (grad_gated * ssm * slope).astype(bf16)
        projected_ref[at] = (normed * rows_ref[0:1, :]).astype(bf16)
    for k in range(2):

        @pl.when(core == k)
        def _(k=k):
            for plane, first, _, count in local_slices(k, 2 * third):
                if count == 4 * third:
                    source = first + 3 * third if k == 0 else first
                    to = plane // 2 * third
                    lent_ref[:, to : to + third] = projected_ref[:, source : source + third]


def gate_grad_kernel(where_ref, normed_ref, grad_gate_ref, b0, b1, b2, b3):
    total = mm(normed_ref[...], grad_gate_ref[...], ((0,), (0,))).astype(bf16)
    for o, out_ref in enumerate((b0, b1, b2, b3)):

        @pl.when(pl.program_id(0) == o)
        def _(out_ref=out_ref):
            out_ref[...] = total


def out_grad_kernel(
    where_ref, projected_ref, borrowed_ref, cot_ref, b0, b1, b2, b3, rows_ref, total_ref, *, third,
):
    step = pl.program_id(0)
    core, plane = lax.bitwise_and(where_ref[0], 1), where_ref[1]
    rows = 3 * third
    block = b0.shape[1]
    for k in range(2):

        @pl.when(core == k)
        def _(k=k):
            for at_plane, at, _, count in local_slices(k, 2 * third):
                to = at_plane * rows
                lent = slice(at_plane // 2 * third, (at_plane // 2 + 1) * third)
                if count == rows + third:
                    own_at = at if k == 0 else at + third
                    rows_ref[:, to : to + rows] = projected_ref[:, own_at : own_at + rows]
                elif k == 0:
                    rows_ref[:, to : to + count] = projected_ref[:, at : at + count]
                    rows_ref[:, to + count : to + rows] = borrowed_ref[:, lent]
                else:
                    rows_ref[:, to + third : to + rows] = projected_ref[:, at : at + count]
                    rows_ref[:, to : to + third] = borrowed_ref[:, lent]

    total = mm(rows_ref[...], cot_ref[...], ((0,), (0,)))

    @pl.when(step == 0)
    def _():
        total_ref[...] = total

    @pl.when(step == 1)
    def _():
        total_ref[...] += total
        for o, out_ref in enumerate((b0, b1, b2, b3)):
            first = pl.multiple_of(rows * lax.bitwise_and(plane - o + 4, 3), third)
            for g in range(4):
                own = total_ref[pl.ds(first, rows), g * block : (g + 1) * block]
                out_ref[g * rows : (g + 1) * rows, :] = own.astype(bf16)


def backward_kernel(
    where_ref, grad_ref, inter_ref, state_ref, conv_ref, pre_ref, mixed_ref, raw_ref,
    taps_ref, heads_ref, rows_ref,
    grad_pre_ref, grad_taps_ref, grad_heads_ref,
    ext, grad_state, next_state, *, n_taps, head_width, states,
):
    span, own = grad_ref.shape[1:]

    @pl.when(pl.program_id(0) == 0)
    def _():
        ext[span : span + 8, :] = jnp.zeros((8, ext.shape[1]), f32)
        grad_state[...] = jnp.zeros_like(grad_state)
        next_state[...] = jnp.zeros_like(next_state)
        grad_taps_ref[...] = jnp.zeros_like(grad_taps_ref)
        grad_heads_ref[...] = jnp.zeros_like(grad_heads_ref)

    key, query = conv_ref[0, :, own : own + states], conv_ref[0, :, own + states :]
    rate = heads_ref[1:2, :]
    raw = raw_ref[0] + heads_ref[0:1, :]
    step, cum = step_tables(raw, rate)
    cum_t, step_t = cum.T, step.T
    tail = jnp.exp(cum[span - 1 : span, :] - cum)
    affinity = mm(query, key, ((1,), (1,)))
    causal = iota((span, span), 0) >= iota((span, span), 1)
    after = grad_state[...]
    after_halves = stacked_halves(after)
    grad_weighted = mm(twice(key), after_halves)
    grad_affinity = jnp.zeros((span, span), f32)
    direct_t = jnp.zeros((span, span), f32)
    grad_cum = jnp.zeros((span, LANES), f32)
    row, lane = iota((span, span), 0), iota((span, LANES), 1)
    weighted, grown, grown_rest, kept = [], [], [], []
    products = [[], [], []]
    mixed = mixed_ref[0]
    logistic = jax.nn.sigmoid(mixed)
    slope = logistic * (1.0 + mixed * (1.0 - logistic))
    for pair in range(own // (2 * head_width)):
        lanes = slice(2 * pair * head_width, 2 * (pair + 1) * head_width)
        value, grad_y = conv_ref[0, :, lanes], grad_ref[0, :, lanes]
        value_f, grad_low = value.astype(f32), grad_y.astype(bf16)
        cum_pair = by_pair_lanes(cum, pair, head_width)
        growth = jnp.exp(cum_pair)
        tailed = jnp.exp(cum_pair[span - 1 : span, :] - cum_pair) * by_pair_lanes(step, pair, head_width)
        kept.append(growth[span - 1 : span, :])
        high, low = halves(grad_y * growth)
        grown.append(high)
        grown_rest.append(low)
        weighted.append((tailed * value_f).astype(bf16))
        grad_mixing = mm(grad_low, pair_masked(value, head_width), ((1,), (1,)))
        mixing = []
        for i in (0, 1):
            h = 2 * pair + i
            given = grad_mixing[:, i * span : (i + 1) * span]
            decay = jnp.exp(jnp.where(causal, cum[:, h : h + 1] - cum_t[h : h + 1, :], -1e30))
            grad_affinity = grad_affinity + given * decay * step_t[h : h + 1, :]
            table = affinity * decay
            scores = table * step_t[h : h + 1, :]
            mixing.append(scores.astype(bf16))
            direct_t = jnp.where(row == h, jnp.sum(given * table, axis=0, keepdims=True), direct_t)
            grad_cum = jnp.where(lane == h, jnp.sum(given * scores, axis=1, keepdims=True), grad_cum)
        grad_value = mm(jnp.concatenate(mixing, axis=0), pair_masked(grad_low, head_width), ((0,), (0,)))
        by_state = grad_weighted[:, lanes]
        grad_value = grad_value + tailed * by_state + rows_ref[1:2, lanes] * grad_y
        ext[0:span, lanes] = grad_value * slope[:, lanes]
        products[0].append(by_state * value_f)
        products[1].append(grad_y * inter_ref[0, :, lanes])
        products[2].append(jnp.sum(grad_y * value_f, axis=0, keepdims=True))
    weighted, grown = jnp.concatenate(weighted, axis=1), jnp.concatenate(grown, axis=1)
    grown_rest, kept = jnp.concatenate(grown_rest, axis=1), jnp.concatenate(kept, axis=1)
    grad_affinity = grad_affinity.astype(bf16)
    grad_query = mm(grown, state_ref[0].astype(bf16), ((1,), (1,))) + mm(grad_affinity, key)
    grad_key = mm(weighted, after_halves[:states], ((1,), (1,))) + mm(grad_affinity, query, ((0,), (0,)))
    ext[0:span, own : own + states] = grad_key * slope[:, own : own + states]
    ext[0:span, own + states :] = grad_query * slope[:, own + states :]
    to_lanes = head_map(own, head_width).astype(bf16)
    last = jnp.sum(after * next_state[...], axis=0, keepdims=True)
    by_head = jnp.concatenate(
        [
            jnp.concatenate(products[0], axis=1),
            jnp.concatenate(products[1], axis=1),
            jnp.broadcast_to(jnp.concatenate(products[2], axis=1), (8, own)),
            jnp.broadcast_to(last, (8, own)),
        ],
        axis=0,
    )
    high, low = halves(by_head)
    by_head = mm(high, to_lanes, ((1,), (1,))) + mm(low, to_lanes, ((1,), (1,)))
    direct = direct_t.T + by_head[:span] * tail
    grad_cum = grad_cum + by_head[span : 2 * span] - step * direct
    last = by_head[2 * span + 8 : 2 * span + 9]
    grad_cum = grad_cum + jnp.where(iota(grad_cum.shape, 0) == span - 1, last, 0.0)
    grad_log = triangle_sum(iota((span, span), 0) <= iota((span, span), 1), grad_cum)
    grad_raw = (direct + grad_log * rate) * jax.nn.sigmoid(raw)
    grad_heads_ref[0:1, :] += jnp.sum(grad_raw, axis=0, keepdims=True)
    grad_heads_ref[1:2, :] += jnp.sum(grad_log * step, axis=0, keepdims=True) * rate
    grad_heads_ref[2:3, :] += by_head[2 * span : 2 * span + 1]
    pre = pre_ref[0].astype(f32)
    grad_pre = jnp.zeros(pre.shape, f32)
    for k in range(n_taps):
        ahead = ext[n_taps - 1 - k : n_taps - 1 - k + span, :]
        grad_pre = grad_pre + ahead * taps_ref[k : k + 1, :]
        grad_taps_ref[k : k + 1, :] += jnp.sum(ahead * pre, axis=0, keepdims=True)
    grad_taps_ref[n_taps : n_taps + 1, :] += jnp.sum(ext[0:span, :], axis=0, keepdims=True)
    ext[span : span + 8, :] = ext[0:8, :]
    grad_pre_ref[0, :, : own + 2 * states] = grad_pre.astype(bf16)
    grad_pre_ref[0, :, own + 2 * states :] = grad_raw.astype(bf16)
    grad_state[...] = kept * after + mm(
        jnp.concatenate([query, query], axis=0), jnp.concatenate([grown, grown_rest], axis=0), ((0,), (0,))
    )
    next_state[...] = state_ref[0]


def input_grad_kernel(gate_ref, rest_ref, w_gate_ref, w_rest_ref, mine_ref, other_ref):
    half = mine_ref.shape[0]
    total = mm(gate_ref[...], w_gate_ref[...], ((1,), (1,))) + mm(rest_ref[...], w_rest_ref[...], ((1,), (1,)))
    mine_ref[...] = total[:half].astype(bf16)
    other_ref[...] = total[half:].astype(bf16)


def input_grad_call(gate, rest, w_gate, w_rest):
    half, width, block = gate.shape[0] // 2, w_gate.shape[0], w_gate.shape[0] // 3
    return pl.pallas_call(
        input_grad_kernel,
        out_shape=[jax.ShapeDtypeStruct((half, width), bf16)] * 2,
        grid=(3,),
        in_specs=[pl.BlockSpec(a.shape, lambda i: (0, 0)) for a in (gate, rest)]
        + [pl.BlockSpec((block, a.shape[1]), lambda i: (i, 0)) for a in (w_gate, w_rest)],
        out_specs=[pl.BlockSpec((half, block), lambda i: (0, i))] * 2,
        compiler_params=grant,
    )(gate, rest, w_gate, w_rest)


def by_span(shape, order):
    return pl.BlockSpec((1, *shape), lambda i, where: (order(i, where), 0, 0))


def spans_call(kernel, where, spans, inputs, outputs, scratch=()):
    in_specs = [
        by_span(a.shape[1:], order) if order else pl.BlockSpec(a.shape, lambda i, where, n=a.ndim: (0,) * n)
        for a, order in inputs
    ]
    out_specs = [
        by_span(shape, order) if order else pl.BlockSpec(shape, lambda i, where, n=len(shape): (0,) * n)
        for shape, _, order in outputs
    ]
    out_shape = [
        jax.ShapeDtypeStruct(
            (spans, *shape) if order else shape, dtype
        )
        for shape, dtype, order in outputs
    ]
    return pl.pallas_call(
        kernel,
        out_shape=out_shape,
        grid_spec=pltpu.PrefetchScalarGridSpec(
            num_scalar_prefetch=1,
            grid=(spans,),
            in_specs=in_specs,
            out_specs=out_specs,
            scratch_shapes=list(scratch),
        ),
        compiler_params=grant,
    )(where, *[a for a, _ in inputs])


def in_time(i, where):
    return i


def in_reverse(i, where):
    return 7 - i


def relative(i, where):
    return place(i, where[0])


def relative_reverse(i, where):
    return place(7 - i, where[0])


class Columns(typing.NamedTuple):
    shape: tuple
    first: int = 0


def rows_call(kernel, where, steps, rows, inputs, outputs, scratch=(), params=grant):
    def spec(shape, index):
        if isinstance(index, Columns):
            return pl.BlockSpec(index.shape, lambda i, where: (0, index.first + i))
        if index is None:
            return pl.BlockSpec(shape, lambda i, where, n=len(shape): (0,) * n)
        return pl.BlockSpec((rows, *shape[1:]), lambda i, where: (index(i), 0))

    return pl.pallas_call(
        kernel,
        out_shape=[jax.ShapeDtypeStruct(shape, dtype) for shape, dtype, _ in outputs],
        grid_spec=pltpu.PrefetchScalarGridSpec(
            num_scalar_prefetch=1,
            grid=(steps,),
            in_specs=[spec(a.shape, index) for a, index in inputs],
            out_specs=[spec(shape, index) for shape, _, index in outputs],
            scratch_shapes=list(scratch),
        ),
        compiler_params=params,
    )(where, *[a for a, _ in inputs])


def each(i):
    return i


def halves_swapped(i):
    return 1 - i


def lower(i):
    return lax.min(i, 1)


def upper(i):
    return lax.max(i - 2, 0)


def local_slices(core, width):
    at, slices = 0, []
    for plane in range(4):
        count = 2 * width if plane % 2 == core else width
        slices.append((plane, at, 0 if core == 0 else 3 * width - count, count))
        at += count
    return slices


def pack_kernel(
    gate_ref, conv_ref, step_ref, norm_ref, gain_ref, bias_ref, taps_ref,
    cols_ref, message_ref, *, head_width,
):
    inner = gate_ref.shape[1]
    group = 3 * head_width
    for chip in range(4):
        for core in range(2):
            for plane, at, start, count in local_slices(core, head_width):
                source = group * (4 * plane + chip) + start
                for first, ref in ((0, conv_ref), (cols_ref.shape[2] // 2, gate_ref)):
                    to = slice(first + at, first + at + count)
                    cols_ref[2 * chip + core, :, to] = ref[:, source : source + count]
    rest = conv_ref.shape[1] - inner
    rows = gate_ref.shape[0]
    message_ref[...] = jnp.zeros_like(message_ref)
    message_ref[:rows, :rest] = conv_ref[:, inner:]
    message_ref[:rows, rest : rest + step_ref.shape[1]] = step_ref[...]
    vectors = jnp.zeros((8, LANES), f32)

    def put(vectors, ref, at):
        value = ref[...].astype(f32)
        value = jnp.pad(value, ((at, 8 - at - value.shape[0]), (0, LANES - value.shape[1])))
        return vectors + value

    for ref, at in ((norm_ref, 0), (gain_ref, 1), (bias_ref, 2), (taps_ref, 3)):
        vectors = put(vectors, ref, at)
    message_ref[rows:, :LANES] = vectors.astype(bf16)


def setup_kernel(
    where_ref, mine_ref, other_ref, heads_ref,
    shared_ref, norm_ref, taps_ref, channels_ref, head_rows_ref, pick_ref,
    gain_all, taps_all, held, *, n_taps, head_width,
):
    rank, plane = where_ref[0], where_ref[1]
    padded = shared_ref.shape[1]
    rows = norm_ref.shape[1] // 32
    block = 8 * rows
    rows_in, rows_out = norm_ref.shape[1] // 32, gain_all.shape[1] // 32
    piece = taps_all.shape[1] // 32
    inner = gain_all.shape[1]
    own = channels_ref.shape[1]
    for p in range(8):
        source = lax.bitwise_xor(rank, 2 * (p % 4) + p // 4)
        part_ref, top = (mine_ref, other_ref)[p // 4], p % 4 * (rows + 8)
        for o in range(4):
            at = pl.multiple_of(o * block + source * rows, 16)
            lanes = slice(o * padded, (o + 1) * padded)
            shared_ref[pl.ds(at, rows), :] = part_ref[top : top + rows, lanes]
            device = 8 * lax.bitwise_and(plane - o + 4, 3) + source
            held[device] = part_ref[top + rows : top + rows + 8, o * padded : o * padded + LANES].astype(f32)
    for i in range(32):
        vectors = held[i]
        norm_ref[:, i * rows_in : (i + 1) * rows_in] = vectors[0:1, :rows_in]
        gain_all[:, i * rows_out : (i + 1) * rows_out] = vectors[1:2, :rows_out]
        taps_all[:, i * piece : (i + 1) * piece] = vectors[:, :piece]
    taps_ref[...] = jnp.zeros_like(taps_ref)
    channels_ref[...] = jnp.zeros_like(channels_ref)
    taps_ref[0:n_taps, own:] = taps_all[3 : 3 + n_taps, inner:]
    taps_ref[n_taps : n_taps + 1, own:] = taps_all[2:3, inner:]
    for r in range(8):

        @pl.when(rank == r)
        def _(r=r):
            chip, core = r // 2, r % 2
            local, heads = iota((LANES, LANES), 0), iota((LANES, LANES), 1)
            chosen = jnp.zeros((LANES, LANES), jnp.bool_)
            for plane, at, start, count in local_slices(core, head_width):
                source = 3 * head_width * (4 * plane + chip) + start
                taps_ref[0:n_taps, at : at + count] = taps_all[3 : 3 + n_taps, source : source + count]
                taps_ref[n_taps : n_taps + 1, at : at + count] = taps_all[2:3, source : source + count]
                channels_ref[0:1, at : at + count] = gain_all[:, source : source + count]
                for j in range(count // head_width):
                    chosen |= (local == at // head_width + j) & (heads == source // head_width + j)
            pick_ref[...] = chosen.astype(f32)

    states = (padded - LANES) // 2
    chosen = pick_ref[...].astype(bf16)
    shared_ref[:, 2 * states :] = mm(shared_ref[:, 2 * states :], chosen, ((1,), (1,))).astype(bf16)
    head_rows = mm_exact(heads_ref[...], pick_ref[...], ((1,), (1,)))
    used = iota((1, LANES), 1) < own // head_width
    head_rows_ref[...] = jnp.zeros_like(head_rows_ref)
    head_rows_ref[0:1, :] = head_rows[0:1]
    head_rows_ref[1:2, :] = jnp.where(used, -jnp.exp(head_rows[1:2]), 0.0)
    channels_ref[1:2, :] = mm_exact(head_rows, head_map(own, head_width))[2:3]


def place_rows(out_ref, part_ref, borrowed_ref, o, core, at_plane):
    rows = part_ref.shape[0]
    third = rows // 3
    for k in range(2):
        for slices_plane, at, _, count in local_slices(k, 2 * third):

            @pl.when((core == k) & (at_plane == slices_plane))
            def _(k=k, at=at, count=count):
                if count == rows + third and k == 0:
                    out_ref[at : at + rows, :] = part_ref[...]
                    out_ref[at + rows : at + count, :] = borrowed_ref[o]
                elif count == rows + third:
                    out_ref[at : at + third, :] = borrowed_ref[o]
                    out_ref[at + third : at + count, :] = part_ref[...]
                elif k == 0:
                    out_ref[at : at + count, :] = part_ref[: 2 * third, :]
                else:
                    out_ref[at : at + count, :] = part_ref[third:, :]


def total_of(refs, rows=slice(None)):
    total = refs[0][rows].astype(f32)
    for ref in refs[1:]:
        total = total + ref[rows].astype(f32)
    return total


def as_row(column, count):
    return jnp.broadcast_to(column, (column.shape[0], LANES)).T[:1, :count]


def early_rows_kernel(p0, p1, p2, w_ref, gain_ref, out_ref, dot_ref):
    rows = out_ref.shape[0]
    block = p0.shape[1]
    for g in range(4):
        at = slice(g * rows, (g + 1) * rows)
        out_ref[:, g * block : (g + 1) * block] = total_of((p0, p1, p2), at)
    dot = jnp.sum(w_ref[...].astype(f32) * out_ref[...], axis=1, keepdims=True)
    dot_ref[...] = as_row(dot, rows) / gain_ref[...].astype(f32)


def late_rows_kernel(g0, g1, g2, c0, c1, c2, out_ref):
    own = g0.shape[1]
    rows = out_ref.shape[1]
    for r in range(8):
        at = slice(r * rows, (r + 1) * rows)
        out_ref[r, :, :own] = total_of((g0, g1, g2), at).astype(bf16)
        out_ref[r, :, own:] = total_of((c0, c1, c2), at).astype(bf16)


def columns_kernel(
    table_ref, w_gate_ref, w_conv_ref, w_step_ref, gain_ref, s0, s1, s2, s3,
    gate_ref, conv_ref, dot_ref, step_ref, taps_ref, bias_ref, step_bias_ref, decay_ref, skip_ref, *, head_width,
):
    group = 3 * head_width
    inner = 16 * group
    half = table_ref.shape[2] // 2
    for chip in range(4):
        for core in range(2):
            for plane, at, start, count in local_slices(core, head_width):
                to = slice(group * (4 * plane + chip) + start, group * (4 * plane + chip) + start + count)
                gate_ref[:, to] = table_ref[2 * chip + core, :, at : at + count].astype(f32)
                conv_ref[:, to] = table_ref[2 * chip + core, :, half + at : half + at + count].astype(f32)
    rows = gate_ref.shape[0]
    rest = conv_ref.shape[1] - inner
    shared = total_of((s0, s1, s2, s3))
    conv_ref[:, inner:] = shared[:rows, :rest]
    step_ref[...] = shared[:rows, rest : rest + step_ref.shape[1]]
    small = shared[rows:, :LANES] + shared[rows:, LANES : 2 * LANES]
    at = 0
    for ref in (taps_ref, bias_ref, step_bias_ref, decay_ref, skip_ref):
        ref[...] = small[at : at + ref.shape[0], : ref.shape[1]]
        at += ref.shape[0]
    total = jnp.sum(w_step_ref[...].astype(f32) * step_ref[...], axis=1, keepdims=True)
    for weight_ref, grad_ref in ((w_gate_ref, gate_ref), (w_conv_ref, conv_ref)):
        total = total + jnp.sum(weight_ref[...].astype(f32) * grad_ref[...], axis=1, keepdims=True)
    dot_ref[...] = as_row(total, rows) / gain_ref[...].astype(f32)


def output_kernel(where_ref, o0, o1, o2, o3, hidden_ref, sums_ref, output_ref, *, inner):
    sums = jnp.concatenate([sums_ref[where_ref[0]], jnp.zeros((LANES - 8, LANES), f32)], axis=0).T
    inv_gate = lax.rsqrt(sums[:, 0:1] / inner + norm_epsilon)
    output_ref[...] = (hidden_ref[...].astype(f32) + inv_gate * total_of((o0, o1, o2, o3))).astype(bf16)


def hidden_grad_kernel(where_ref, g0, g1, g2, g3, hidden_ref, cot_ref, norm_ref, grad_ref, held):
    plane = where_ref[1]
    tokens = hidden_ref[...].astype(f32)
    inv_rms = lax.rsqrt(jnp.mean(tokens * tokens, axis=1, keepdims=True) + norm_epsilon)
    block = tokens.shape[1] // 4
    grad_ref[...] = total_of((g0, g1, g2, g3))
    for p in range(4):
        at = pl.multiple_of(block * lax.bitwise_and(plane - p + 4, 3), LANES)
        lanes = slice(p * block, (p + 1) * block)
        held[:, lanes] = grad_ref[:, pl.ds(at, block)] * norm_ref[:, lanes]
    grad_unit, unit = held[...], tokens * inv_rms
    mean = jnp.mean(grad_unit * unit, axis=1, keepdims=True)
    grad_ref[...] = cot_ref[...].astype(f32) + inv_rms * (grad_unit - unit * mean)


def once(kernel, inputs, outputs, where=None, scratch=(), params=grant):
    specs = lambda shapes: [pl.BlockSpec(s, lambda *_, n=len(s): (0,) * n) for s in shapes]
    out_shape = [jax.ShapeDtypeStruct(shape, dtype) for shape, dtype in outputs]
    grid_spec = pltpu.PrefetchScalarGridSpec(
        num_scalar_prefetch=0 if where is None else 1,
        grid=(1,),
        in_specs=specs([a.shape for a in inputs]),
        out_specs=specs([shape for shape, _ in outputs]),
        scratch_shapes=list(scratch),
    )
    call = pl.pallas_call(kernel, out_shape=out_shape, grid_spec=grid_spec, compiler_params=params)
    return call(*([] if where is None else [where]), *inputs)


def hop(value, distance):
    count = lax.axis_size("seq")
    pairs = [(i, i ^ distance) for i in range(count)]
    return lax.ppermute(value, "seq", pairs)


def plane_hop(value, distance):
    count = lax.axis_size("batch")
    pairs = [(i, (i + distance) % count) for i in range(count)]
    return lax.ppermute(value, "batch", pairs)


def planes_gather(value, direct=False):
    one, three = plane_hop(value, 1), plane_hop(value, -1)
    two = plane_hop(value, 2) if direct else plane_hop(one, 1)
    return [value, one, two, three]


def planes_parts(blocks):
    near, far = plane_hop(blocks[1], -1), plane_hop(blocks[2], 1)
    sent = (blocks[3].astype(f32) + far.astype(f32)).astype(blocks[3].dtype)
    return [blocks[0], near, plane_hop(sent, 1)]


def planes_direct(blocks):
    return [blocks[0]] + [plane_hop(blocks[o], -o) for o in (1, 2, 3)]


def plane_gather(value):
    chips = [value] + [hop(value, distance) for distance in (2, 4, 6)]
    return chips + [hop(part, 1) for part in chips]


def small_gather(value):
    parts = [value] + [hop(value, distance) for distance in (2, 4, 6)]
    mine = jnp.concatenate(parts)
    return mine, hop(mine, 1)


def plane_parts(mine, other):
    count = mine.shape[0] // 4
    other = hop(other, 1)
    half = []
    for j in range(4):
        rows = slice(j * count, (j + 1) * count)
        half.append((mine[rows].astype(f32) + other[rows].astype(f32)).astype(bf16))
    return half[:1] + [hop(half[j], 2 * j) for j in (1, 2, 3)]


def plane_total(value):
    value = value + hop(value, 1)
    return value + hop(value, 2) + hop(value, 4) + hop(value, 6)


def local_group(index, core, width):
    plane, at = jnp.zeros_like(index), jnp.zeros_like(index)
    for k in range(2):
        for slices_plane, first, start, count in local_slices(k, width):
            inside = (core == k) & (index >= first) & (index < first + count)
            plane = jnp.where(inside, slices_plane, plane)
            at = jnp.where(inside, index - first + start, at)
    return plane, at


def shared_back_kernel(where_ref, rows_ref, taps_ref, heads_ref, pick_ref, mine_ref, other_ref, *, head_width, piece):
    rank, plane = where_ref[0], where_ref[1]
    rows = mine_ref.shape[2] - 8
    local = taps_ref.shape[1]
    own = 6 * head_width
    inner = 8 * own
    core, chip = lax.bitwise_and(rank, 1), lax.shift_right_logical(rank, 1)
    at = iota((local, LANES), 0)
    at_plane, offset = local_group(at, core, head_width)
    column = jnp.where(at < own, 3 * head_width * (4 * at_plane + chip) + offset, inner + at - own)
    heads = mm_exact(heads_ref[...], pick_ref[...])
    heads = jnp.concatenate([jnp.zeros((5, LANES), f32), heads[:3]], axis=0)
    high, low = halves(taps_ref[...])
    both = jnp.concatenate([high, low], axis=0)
    target = LANES * (column // piece) + column % piece - iota((local, LANES), 1)
    head_halves = halves(heads)
    for o in range(4):
        first = 8 * lax.bitwise_and(plane - o + 4, 3)
        for p in range(8):
            r = lax.bitwise_xor(rank, 2 * (p % 4) + p // 4)
            out_ref, q = (mine_ref, other_ref)[p // 4], p % 4
            chosen = (target == LANES * (first + r)).astype(bf16)
            spread = mm(both, chosen)
            own_rows = rows_ref[pl.ds(pl.multiple_of((8 * o + r) * rows, 16), rows), :]
            out_ref[q, o, :rows, : 2 * LANES] = own_rows[:, : 2 * LANES]
            out_ref[q, o, :rows, 2 * LANES :] = mm(own_rows[:, 2 * LANES :], pick_ref[...].astype(bf16)).astype(bf16)
            for half in (0, 1):
                value = spread[8 * half : 8 * half + 8].astype(bf16) + head_halves[half]
                out_ref[q, o, rows:, half * LANES : (half + 1) * LANES] = value
            out_ref[q, o, rows:, 2 * LANES :] = jnp.zeros((8, out_ref.shape[3] - 2 * LANES), bf16)


def split_local(
    hidden,
    norm_gain,
    w_gate_in,
    w_conv_in,
    w_step,
    conv_weight,
    conv_bias,
    step_bias,
    decay_log,
    skip_gain,
    gate_gain,
    w_out,
    cotangent,
):
    plane, rank = lax.axis_index("batch"), lax.axis_index("seq")
    core = rank % 2
    planes, ranks = lax.axis_size("batch"), lax.axis_size("seq")
    _, span, width = hidden.shape
    rows_in, inner = w_gate_in.shape
    channels = w_conv_in.shape[1]
    heads = w_step.shape[1]
    head_width = inner // heads
    states = (channels - inner) // 2
    taps = conv_weight.shape[0]
    own = inner // ranks
    rows_out = w_out.shape[0]
    tokens = ranks * span
    block = width // planes
    piece = conv_bias.shape[0]
    devices = planes * ranks
    padded = -(-(2 * states + heads) // LANES) * LANES
    local = own + 2 * states
    third = rows_out // 3
    fixed = None
    where = jnp.stack([rank, plane]).astype(jnp.int32)

    out_parts = planes_gather(w_out)
    cols, message = once(
        functools.partial(pack_kernel, head_width=head_width),
        [w_gate_in, w_conv_in, w_step, norm_gain[None], gate_gain[None], conv_bias[None], conv_weight],
        [((ranks, rows_in, 2 * own), bf16), ((rows_in + 8, padded), bf16)],
        params=whole_grant,
    )
    cols = lax.all_to_all(cols, "seq", 0, 0).reshape(ranks * rows_in, 2 * own)
    message = planes_gather(message, True)
    message = jnp.concatenate(message, axis=1)
    tokens_rel, cot_rel = plane_gather(hidden[0]), plane_gather(cotangent[0])
    shared_mine, shared_other = small_gather(message)
    conv_cols, gate_cols = cols[:, :own], cols[:, own:]
    conv_w, gate_w = planes_gather(conv_cols), planes_gather(gate_cols)
    head_values = jnp.pad(jnp.stack([step_bias, decay_log, skip_gain]), ((0, 5), (0, LANES - heads)))
    shared_w, norm_full, taps_rows, channel_rows, head_rows, head_table = rows_call(
        functools.partial(setup_kernel, n_taps=taps, head_width=head_width),
        where,
        1,
        None,
        [(a, fixed) for a in (shared_mine, shared_other, head_values)],
        [
            ((width, padded), bf16, fixed),
            ((1, width), f32, fixed),
            ((8, local), f32, fixed),
            ((8, own), f32, fixed),
            ((8, LANES), f32, fixed),
            ((LANES, LANES), f32, fixed),
        ],
        [
            pltpu.VMEM((1, inner), f32),
            pltpu.VMEM((8, channels), f32),
            pltpu.VMEM((devices, 8, LANES), f32),
        ],
    )
    lent_rows = jnp.stack([jnp.where(core == 1, part[:third], part[2 * third :]) for part in out_parts])
    out_borrowed = hop(lent_rows, 1)

    sizes = dict(n_taps=taps, head_width=head_width, states=states)
    rows = tokens // 4
    normed, pre, raw, rest_w = rows_call(
        functools.partial(project_kernel, states=states),
        where,
        4,
        rows,
        [(a, fixed) for a in (*tokens_rel, norm_full, *conv_w, shared_w)],
        [
            ((tokens, width), bf16, each),
            ((tokens, local), bf16, each),
            ((tokens, LANES), f32, each),
            ((width, own + padded), bf16, fixed),
        ],
        params=wide_grant,
    )
    pre, raw = pre.reshape(ranks, span, local), raw.reshape(ranks, span, LANES)
    mixed, conv, inter, ssm, entering = spans_call(
        functools.partial(forward_kernel, **sizes),
        where,
        ranks,
        [(pre, relative), (raw, relative)]
        + [(a, fixed) for a in (taps_rows, head_rows, channel_rows)],
        [
            ((span, local), f32, in_time),
            ((span, local), bf16, in_time),
            ((span, own), f32, in_time),
            ((span, own), f32, relative),
            ((states, own), f32, in_time),
        ],
        [pltpu.VMEM((span + 8, local), f32), pltpu.VMEM((states, own), f32)],
    )
    ssm = ssm.reshape(tokens, own)
    gate, ngate, sums, gated, gate_all, cot, out_w = rows_call(
        gate_kernel,
        where,
        4,
        rows,
        [(normed, each)]
        + [(a, fixed) for a in (*gate_w, *cot_rel, *out_parts, out_borrowed, channel_rows)]
        + [(ssm, each)],
        [
            ((tokens, own), f32, each),
            ((tokens, own), f32, each),
            ((ranks, 8, LANES), f32, fixed),
            ((tokens, own), bf16, each),
            ((width, own), bf16, fixed),
            ((tokens, width), bf16, each),
            ((own, width), bf16, fixed),
        ],
        params=wide_grant,
    )
    sums = plane_total(sums)
    part_mine, part_other = rows_call(
        out_part_kernel,
        where,
        4,
        rows,
        [(gated, each), (out_w, fixed)],
        [((tokens // 2, width), bf16, lower), ((tokens // 2, width), bf16, upper)],
    )
    out_own = plane_parts(part_mine, part_other)

    grad_y, grad_gate, projected, lent = rows_call(
        functools.partial(gate_back_kernel, inner=inner, third=third),
        where,
        4,
        rows,
        [(sums, fixed), (ssm, each), (gate, each), (ngate, each), (channel_rows, fixed)],
        [
            ((tokens, own), f32, each),
            ((tokens, own), bf16, each),
            ((tokens, own), bf16, each),
            ((tokens, LANES), bf16, each),
        ],
    )
    borrowed = hop(lent, 1)
    d_gate = rows_call(
        gate_grad_kernel,
        where,
        planes,
        None,
        [(normed, Columns((tokens, block))), (grad_gate, fixed)],
        [((block, own), bf16, fixed)] * 4,
    )
    d_gate = planes_parts(d_gate)
    d_out = rows_call(
        functools.partial(out_grad_kernel, third=third),
        where,
        2,
        tokens // 2,
        [(projected, each), (borrowed, halves_swapped), (cot, each)],
        [((4 * rows_out, block), bf16, fixed)] * 4,
        [pltpu.VMEM((tokens // 2, own), bf16), pltpu.VMEM((own, width), f32)],
    )
    d_out = planes_parts(d_out)
    grad_rest, grad_taps, grad_heads = spans_call(
        functools.partial(backward_kernel, **sizes),
        where,
        ranks,
        [(grad_y.reshape(ranks, span, own), relative_reverse)]
        + [(a, in_reverse) for a in (inter, entering, conv)]
        + [(pre, relative_reverse), (mixed, in_reverse), (raw, relative_reverse)]
        + [(a, fixed) for a in (taps_rows, head_rows, channel_rows)],
        [
            ((span, own + padded), bf16, relative_reverse),
            ((8, local), f32, fixed),
            ((8, LANES), f32, fixed),
        ],
        [
            pltpu.VMEM((span + 8, local), f32),
            pltpu.VMEM((states, own), f32),
            pltpu.VMEM((states, own), f32),
        ],
    )
    grad_rest = grad_rest.reshape(tokens, own + padded)
    d_rest = jnp.dot(normed.T, grad_rest, preferred_element_type=f32).astype(bf16)
    d_conv = planes_parts([d_rest[o * block : (o + 1) * block, :own] for o in range(planes)])
    d_shared = rows_call(
        functools.partial(shared_back_kernel, head_width=head_width, piece=piece),
        where,
        1,
        None,
        [(d_rest, Columns((width, padded), own // padded))]
        + [(a, fixed) for a in (grad_taps, grad_heads, head_table)],
        [((ranks // 2, planes, rows_in + 8, padded), bf16, fixed)] * 2,
    )
    gate_all, *d_shared = lax.optimization_barrier((gate_all, *d_shared))
    mine, other = input_grad_call(grad_gate, grad_rest, gate_all, rest_w)
    grad_own = plane_parts(mine, other)
    d_shared = [a.reshape(ranks // 2 * planes, rows_in + 8, padded) for a in d_shared]
    d_shared = plane_parts(d_shared[0], d_shared[1])
    d_shared = sum(part.astype(f32) for part in d_shared)
    d_shared = planes_direct([d_shared[o] for o in range(planes)])

    d_out, d_gain = once(
        early_rows_kernel,
        [*d_out, w_out, gate_gain[None]],
        [((rows_out, width), f32), ((1, rows_out), f32)],
    )
    (d_in,) = once(late_rows_kernel, [*d_gate, *d_conv], [((ranks, rows_in, 2 * own), bf16)])
    d_in = lax.all_to_all(d_in, "seq", 0, 0)
    (output,) = once(
        functools.partial(output_kernel, inner=inner),
        [*out_own, hidden[0], sums],
        [((span, width), bf16)],
        where,
        params=whole_grant,
    )
    (grad_hidden,) = once(
        hidden_grad_kernel,
        [*grad_own, hidden[0], cotangent[0], norm_full],
        [((span, width), f32)],
        where,
        [pltpu.VMEM((span, width), f32)],
        params=whole_grant,
    )
    d_gate, d_conv, d_norm, d_step, *small = once(
        functools.partial(columns_kernel, head_width=head_width),
        [d_in, w_gate_in, w_conv_in, w_step, norm_gain[None], *d_shared],
        [
            ((rows_in, inner), f32),
            ((rows_in, channels), f32),
            ((1, rows_in), f32),
            ((rows_in, heads), f32),
            ((taps, piece), f32),
            ((1, piece), f32),
            ((1, heads), f32),
            ((1, heads), f32),
            ((1, heads), f32),
        ],
    )
    return (
        output[None],
        grad_hidden[None],
        d_norm[0],
        d_gate,
        d_conv,
        d_step,
        small[0],
        small[1][0],
        small[2][0],
        small[3][0],
        small[4][0],
        d_gain[0],
        d_out,
    )


def split_block(*args):
    return split_local(*args)


def solution(mesh):
    split = (mesh.shape["batch"], mesh.shape["seq"]) == (4, 8)
    body = split_block if split else local
    return jax.shard_map(
        body,
        mesh=mesh,
        in_specs=(
            P("batch", "seq", None),
            P(("batch", "seq")),
            P(("batch", "seq"), None),
            P(("batch", "seq"), None),
            P(("batch", "seq"), None),
            P(None, ("batch", "seq")),
            P(("batch", "seq")),
            P(),
            P(),
            P(),
            P(("batch", "seq")),
            P(("batch", "seq"), None),
            P("batch", "seq", None),
        ),
        out_specs=(
            P("batch", "seq", None),
            P("batch", "seq", None),
            P(("batch", "seq")),
            P(("batch", "seq"), None),
            P(("batch", "seq"), None),
            P(("batch", "seq"), None),
            P(None, ("batch", "seq")),
            P(("batch", "seq")),
            P(),
            P(),
            P(),
            P(("batch", "seq")),
            P(("batch", "seq"), None),
        ),
        check_vma=False,
    )
```
